256 devices in a mesh: section: 2 (over core), seq: 16 (over y, x), traj: 8 (over z).
Axes of the slice: x: 4, y: 4, z: 8, core: 2. Of those that a mesh axis runs over, the one named last changes fastest.
Arguments:
- tokens: bfloat16 [16384, 2048], P(('traj', 'seq')), parts along dimension 0, may hold values from -6 to 6
- norm_gain: float32 [2, 2048], P('section'), may hold values from 0.25 to 1.75
- w_qkv: bfloat16 [2, 2048, 3072], P('section'), may hold values from -0.125 to 0.125
- w_rate: bfloat16 [2, 2048, 16], P('section'), may hold values from -0.125 to 0.125
- rate_base: float32 [2, 16], P('section'), may hold values from 0.00625 to 0.015625
- init_state: float32 [2, 16, 64, 64], P('section'), may hold values from -6 to 6
- w_out: bfloat16 [2, 1024, 2048], P('section'), may hold values from -0.1875 to 0.1875
Outputs:
- layer_out: bfloat16 [2, 16384, 2048], P('section', ('traj', 'seq')), parts along dimension 1
The draws below stay inside these ranges and needn't reach their ends.
There are 8 independent parts, one for each index of `traj`. The reference program is written for one: setup_inputs(seed, part) draws one part's arguments, and reference() takes and returns one part's arrays. A program takes and returns all parts, laid end to end along the dimension named above; an argument that names none is the same for every part. Nothing has to cross between parts.
All inputs are finite; a program needn't handle non-finite values.
Results may differ from the reference program's by a relative error of at most 0.017.
Values may be sent and summed in bfloat16 or wider, within the bound.
A program may use at most 128 MiB of HBM per device.

```python
import math
import jax
import jax.numpy as jnp
from jax import lax

D = 2048
HEADS = 16
HD = 64
MB = 64
LAYERS = 2
TOKENS = 2048


def steps_of(own_key, shape, cuts, least, top_value):
    level, own = 1.0, jax.random.fold_in(own_key, 6)
    for position, parts in cuts:
        heights = jnp.exp(jax.random.uniform(jax.random.fold_in(own, position), (parts,), jnp.float32, least / len(cuts), top_value / len(cuts)))
        level = level * jnp.repeat(heights, shape[position] // parts).reshape([-1 if axis == position else 1 for axis in range(len(shape))])
    return level


def gaussian(rng, extent, deviation, bound, pieces=(), kind=jnp.bfloat16):
    drawn = deviation * jax.random.normal(rng, extent, jnp.float32)
    if pieces:
        drawn = drawn * steps_of(rng, extent, pieces, -0.22, 0.18)
    return jnp.clip(drawn, -bound, bound).astype(kind)


def setup_inputs(seed: int = 0, part: int = 0) -> dict:
    streams_of = jax.random.split(jax.random.key(seed), 8)
    part_splits = jax.random.split(jax.random.fold_in(streams_of[7], part), 8)
    return {
        "tokens": gaussian(part_splits[0], (TOKENS, D), 1.0, 6.0, ((0, 16),)),
        "norm_gain": jnp.clip(1.0 + 0.15 * jax.random.normal(streams_of[1], (LAYERS, D), jnp.float32), 0.25, 1.75),
        "w_qkv": gaussian(streams_of[2], (LAYERS, D, 3 * HEADS * HD), D ** -0.5, 0.125, ((0, 2),)),
        "w_rate": gaussian(streams_of[3], (LAYERS, D, HEADS), D ** -0.5, 0.125, ((0, 2),)),
        "rate_base": jnp.clip(jnp.exp(math.log(0.015625) - 0.9162907 * jax.random.uniform(streams_of[4], (LAYERS, HEADS), jnp.float32) ** steps_of(streams_of[4], (LAYERS, HEADS), ((0, 2),), -0.2, 0.2)), 0.00625, 0.015625),
        "init_state": gaussian(streams_of[5], (LAYERS, HEADS, HD, HD), 1.0, 6.0, ((0, 2),), jnp.float32),
        "w_out": gaussian(streams_of[6], (LAYERS, HEADS * HD, D), (HEADS * HD) ** -0.5, 0.1875, ((0, 2),)),
    }


def inner_block(weight_state, block):
    precise_mode = lax.Precision.HIGHEST
    query_rows, key_input, value_input, rates = block
    predicted_values = jnp.einsum('ylc,yci->yli', key_input, weight_state, precision=precise_mode)
    scaled_gradient = rates[..., None] * (predicted_values - value_input)
    causal_mask = jnp.tril(jnp.ones((query_rows.shape[1], query_rows.shape[1]), query_rows.dtype))
    attention_scores = jnp.einsum('kxw,kqw->kxq', query_rows, key_input, precision=precise_mode) * causal_mask
    inner_output = jnp.einsum('ylc,yci->yli', query_rows, weight_state, precision=precise_mode) - jnp.einsum('ixb,ibt->ixt', attention_scores, scaled_gradient, precision=precise_mode)
    updated_state = weight_state - jnp.einsum('ncz,ncp->nzp', key_input, scaled_gradient, precision=precise_mode)
    return (updated_state, inner_output)

def inner_inputs(hidden, gain, w_qkv, w_rate, rate_base):
    wide = hidden.astype(jnp.float32)
    mean_sq = lax.optimization_barrier(jnp.mean(wide * wide, axis=-1, keepdims=True))
    normed = (wide * lax.rsqrt(mean_sq + 1e-06) * gain).astype(jnp.bfloat16)
    projected = jnp.dot(normed, w_qkv, preferred_element_type=jnp.float32)
    rows = hidden.shape[0]
    heads = rate_base.shape[0]
    width = heads * HD
    query_rows = projected[:, :width].reshape(rows, heads, HD)
    key_input = projected[:, width:2 * width].reshape(rows, heads, HD)
    value_input = projected[:, 2 * width:].reshape(rows, heads, HD)
    query_rows = query_rows * lax.rsqrt(lax.optimization_barrier(jnp.sum(query_rows * query_rows, axis=-1, keepdims=True)) + 1e-06)
    key_input = key_input * lax.rsqrt(lax.optimization_barrier(jnp.sum(key_input * key_input, axis=-1, keepdims=True)) + 1e-06)
    rates = rate_base[None, :] * jax.nn.sigmoid(jnp.dot(normed, w_rate, preferred_element_type=jnp.float32))
    blocks = rows // MB

    def to_blocks(array):
        return array.reshape(blocks, MB, heads, HD).transpose(0, 2, 1, 3)
    rate_blocks = rates.reshape(blocks, MB, heads).transpose(0, 2, 1)
    return (to_blocks(query_rows), to_blocks(key_input), to_blocks(value_input), rate_blocks)

def reference(tokens, norm_gain, w_qkv, w_rate, rate_base, init_state, w_out):
    hidden = tokens
    outputs = []
    for layer_index in range(LAYERS):
        blocks = inner_inputs(hidden, norm_gain[layer_index], w_qkv[layer_index], w_rate[layer_index], rate_base[layer_index])
        final_state, inner_output = lax.scan(inner_block, init_state[layer_index], blocks)
        rows = hidden.shape[0]
        inner_bf = inner_output.transpose(0, 2, 1, 3).reshape(rows, -1).astype(jnp.bfloat16)
        mixed = jnp.dot(inner_bf, w_out[layer_index], preferred_element_type=jnp.float32)
        hidden = (hidden.astype(jnp.float32) + mixed).astype(jnp.bfloat16)
        outputs.append(hidden)
    return jnp.stack(outputs)
```

```python
import jax
import jax.numpy as jnp
from jax import lax
from jax.experimental import pallas as pl
from jax.experimental.pallas import tpu as pltpu
from jax.sharding import PartitionSpec as P

HD = 64
MB = 64
PAIR = 2 * HD
GROUP = 4 * HD
EPS = 1e-06
MESH = pl.DeviceIdType.MESH
F32 = jnp.float32
BF16 = jnp.bfloat16


def dot(a, b, dims=((1,), (0,))):
    return lax.dot_general(a, b, (dims, ((), ())), preferred_element_type=F32)


def split(x):
    high = x.astype(BF16)
    return high, (x - high.astype(F32)).astype(BF16)


def iota(shape, axis):
    return lax.broadcasted_iota(jnp.int32, shape, axis)


def head_ones():
    same = iota((GROUP, GROUP), 0) // HD == iota((GROUP, GROUP), 1) // HD
    return jnp.where(same, 1.0, 0.0).astype(BF16)


def unit_rows(x, ones):
    high, low = split(x * x)
    return x * lax.rsqrt(dot(high, ones) + dot(low, ones) + EPS)


def kernel(
    seq_count,
    tok, gain, w_qkv, w_rate, rate_base, init_state, w_out,
    out,
    hidden, gain_v, wkv_v, wq_v, wrate_v, rbase_v, wout_v, init_v,
    normed, rate_hl, keys, scaled, first_map, sent_map, got_map, sent_state, got_state,
    query_map, offset, inner, result,
    load_sem, weight_sem, out_sem,
    map_send, map_recv, state_send, state_recv, hid_send, hid_recv,
):
    section = lax.axis_index("section")
    me = lax.axis_index("seq")
    rows, width = tok.shape
    heads = rate_base.shape[1]
    inner_width = heads * HD
    groups = inner_width // GROUP
    chunks = hid_send.shape[0]
    chunk = width // chunks

    token_copy = pltpu.make_async_copy(tok, hidden, load_sem.at[0])

    @pl.when(section == 0)
    def _():
        token_copy.start()

    small = [
        pltpu.make_async_copy(gain, gain_v, load_sem.at[1]),
        pltpu.make_async_copy(w_rate.at[0], wrate_v, load_sem.at[2]),
        pltpu.make_async_copy(rate_base, rbase_v, load_sem.at[3]),
        pltpu.make_async_copy(init_state.at[0, me], init_v, load_sem.at[4]),
    ]
    for copy in small:
        copy.start()

    def key_copy(g):
        return pltpu.make_async_copy(
            w_qkv.at[0, :, pl.ds(pl.multiple_of(inner_width + g * GROUP, GROUP), GROUP)],
            wkv_v.at[g, :, pl.ds(0, GROUP)], weight_sem.at[0, g])

    def value_copy(g):
        return pltpu.make_async_copy(
            w_qkv.at[0, :, pl.ds(pl.multiple_of(2 * inner_width + g * GROUP, GROUP), GROUP)],
            wkv_v.at[g, :, pl.ds(GROUP, GROUP)], weight_sem.at[1, g])

    def query_copy(g):
        return pltpu.make_async_copy(
            w_qkv.at[0, :, pl.ds(pl.multiple_of(g * GROUP, GROUP), GROUP)],
            wq_v.at[g], weight_sem.at[2, g])

    def out_weight_copy(n):
        return pltpu.make_async_copy(
            w_out.at[0, :, pl.ds(pl.multiple_of(n * chunk, chunk), chunk)],
            wout_v.at[n], weight_sem.at[3, n])

    for g in range(groups):
        key_copy(g).start()
        value_copy(g).start()
    for g in range(groups):
        query_copy(g).start()
    for n in range(chunks):
        out_weight_copy(n).start()

    barrier = pltpu.get_barrier_semaphore()
    for step in range(1, seq_count):
        pl.semaphore_signal(
            barrier, inc=1, device_id={"seq": lax.rem(me + step, seq_count)}, device_id_type=MESH)
    pl.semaphore_signal(barrier, inc=1, device_id={"section": 1 - section}, device_id_type=MESH)
    pl.semaphore_wait(barrier, seq_count)

    def hidden_copy(n):
        piece = pl.ds(pl.multiple_of(n * chunk, chunk), chunk)
        return pltpu.make_async_remote_copy(
            src_ref=result.at[:, piece], dst_ref=hidden.at[:, piece],
            send_sem=hid_send.at[n], recv_sem=hid_recv.at[n],
            device_id={"section": 1 - section}, device_id_type=MESH)

    def result_copy(n):
        piece = pl.ds(pl.multiple_of(n * chunk, chunk), chunk)
        return pltpu.make_async_copy(result.at[:, piece], out.at[0, :, piece], out_sem.at[n])

    @pl.when(section == 0)
    def _():
        token_copy.wait()

    for copy in small:
        copy.wait()

    @pl.when(section == 1)
    def _():
        for n in range(chunks):
            hidden_copy(n).wait_recv()

    wide = hidden[...].astype(F32)
    mean_sq = jnp.mean(wide * wide, axis=-1, keepdims=True)
    normed[...] = (wide * lax.rsqrt(mean_sq + EPS) * gain_v[...]).astype(BF16)
    rates = rbase_v[...] * jax.nn.sigmoid(dot(normed[...], wrate_v[...], ((1,), (1,))))
    high, low = split(rates)
    rate_hl[0] = high
    rate_hl[1] = low

    lane_low = iota((MB, PAIR), 1) < HD
    diagonal = iota((PAIR, 2 * PAIR), 0) // HD == (iota((PAIR, 2 * PAIR), 1) % PAIR) // HD

    def map_copy(h):
        return pltpu.make_async_remote_copy(
            src_ref=sent_map.at[h], dst_ref=got_map.at[me],
            send_sem=map_send.at[h], recv_sem=map_recv.at[me],
            device_id={"seq": h}, device_id_type=MESH)

    def key_group(g, carry):
        key_copy(g).wait()
        value_copy(g).wait()
        ones = head_ones()
        both = dot(normed[...], wkv_v[g])
        key = unit_rows(both[:, :GROUP], ones)
        spread = jnp.where(
            iota((heads, GROUP), 0) == 4 * g + iota((heads, GROUP), 1) // HD, 1.0, 0.0).astype(BF16)
        rate = dot(rate_hl[0], spread) + dot(rate_hl[1], spread)
        key_bf = key.astype(BF16)
        rated_key = (rate * key).astype(BF16)
        rated_value = (rate * both[:, GROUP:]).astype(BF16)
        for i in range(2):
            lanes = slice(i * PAIR, (i + 1) * PAIR)
            pair = 2 * g + i
            pair_key = key_bf[:, lanes]
            pair_scaled = jnp.concatenate([rated_value[:, lanes], rated_key[:, lanes]], axis=1)
            keys[pair] = pair_key
            scaled[pair] = pair_scaled
            first = jnp.where(diagonal, dot(pair_key[:MB], pair_scaled[:MB], ((0,), (0,))), 0.0)
            second = jnp.where(diagonal, dot(pair_key[MB:], pair_scaled[MB:], ((0,), (0,))), 0.0)
            first_bf = first.astype(BF16)
            first_map[pair] = first_bf
            total = first + second - dot(second[:, PAIR:].astype(BF16), first_bf)
            packed = total[:HD] + total[HD:]
            pack_b, pack_d = packed[:, :PAIR], packed[:, PAIR:]
            even = jnp.where(lane_low, pack_b, pltpu.roll(pack_d, HD, 1)).astype(BF16)
            odd = jnp.where(lane_low, pltpu.roll(pack_b, HD, 1), pack_d).astype(BF16)
            for parity, message in enumerate((even, odd)):
                h = 2 * pair + parity
                sent_map[h] = message

                @pl.when(h == me)
                def _():
                    got_map[me] = message

                @pl.when(h != me)
                def _():
                    map_copy(h).start()

        return carry

    lax.fori_loop(0, groups, key_group, 0)

    row = iota((4 * MB, PAIR), 0)
    column = iota((4 * MB, PAIR), 1)
    causal = (column // MB == row // PAIR) & (column % MB <= row % MB)
    low_half = iota((MB, 2 * PAIR), 1) % PAIR < HD

    def query_group(g, carry):
        query_copy(g).wait()
        query_all = unit_rows(dot(normed[...], wq_v[g]), head_ones())
        for i in range(2):
            pair = 2 * g + i
            query = query_all[:, i * PAIR:(i + 1) * PAIR]
            parts = []
            for b in range(2):
                piece = query[b * MB:(b + 1) * MB]
                parts += [jnp.where(lane_low, piece, 0.0), jnp.where(lane_low, 0.0, piece)]
            stacked = jnp.concatenate(parts, axis=0).astype(BF16)
            scores = jnp.where(causal, dot(stacked, keys[pair], ((1,), (1,))), 0.0).astype(BF16)
            mixed = dot(scores, scaled[pair])
            mix_one = jnp.where(low_half, mixed[:MB], mixed[MB:2 * MB])
            mix_two = jnp.where(low_half, mixed[2 * MB:3 * MB], mixed[3 * MB:])
            map_one = query[:MB] - mix_one[:, PAIR:]
            map_two = query[MB:] - mix_two[:, PAIR:]
            through = dot(map_two.astype(BF16), first_map[pair])
            query_map[pair, pl.ds(0, MB), :] = map_one.astype(BF16)
            query_map[pair, pl.ds(MB, MB), :] = (map_two - through[:, PAIR:]).astype(BF16)
            offset[pair, pl.ds(0, MB), :] = mix_one[:, :PAIR]
            offset[pair, pl.ds(MB, MB), :] = mix_two[:, :PAIR] + through[:, :PAIR]
        return carry

    lax.fori_loop(0, groups, query_group, 0)

    own_half = (iota((HD, PAIR), 1) // HD) == lax.rem(me, 2)

    def state_copy(s):
        return pltpu.make_async_remote_copy(
            src_ref=sent_state.at[s], dst_ref=got_state.at[me],
            send_sem=state_send.at[s], recv_sem=state_recv.at[me],
            device_id={"seq": s}, device_id_type=MESH)

    def map_arrival(s):
        return pltpu.make_async_remote_copy(
            src_ref=sent_map.at[s], dst_ref=got_map.at[s],
            send_sem=map_send.at[s], recv_sem=map_recv.at[s],
            device_id={"seq": s}, device_id_type=MESH)

    def state_arrival(h):
        return pltpu.make_async_remote_copy(
            src_ref=sent_state.at[h], dst_ref=got_state.at[h],
            send_sem=state_send.at[h], recv_sem=state_recv.at[h],
            device_id={"seq": h}, device_id_type=MESH)

    def chain(s, state):
        message = jnp.where(own_half, state, 0.0).astype(BF16)
        sent_state[s] = message

        @pl.when(s == me)
        def _():
            got_state[me] = message

        @pl.when(s != me)
        def _():
            state_copy(s).start()
            map_arrival(s).wait_recv()

        step = got_map[s]
        wide_step = step.astype(F32)
        offsets = jnp.where(lane_low, wide_step, pltpu.roll(wide_step, HD, 1))
        operand = jnp.concatenate([jnp.zeros((HD, PAIR), BF16), state.astype(BF16)], axis=0)
        return state - dot(step, operand) + offsets

    start = jnp.concatenate([init_v[...], init_v[...]], axis=1)
    lax.fori_loop(0, seq_count, chain, start)

    for pair in range(heads // 2):
        for h in (2 * pair, 2 * pair + 1):
            @pl.when(h != me)
            def _():
                state_arrival(h).wait_recv()
        state = jnp.concatenate([got_state[2 * pair], got_state[2 * pair + 1]], axis=0)
        inner[:, pair * PAIR:(pair + 1) * PAIR] = (
            dot(query_map[pair], state) + offset[pair]).astype(BF16)

    for n in range(chunks):
        out_weight_copy(n).wait()
        piece = slice(n * chunk, (n + 1) * chunk)
        result[:, piece] = (
            hidden[:, piece].astype(F32) + dot(inner[...], wout_v[n])).astype(BF16)

        @pl.when(section == 0)
        def _():
            hidden_copy(n).start()

        result_copy(n).start()

    for n in range(chunks):
        result_copy(n).wait()

    @pl.when(section == 0)
    def _():
        for n in range(chunks):
            hidden_copy(n).wait_send()

    def drain(s, carry):
        @pl.when(s != me)
        def _():
            map_copy(s).wait_send()
            state_copy(s).wait_send()
        return carry

    lax.fori_loop(0, seq_count, drain, 0)


def solution(mesh):
    seq_count = mesh.shape["seq"]

    def shards(tokens, norm_gain, w_qkv, w_rate, rate_base, init_state, w_out):
        rows, width = tokens.shape
        heads = rate_base.shape[1]
        inner_width = heads * HD
        groups = inner_width // GROUP
        chunks = 4
        chunk = width // chunks
        hbm = pl.BlockSpec(memory_space=pltpu.HBM)

        def body(*refs):
            kernel(seq_count, *refs)

        return pl.pallas_call(
            body,
            name="layers",
            out_shape=jax.ShapeDtypeStruct((1, rows, width), BF16),
            in_specs=[hbm] * 7,
            out_specs=hbm,
            scratch_shapes=[
                pltpu.VMEM((rows, width), BF16),
                pltpu.VMEM((1, width), F32),
                pltpu.VMEM((groups, width, 2 * GROUP), BF16),
                pltpu.VMEM((groups, width, GROUP), BF16),
                pltpu.VMEM((heads, width), BF16),
                pltpu.VMEM((1, heads), F32),
                pltpu.VMEM((chunks, inner_width, chunk), BF16),
                pltpu.VMEM((HD, HD), F32),
                pltpu.VMEM((rows, width), BF16),
                pltpu.VMEM((2, rows, heads), BF16),
                pltpu.VMEM((heads // 2, rows, PAIR), BF16),
                pltpu.VMEM((heads // 2, rows, 2 * PAIR), BF16),
                pltpu.VMEM((heads // 2, PAIR, 2 * PAIR), BF16),
                pltpu.VMEM((heads, HD, PAIR), BF16),
                pltpu.VMEM((seq_count, HD, PAIR), BF16),
                pltpu.VMEM((seq_count, HD, PAIR), BF16),
                pltpu.VMEM((heads, HD, PAIR), BF16),
                pltpu.VMEM((heads // 2, rows, PAIR), BF16),
                pltpu.VMEM((heads // 2, rows, PAIR), F32),
                pltpu.VMEM((rows, inner_width), BF16),
                pltpu.VMEM((rows, width), BF16),
                pltpu.SemaphoreType.DMA((5,)),
                pltpu.SemaphoreType.DMA((4, max(groups, chunks))),
                pltpu.SemaphoreType.DMA((chunks,)),
                pltpu.SemaphoreType.DMA((heads,)),
                pltpu.SemaphoreType.DMA((seq_count,)),
                pltpu.SemaphoreType.DMA((seq_count,)),
                pltpu.SemaphoreType.DMA((heads,)),
                pltpu.SemaphoreType.DMA((chunks,)),
                pltpu.SemaphoreType.DMA((chunks,)),
            ],
            compiler_params=pltpu.CompilerParams(
                collective_id=0, has_side_effects=True, vmem_limit_bytes=63 * 1024 * 1024),
        )(tokens, norm_gain, w_qkv, jnp.swapaxes(w_rate, 1, 2), rate_base, init_state, w_out)

    return jax.shard_map(
        shards,
        mesh=mesh,
        in_specs=(
            P(("traj", "seq"), None),
            P("section", None),
            P("section", None, None),
            P("section", None, None),
            P("section", None),
            P("section", None, None, None),
            P("section", None, None),
        ),
        out_specs=P("section", ("traj", "seq"), None),
        check_vma=False,
    )
```

```python
import jax
import jax.numpy as jnp
from jax import lax
from jax.experimental import pallas as pl
from jax.experimental.pallas import tpu as pltpu
from jax.sharding import PartitionSpec as P

HD = 64
MB = 64
PAIR = 2 * HD
GROUP = 4 * HD
EPS = 1e-06
MESH = pl.DeviceIdType.MESH
F32 = jnp.float32
BF16 = jnp.bfloat16


def dot(a, b, dims=((1,), (0,))):
    return lax.dot_general(a, b, (dims, ((), ())), preferred_element_type=F32)


def split(x):
    high = x.astype(BF16)
    return high, (x - high.astype(F32)).astype(BF16)


def iota(shape, axis):
    return lax.broadcasted_iota(jnp.int32, shape, axis)


def head_ones():
    same = iota((GROUP, GROUP), 0) // HD == iota((GROUP, GROUP), 1) // HD
    return jnp.where(same, 1.0, 0.0).astype(BF16)


def unit_scale(x, ones):
    return lax.rsqrt(dot((x * x).astype(BF16), ones) + EPS)


def kernel(
    seq_count,
    tok, gain, w_qkv, w_rate, rate_base, init_state, w_out,
    out,
    hidden, gain_v, wkv_v, wq_v, wrate_v, rbase_v, wout_v, init_v,
    normed, rate_all, keys, scaled, first_map, sent_map, got_map, sent_state, got_state,
    query_map, offset, result,
    load_sem, weight_sem, out_sem,
    map_send, map_recv, state_send, state_recv, hid_send, hid_recv,
):
    section = lax.axis_index("section")
    me = lax.axis_index("seq")
    rows, width = tok.shape
    heads = rate_base.shape[1]
    inner_width = heads * HD
    groups = inner_width // GROUP
    chunks = hid_send.shape[0]
    chunk = width // chunks

    token_copy = pltpu.make_async_copy(tok, hidden, load_sem.at[0])

    @pl.when(section == 0)
    def _():
        token_copy.start()

    small = [
        pltpu.make_async_copy(gain, gain_v, load_sem.at[1]),
        pltpu.make_async_copy(w_rate.at[0], wrate_v, load_sem.at[2]),
        pltpu.make_async_copy(rate_base, rbase_v, load_sem.at[3]),
        pltpu.make_async_copy(init_state.at[0, me], init_v, load_sem.at[4]),
    ]
    for copy in small:
        copy.start()

    def key_copy(g):
        return pltpu.make_async_copy(
            w_qkv.at[0, :, pl.ds(inner_width + g * GROUP, GROUP)],
            wkv_v.at[g, :, pl.ds(0, GROUP)], weight_sem.at[0, g])

    def value_copy(g):
        return pltpu.make_async_copy(
            w_qkv.at[0, :, pl.ds(2 * inner_width + g * GROUP, GROUP)],
            wkv_v.at[g, :, pl.ds(GROUP, GROUP)], weight_sem.at[1, g])

    def query_copy(g):
        return pltpu.make_async_copy(
            w_qkv.at[0, :, pl.ds(g * GROUP, GROUP)], wq_v.at[g], weight_sem.at[2, g])

    def out_weight_copy(n):
        return pltpu.make_async_copy(
            w_out.at[0, :, pl.ds(n * chunk, chunk)], wout_v.at[n], weight_sem.at[3, n])

    for g in range(groups):
        key_copy(g).start()
        value_copy(g).start()

    barrier = pltpu.get_barrier_semaphore()
    peers = [lax.rem(me + step, seq_count) for step in range(1, seq_count)]
    for peer in peers:
        pl.semaphore_signal(barrier, inc=1, device_id={"seq": peer}, device_id_type=MESH)
    pl.semaphore_signal(barrier, inc=1, device_id={"section": 1 - section}, device_id_type=MESH)

    def hidden_copy(n):
        piece = pl.ds(n * chunk, chunk)
        return pltpu.make_async_remote_copy(
            src_ref=result.at[:, piece], dst_ref=hidden.at[:, piece],
            send_sem=hid_send.at[n], recv_sem=hid_recv.at[n],
            device_id={"section": 1 - section}, device_id_type=MESH)

    def result_copy(n):
        piece = pl.ds(n * chunk, chunk)
        return pltpu.make_async_copy(result.at[:, piece], out.at[0, :, piece], out_sem.at[n])

    for copy in small:
        copy.wait()

    @pl.when(section == 0)
    def _():
        token_copy.wait()

    @pl.when(section == 1)
    def _():
        for n in range(chunks):
            hidden_copy(n).wait_recv()

    wide = hidden[...].astype(F32)
    mean_sq = jnp.mean(wide * wide, axis=-1, keepdims=True)
    normed[...] = (wide * lax.rsqrt(mean_sq + EPS) * gain_v[...]).astype(BF16)
    rates = rbase_v[...] * jax.nn.sigmoid(dot(normed[...], wrate_v[...], ((1,), (1,))))
    spread = jnp.where(
        iota((heads, inner_width), 0) == iota((heads, inner_width), 1) // HD, 1.0, 0.0).astype(BF16)
    high, low = split(rates)
    rate_all[...] = dot(high, spread) + dot(low, spread)

    lane_low = iota((HD, PAIR), 1) < HD
    wide_shape = (PAIR, 4 * PAIR)
    diagonal = iota(wide_shape, 0) // HD == (iota(wide_shape, 1) % PAIR) // HD
    ones = head_ones()
    blank = jnp.zeros((MB, 2 * PAIR), BF16)

    def map_copy(peer):
        return pltpu.make_async_remote_copy(
            src_ref=sent_map.at[peer], dst_ref=got_map.at[me],
            send_sem=map_send.at[peer], recv_sem=map_recv.at[me],
            device_id={"seq": peer}, device_id_type=MESH)

    def key_group(g):
        both = dot(normed[...], wkv_v[g])
        key, value = both[:, :GROUP], both[:, GROUP:]
        scale = unit_scale(key, ones)
        rate = rate_all[:, g * GROUP:(g + 1) * GROUP] * scale
        key_bf = key.astype(BF16)
        rated_value = (rate * value).astype(BF16)
        rated_key = (rate * scale * key).astype(BF16)
        for i in range(2):
            lanes = slice(i * PAIR, (i + 1) * PAIR)
            pair = 2 * g + i
            pair_key = key_bf[:, lanes]
            pair_scaled = jnp.concatenate([rated_value[:, lanes], rated_key[:, lanes]], axis=1)
            keys[pair] = pair_key
            scaled[pair] = pair_scaled
            by_block = jnp.concatenate([
                jnp.concatenate([pair_scaled[:MB], blank], axis=1),
                jnp.concatenate([blank, pair_scaled[MB:]], axis=1)], axis=0)
            maps = jnp.where(diagonal, dot(pair_key, by_block, ((0,), (0,))), 0.0)
            first, second = maps[:, :2 * PAIR], maps[:, 2 * PAIR:]
            first_bf = first.astype(BF16)
            first_map[pair] = first_bf
            total = first + second - dot(second[:, PAIR:].astype(BF16), first_bf)
            packed = total[:HD] + total[HD:]
            pack_b, pack_d = packed[:, :PAIR], pltpu.roll(packed[:, PAIR:], HD, 1)
            sent_map[2 * pair] = jnp.where(lane_low, pack_b, pack_d).astype(BF16)
            sent_map[2 * pair + 1] = jnp.where(lane_low, pack_d, pack_b).astype(BF16)

    half = groups // 2
    for g in range(half):
        key_copy(g).wait()
        value_copy(g).wait()
    for g in range(groups):
        query_copy(g).start()
    for g in range(half):
        key_group(g)
    for g in range(half, groups):
        key_copy(g).wait()
        value_copy(g).wait()
    for n in range(chunks):
        out_weight_copy(n).start()
    for g in range(half, groups):
        key_group(g)

    pl.semaphore_wait(barrier, seq_count)
    for peer in peers:
        map_copy(peer).start()
    got_map[me] = sent_map[me]

    row = iota((4 * MB, PAIR), 0)
    column = iota((4 * MB, PAIR), 1)
    causal = (column // MB == row // PAIR) & (column % MB <= row % MB)
    low_half = iota((MB, 2 * PAIR), 1) % PAIR < HD

    def query_group(g):
        query_all = dot(normed[...], wq_v[g])
        scale_all = unit_scale(query_all, ones)
        for i in range(2):
            pair = 2 * g + i
            query = query_all[:, i * PAIR:(i + 1) * PAIR]
            scale = scale_all[:, i * PAIR:(i + 1) * PAIR]
            parts = []
            for b in range(2):
                piece = query[b * MB:(b + 1) * MB]
                parts += [jnp.where(lane_low, piece, 0.0), jnp.where(lane_low, 0.0, piece)]
            stacked = jnp.concatenate(parts, axis=0).astype(BF16)
            scores = jnp.where(causal, dot(stacked, keys[pair], ((1,), (1,))), 0.0).astype(BF16)
            mixed = dot(scores, scaled[pair])
            mix_one = jnp.where(low_half, mixed[:MB], mixed[MB:2 * MB])
            mix_two = jnp.where(low_half, mixed[2 * MB:3 * MB], mixed[3 * MB:])
            map_one = query[:MB] - mix_one[:, PAIR:]
            map_two = query[MB:] - mix_two[:, PAIR:]
            through = dot(map_two.astype(BF16), first_map[pair])
            query_map[pair, pl.ds(0, MB), :] = (scale[:MB] * map_one).astype(BF16)
            query_map[pair, pl.ds(MB, MB), :] = (
                scale[MB:] * (map_two - through[:, PAIR:])).astype(BF16)
            offset[pair, pl.ds(0, MB), :] = scale[:MB] * mix_one[:, :PAIR]
            offset[pair, pl.ds(MB, MB), :] = (
                scale[MB:] * (mix_two[:, :PAIR] + through[:, :PAIR]))

    for g in range(groups):
        query_copy(g).wait()
    for g in range(half):
        query_group(g)

    odd = lax.rem(me, 2)
    offset_half = (iota((HD, PAIR), 1) // HD) == odd

    def state_copy(peer):
        return pltpu.make_async_remote_copy(
            src_ref=sent_state.at[peer], dst_ref=got_state.at[me],
            send_sem=state_send.at[peer], recv_sem=state_recv.at[me],
            device_id={"seq": peer}, device_id_type=MESH)

    def map_arrival(peer):
        return pltpu.make_async_remote_copy(
            src_ref=sent_map.at[peer], dst_ref=got_map.at[peer],
            send_sem=map_send.at[peer], recv_sem=map_recv.at[peer],
            device_id={"seq": peer}, device_id_type=MESH)

    def state_arrival(peer):
        return pltpu.make_async_remote_copy(
            src_ref=sent_state.at[peer], dst_ref=got_state.at[peer],
            send_sem=state_send.at[peer], recv_sem=state_recv.at[peer],
            device_id={"seq": peer}, device_id_type=MESH)

    for peer in peers:
        map_arrival(peer).wait_recv()

    def after(later, earlier):
        contracted = jnp.where(offset_half, 0.0, later).astype(BF16)
        operand = earlier.astype(BF16)
        return earlier + later - dot(contracted, jnp.concatenate([operand, operand], axis=0))

    step = [got_map[s].astype(F32) for s in range(seq_count)]
    state = [None] * seq_count
    state[0] = jnp.where(offset_half, jnp.concatenate([init_v[...], init_v[...]], axis=1), 0.0)
    prefix = {}
    for g in range(seq_count // 4):
        lead = 4 * g
        prefix[g, 1] = step[lead]
        prefix[g, 2] = after(step[lead + 1], step[lead])
        if g + 1 < seq_count // 4:
            prefix[g, 4] = after(after(step[lead + 3], step[lead + 2]), prefix[g, 2])
        prefix[g, 3] = after(step[lead + 2], prefix[g, 2])
    state[4] = after(prefix[0, 4], state[0])
    state[8] = after(after(prefix[1, 4], prefix[0, 4]), state[0])
    state[12] = after(after(prefix[2, 4], prefix[1, 4]), state[4])
    for g in range(seq_count // 4):
        for i in range(1, 4):
            state[4 * g + i] = after(prefix[g, i], state[4 * g])
    for s in range(seq_count):
        sent_state[s] = jnp.where(offset_half, state[s], 0.0).astype(BF16)
    for peer in peers:
        state_copy(peer).start()
    got_state[me] = sent_state[me]

    for g in range(half, groups):
        query_group(g)

    for n in range(chunks):
        out_weight_copy(n).wait()
    for peer in peers:
        state_arrival(peer).wait_recv()
    parts = []
    for pair in range(heads // 2):
        start = jnp.concatenate([got_state[2 * pair], got_state[2 * pair + 1]], axis=0)
        parts.append((dot(query_map[pair], start) + offset[pair]).astype(BF16))
    inner = jnp.concatenate(parts, axis=1)

    for n in range(chunks):
        piece = slice(n * chunk, (n + 1) * chunk)
        result[:, piece] = (hidden[:, piece].astype(F32) + dot(inner, wout_v[n])).astype(BF16)

        @pl.when(section == 0)
        def _():
            hidden_copy(n).start()

        result_copy(n).start()

    for peer in peers:
        map_copy(peer).wait_send()
        state_copy(peer).wait_send()
    for n in range(chunks):
        result_copy(n).wait()

    @pl.when(section == 0)
    def _():
        for n in range(chunks):
            hidden_copy(n).wait_send()


def solution(mesh):
    seq_count = mesh.shape["seq"]

    def shards(tokens, norm_gain, w_qkv, w_rate, rate_base, init_state, w_out):
        rows, width = tokens.shape
        heads = rate_base.shape[1]
        inner_width = heads * HD
        groups = inner_width // GROUP
        chunks = 4
        chunk = width // chunks
        hbm = pl.BlockSpec(memory_space=pltpu.HBM)

        def body(*refs):
            kernel(seq_count, *refs)

        return pl.pallas_call(
            body,
            name="layers",
            out_shape=jax.ShapeDtypeStruct((1, rows, width), BF16),
            in_specs=[hbm] * 7,
            out_specs=hbm,
            scratch_shapes=[
                pltpu.VMEM((rows, width), BF16),
                pltpu.VMEM((1, width), F32),
                pltpu.VMEM((groups, width, 2 * GROUP), BF16),
                pltpu.VMEM((groups, width, GROUP), BF16),
                pltpu.VMEM((heads, width), BF16),
                pltpu.VMEM((1, heads), F32),
                pltpu.VMEM((chunks, inner_width, chunk), BF16),
                pltpu.VMEM((HD, HD), F32),
                pltpu.VMEM((rows, width), BF16),
                pltpu.VMEM((rows, inner_width), F32),
                pltpu.VMEM((heads // 2, rows, PAIR), BF16),
                pltpu.VMEM((heads // 2, rows, 2 * PAIR), BF16),
                pltpu.VMEM((heads // 2, PAIR, 2 * PAIR), BF16),
                pltpu.VMEM((heads, HD, PAIR), BF16),
                pltpu.VMEM((seq_count, HD, PAIR), BF16),
                pltpu.VMEM((seq_count, HD, PAIR), BF16),
                pltpu.VMEM((heads, HD, PAIR), BF16),
                pltpu.VMEM((heads // 2, rows, PAIR), BF16),
                pltpu.VMEM((heads // 2, rows, PAIR), F32),
                pltpu.VMEM((rows, width), BF16),
                pltpu.SemaphoreType.DMA((5,)),
                pltpu.SemaphoreType.DMA((4, max(groups, chunks))),
                pltpu.SemaphoreType.DMA((chunks,)),
                pltpu.SemaphoreType.DMA((heads,)),
                pltpu.SemaphoreType.DMA((seq_count,)),
                pltpu.SemaphoreType.DMA((seq_count,)),
                pltpu.SemaphoreType.DMA((heads,)),
                pltpu.SemaphoreType.DMA((chunks,)),
                pltpu.SemaphoreType.DMA((chunks,)),
            ],
            compiler_params=pltpu.CompilerParams(
                collective_id=0, has_side_effects=True, vmem_limit_bytes=63 * 1024 * 1024),
        )(tokens, norm_gain, w_qkv, jnp.swapaxes(w_rate, 1, 2), rate_base, init_state, w_out)

    return jax.shard_map(
        shards,
        mesh=mesh,
        in_specs=(
            P(("traj", "seq"), None),
            P("section", None),
            P("section", None, None),
            P("section", None, None),
            P("section", None),
            P("section", None, None, None),
            P("section", None, None),
        ),
        out_specs=P("section", ("traj", "seq"), None),
        check_vma=False,
    )
```

```python
import jax
import jax.numpy as jnp
from jax import lax
from jax.experimental import pallas as pl
from jax.experimental.pallas import tpu as pltpu
from jax.sharding import PartitionSpec as P

HD = 64
MB = 64
PAIR = 2 * HD
GROUP = 4 * HD
EPS = 1e-06
MESH = pl.DeviceIdType.MESH
F32 = jnp.float32
BF16 = jnp.bfloat16


def dot(a, b, dims=((1,), (0,))):
    return lax.dot_general(a, b, (dims, ((), ())), preferred_element_type=F32)


def split(x):
    high = x.astype(BF16)
    return high, (x - high.astype(F32)).astype(BF16)


def iota(shape, axis):
    return lax.broadcasted_iota(jnp.int32, shape, axis)


def head_ones():
    same = iota((GROUP, GROUP), 0) // HD == iota((GROUP, GROUP), 1) // HD
    return jnp.where(same, 1.0, 0.0).astype(BF16)


def unit_scale(x, ones):
    return lax.rsqrt(dot((x * x).astype(BF16), ones) + EPS)


def kernel(
    seq_count,
    tok, gain, w_qkv, w_rate, rate_base, init_state, w_out,
    out,
    hidden, gain_v, wkv_v, wq_v, wrate_v, rbase_v, wout_v, init_v,
    normed, rate_all, keys, scaled, first_map, sent_map, got_map, sent_state, got_state,
    query_map, offset,
    load_sem, weight_sem,
    map_send, map_recv, state_send, state_recv, hid_send, hid_recv,
):
    section = lax.axis_index("section")
    me = lax.axis_index("seq")
    rows, width = tok.shape
    heads = rate_base.shape[1]
    inner_width = heads * HD
    groups = inner_width // GROUP
    chunks = hid_send.shape[0]
    chunk = width // chunks

    token_copy = pltpu.make_async_copy(tok, hidden, load_sem.at[0])

    @pl.when(section == 0)
    def _():
        token_copy.start()

    small = [
        pltpu.make_async_copy(gain, gain_v, load_sem.at[1]),
        pltpu.make_async_copy(w_rate.at[0], wrate_v, load_sem.at[2]),
        pltpu.make_async_copy(rate_base, rbase_v, load_sem.at[3]),
        pltpu.make_async_copy(init_state.at[0, me], init_v, load_sem.at[4]),
    ]
    for copy in small:
        copy.start()

    def key_copy(g):
        return pltpu.make_async_copy(
            w_qkv.at[0, :, pl.ds(inner_width + g * GROUP, GROUP)],
            wkv_v.at[g, :, pl.ds(0, GROUP)], weight_sem.at[0, g])

    def value_copy(g):
        return pltpu.make_async_copy(
            w_qkv.at[0, :, pl.ds(2 * inner_width + g * GROUP, GROUP)],
            wkv_v.at[g, :, pl.ds(GROUP, GROUP)], weight_sem.at[1, g])

    def query_copy(g):
        return pltpu.make_async_copy(
            w_qkv.at[0, :, pl.ds(g * GROUP, GROUP)], wq_v.at[g], weight_sem.at[2, g])

    def out_weight_copy(n):
        return pltpu.make_async_copy(
            w_out.at[0, :, pl.ds(n * chunk, chunk)], wout_v.at[n], weight_sem.at[3, n])

    for g in range(groups):
        key_copy(g).start()
        value_copy(g).start()

    barrier = pltpu.get_barrier_semaphore()
    side = 4
    row_of, column_of = me // side, lax.rem(me, side)
    steps = [(y, x) for y in range(seq_count // side) for x in range(side)][1:]
    steps.sort(key=lambda s: -min(s[0], seq_count // side - s[0]) - min(s[1], side - s[1]))
    peers = [
        lax.rem(row_of + y, seq_count // side) * side + lax.rem(column_of + x, side)
        for y, x in steps]
    for peer in peers:
        pl.semaphore_signal(barrier, inc=1, device_id={"seq": peer}, device_id_type=MESH)
    pl.semaphore_signal(barrier, inc=1, device_id={"section": 1 - section}, device_id_type=MESH)

    def hidden_copy(n):
        piece = pl.ds(n * chunk, chunk)
        return pltpu.make_async_remote_copy(
            src_ref=out.at[0, :, piece], dst_ref=hidden.at[:, piece],
            send_sem=hid_send.at[n], recv_sem=hid_recv.at[n],
            device_id={"section": 1 - section}, device_id_type=MESH)

    for copy in small:
        copy.wait()

    @pl.when(section == 0)
    def _():
        token_copy.wait()

    @pl.when(section == 1)
    def _():
        for n in range(chunks):
            hidden_copy(n).wait_recv()

    wide = hidden[...].astype(F32)
    mean_sq = jnp.mean(wide * wide, axis=-1, keepdims=True)
    normed[...] = (wide * lax.rsqrt(mean_sq + EPS) * gain_v[...]).astype(BF16)
    rates = rbase_v[...] * jax.nn.sigmoid(dot(normed[...], wrate_v[...], ((1,), (1,))))
    spread = jnp.where(
        iota((heads, inner_width), 0) == iota((heads, inner_width), 1) // HD, 1.0, 0.0).astype(BF16)
    high, low = split(rates)
    rate_all[...] = dot(high, spread) + dot(low, spread)

    lane_low = iota((HD, PAIR), 1) < HD
    wide_shape = (PAIR, 4 * PAIR)
    diagonal = iota(wide_shape, 0) // HD == (iota(wide_shape, 1) % PAIR) // HD
    ones = head_ones()
    blank = jnp.zeros((MB, 2 * PAIR), BF16)

    def map_copy(peer):
        return pltpu.make_async_remote_copy(
            src_ref=sent_map.at[peer], dst_ref=got_map.at[me],
            send_sem=map_send.at[peer], recv_sem=map_recv.at[me],
            device_id={"seq": peer}, device_id_type=MESH)

    def key_group(g):
        both = dot(normed[...], wkv_v[g])
        key, value = both[:, :GROUP], both[:, GROUP:]
        scale = unit_scale(key, ones)
        rate = rate_all[:, g * GROUP:(g + 1) * GROUP] * scale
        key_bf = key.astype(BF16)
        rated_value = (rate * value).astype(BF16)
        rated_key = (rate * scale * key).astype(BF16)
        for i in range(2):
            lanes = slice(i * PAIR, (i + 1) * PAIR)
            pair = 2 * g + i
            pair_key = key_bf[:, lanes]
            pair_scaled = jnp.concatenate([rated_value[:, lanes], rated_key[:, lanes]], axis=1)
            keys[pair] = pair_key
            scaled[pair] = pair_scaled
            by_block = jnp.concatenate([
                jnp.concatenate([pair_scaled[:MB], blank], axis=1),
                jnp.concatenate([blank, pair_scaled[MB:]], axis=1)], axis=0)
            maps = jnp.where(diagonal, dot(pair_key, by_block, ((0,), (0,))), 0.0)
            first, second = maps[:, :2 * PAIR], maps[:, 2 * PAIR:]
            first_bf = first.astype(BF16)
            first_map[pair] = first_bf
            total = first + second - dot(second[:, PAIR:].astype(BF16), first_bf)
            packed = total[:HD] + total[HD:]
            pack_b, pack_d = packed[:, :PAIR], pltpu.roll(packed[:, PAIR:], HD, 1)
            sent_map[2 * pair] = jnp.where(lane_low, pack_b, pack_d).astype(BF16)
            sent_map[2 * pair + 1] = jnp.where(lane_low, pack_d, pack_b).astype(BF16)

    half = groups // 2
    for g in range(half):
        key_copy(g).wait()
        value_copy(g).wait()
    for g in range(groups):
        query_copy(g).start()
    for g in range(half):
        key_group(g)
    pl.semaphore_wait(barrier, seq_count)
    for h in range(heads // 2):
        @pl.when(h != me)
        def _():
            map_copy(h).start()

    for g in range(half, groups):
        key_copy(g).wait()
        value_copy(g).wait()
    for n in range(chunks):
        out_weight_copy(n).start()
    for g in range(half, groups):
        key_group(g)

    for h in range(heads // 2, heads):
        @pl.when(h != me)
        def _():
            map_copy(h).start()

    got_map[me] = sent_map[me]

    row = iota((4 * MB, PAIR), 0)
    column = iota((4 * MB, PAIR), 1)
    causal = (column // MB == row // PAIR) & (column % MB <= row % MB)
    low_half = iota((MB, 2 * PAIR), 1) % PAIR < HD

    def query_group(g):
        query_all = dot(normed[...], wq_v[g])
        scale_all = unit_scale(query_all, ones)
        for i in range(2):
            pair = 2 * g + i
            query = query_all[:, i * PAIR:(i + 1) * PAIR]
            scale = scale_all[:, i * PAIR:(i + 1) * PAIR]
            parts = []
            for b in range(2):
                piece = query[b * MB:(b + 1) * MB]
                parts += [jnp.where(lane_low, piece, 0.0), jnp.where(lane_low, 0.0, piece)]
            stacked = jnp.concatenate(parts, axis=0).astype(BF16)
            scores = jnp.where(causal, dot(stacked, keys[pair], ((1,), (1,))), 0.0).astype(BF16)
            mixed = dot(scores, scaled[pair])
            mix_one = jnp.where(low_half, mixed[:MB], mixed[MB:2 * MB])
            mix_two = jnp.where(low_half, mixed[2 * MB:3 * MB], mixed[3 * MB:])
            map_one = query[:MB] - mix_one[:, PAIR:]
            map_two = query[MB:] - mix_two[:, PAIR:]
            through = dot(map_two.astype(BF16), first_map[pair])
            query_map[pair, pl.ds(0, MB), :] = (scale[:MB] * map_one).astype(BF16)
            query_map[pair, pl.ds(MB, MB), :] = (
                scale[MB:] * (map_two - through[:, PAIR:])).astype(BF16)
            offset[pair, pl.ds(0, MB), :] = scale[:MB] * mix_one[:, :PAIR]
            offset[pair, pl.ds(MB, MB), :] = (
                scale[MB:] * (mix_two[:, :PAIR] + through[:, :PAIR]))

    for g in range(groups):
        query_copy(g).wait()
    for g in range(half):
        query_group(g)

    odd = lax.rem(me, 2)
    offset_half = (iota((HD, PAIR), 1) // HD) == odd

    def state_copy(peer):
        return pltpu.make_async_remote_copy(
            src_ref=sent_state.at[peer], dst_ref=got_state.at[me],
            send_sem=state_send.at[peer], recv_sem=state_recv.at[me],
            device_id={"seq": peer}, device_id_type=MESH)

    def map_arrival(peer):
        return pltpu.make_async_remote_copy(
            src_ref=sent_map.at[peer], dst_ref=got_map.at[peer],
            send_sem=map_send.at[peer], recv_sem=map_recv.at[peer],
            device_id={"seq": peer}, device_id_type=MESH)

    def state_arrival(peer):
        return pltpu.make_async_remote_copy(
            src_ref=sent_state.at[peer], dst_ref=got_state.at[peer],
            send_sem=state_send.at[peer], recv_sem=state_recv.at[peer],
            device_id={"seq": peer}, device_id_type=MESH)

    for peer in peers:
        map_arrival(peer).wait_recv()

    def after(later, earlier):
        contracted = jnp.where(offset_half, 0.0, later).astype(BF16)
        operand = earlier.astype(BF16)
        return earlier + later - dot(contracted, jnp.concatenate([operand, operand], axis=0))

    step = [got_map[s].astype(F32) for s in range(seq_count)]
    state = [None] * seq_count
    state[0] = jnp.where(offset_half, jnp.concatenate([init_v[...], init_v[...]], axis=1), 0.0)
    prefix = {}
    for g in range(seq_count // 4):
        lead = 4 * g
        prefix[g, 1] = step[lead]
        prefix[g, 2] = after(step[lead + 1], step[lead])
        if g + 1 < seq_count // 4:
            prefix[g, 4] = after(after(step[lead + 3], step[lead + 2]), prefix[g, 2])
        prefix[g, 3] = after(step[lead + 2], prefix[g, 2])
    state[4] = after(prefix[0, 4], state[0])
    state[8] = after(after(prefix[1, 4], prefix[0, 4]), state[0])
    state[12] = after(after(prefix[2, 4], prefix[1, 4]), state[4])
    for g in range(seq_count // 4):
        for i in range(1, 4):
            state[4 * g + i] = after(prefix[g, i], state[4 * g])
    for s in range(seq_count):
        sent_state[s] = jnp.where(offset_half, state[s], 0.0).astype(BF16)
    for peer in peers:
        state_copy(peer).start()
    got_state[me] = sent_state[me]

    for g in range(half, groups):
        query_group(g)

    for n in range(chunks):
        out_weight_copy(n).wait()
    for peer in peers:
        state_arrival(peer).wait_recv()
    parts = []
    for pair in range(heads // 2):
        start = jnp.concatenate([got_state[2 * pair], got_state[2 * pair + 1]], axis=0)
        parts.append((dot(query_map[pair], start) + offset[pair]).astype(BF16))
    inner = jnp.concatenate(parts, axis=1)

    for n in range(chunks):
        piece = slice(n * chunk, (n + 1) * chunk)
        out[0, :, piece] = (hidden[:, piece].astype(F32) + dot(inner, wout_v[n])).astype(BF16)

        @pl.when(section == 0)
        def _():
            hidden_copy(n).start()


    for peer in peers:
        map_copy(peer).wait_send()
        state_copy(peer).wait_send()

    @pl.when(section == 0)
    def _():
        for n in range(chunks):
            hidden_copy(n).wait_send()


def solution(mesh):
    seq_count = mesh.shape["seq"]

    def shards(tokens, norm_gain, w_qkv, w_rate, rate_base, init_state, w_out):
        rows, width = tokens.shape
        heads = rate_base.shape[1]
        inner_width = heads * HD
        groups = inner_width // GROUP
        chunks = 4
        chunk = width // chunks
        hbm = pl.BlockSpec(memory_space=pltpu.HBM)

        def body(*refs):
            kernel(seq_count, *refs)

        return pl.pallas_call(
            body,
            name="layers",
            out_shape=jax.ShapeDtypeStruct((1, rows, width), BF16),
            in_specs=[hbm] * 7,
            out_specs=pl.BlockSpec(memory_space=pltpu.VMEM),
            scratch_shapes=[
                pltpu.VMEM((rows, width), BF16),
                pltpu.VMEM((1, width), F32),
                pltpu.VMEM((groups, width, 2 * GROUP), BF16),
                pltpu.VMEM((groups, width, GROUP), BF16),
                pltpu.VMEM((heads, width), BF16),
                pltpu.VMEM((1, heads), F32),
                pltpu.VMEM((chunks, inner_width, chunk), BF16),
                pltpu.VMEM((HD, HD), F32),
                pltpu.VMEM((rows, width), BF16),
                pltpu.VMEM((rows, inner_width), F32),
                pltpu.VMEM((heads // 2, rows, PAIR), BF16),
                pltpu.VMEM((heads // 2, rows, 2 * PAIR), BF16),
                pltpu.VMEM((heads // 2, PAIR, 2 * PAIR), BF16),
                pltpu.VMEM((heads, HD, PAIR), BF16),
                pltpu.VMEM((seq_count, HD, PAIR), BF16),
                pltpu.VMEM((seq_count, HD, PAIR), BF16),
                pltpu.VMEM((heads, HD, PAIR), BF16),
                pltpu.VMEM((heads // 2, rows, PAIR), BF16),
                pltpu.VMEM((heads // 2, rows, PAIR), F32),
                pltpu.SemaphoreType.DMA((5,)),
                pltpu.SemaphoreType.DMA((4, max(groups, chunks))),
                pltpu.SemaphoreType.DMA((heads,)),
                pltpu.SemaphoreType.DMA((seq_count,)),
                pltpu.SemaphoreType.DMA((seq_count,)),
                pltpu.SemaphoreType.DMA((heads,)),
                pltpu.SemaphoreType.DMA((chunks,)),
                pltpu.SemaphoreType.DMA((chunks,)),
            ],
            compiler_params=pltpu.CompilerParams(
                collective_id=0, has_side_effects=True, vmem_limit_bytes=40 * 1024 * 1024),
        )(*(
            pltpu.with_memory_space_constraint(array, pltpu.HBM)
            for array in (
                tokens, norm_gain, w_qkv, jnp.swapaxes(w_rate, 1, 2), rate_base, init_state, w_out)
        ))

    return jax.shard_map(
        shards,
        mesh=mesh,
        in_specs=(
            P(("traj", "seq"), None),
            P("section", None),
            P("section", None, None),
            P("section", None, None),
            P("section", None),
            P("section", None, None, None),
            P("section", None, None),
        ),
        out_specs=P("section", ("traj", "seq"), None),
        check_vma=False,
    )
```

```python
import jax
import jax.numpy as jnp
from jax import lax
from jax.experimental import pallas as pl
from jax.experimental.pallas import tpu as pltpu
from jax.sharding import PartitionSpec as P

HD = 64
MB = 64
PAIR = 2 * HD
GROUP = 4 * HD
EPS = 1e-06
MESH = pl.DeviceIdType.MESH
F32 = jnp.float32
BF16 = jnp.bfloat16


def dot(a, b, dims=((1,), (0,))):
    return lax.dot_general(a, b, (dims, ((), ())), preferred_element_type=F32)


def split(x):
    high = x.astype(BF16)
    return high, (x - high.astype(F32)).astype(BF16)


def iota(shape, axis):
    return lax.broadcasted_iota(jnp.int32, shape, axis)


def head_ones():
    same = iota((GROUP, GROUP), 0) // HD == iota((GROUP, GROUP), 1) // HD
    return jnp.where(same, 1.0, 0.0).astype(BF16)


def unit_scale(x, row_scale, ones):
    return row_scale * lax.rsqrt(row_scale * row_scale * dot((x * x).astype(BF16), ones) + EPS)


def kernel(
    seq_count,
    tok, gain, w_qkv, w_rate, rate_base, init_state, w_out,
    out,
    hidden, gain_v, wkv_v, wq_v, wrate_v, rbase_v, wout_v, init_v,
    normed, scaled_rows, rate_all, keys, scaled, first_map, sent_map, got_map, sent_state, got_state,
    query_map, offset, wout_first, state_first, query_first, offset_first,
    load_sem, weight_sem,
    map_send, map_recv, state_send, state_recv, first_send, first_recv, side_send, side_recv,
):
    section = lax.axis_index("section")
    me = lax.axis_index("seq")
    rows, width = tok.shape
    heads = rate_base.shape[1]
    inner_width = heads * HD
    groups = inner_width // GROUP
    chunks = wout_v.shape[0]
    chunk = width // chunks

    token_copy = pltpu.make_async_copy(tok, hidden, load_sem.at[0])
    token_copy.start()
    small = [
        pltpu.make_async_copy(gain, gain_v, load_sem.at[1]),
        pltpu.make_async_copy(w_rate.at[0], wrate_v, load_sem.at[2]),
        pltpu.make_async_copy(rate_base, rbase_v, load_sem.at[3]),
        pltpu.make_async_copy(init_state.at[0, me], init_v, load_sem.at[4]),
    ]
    for copy in small:
        copy.start()

    def key_copy(g):
        return pltpu.make_async_copy(
            w_qkv.at[0, :, pl.ds(inner_width + g * GROUP, GROUP)],
            wkv_v.at[g, :, pl.ds(0, GROUP)], weight_sem.at[0, g])

    def value_copy(g):
        return pltpu.make_async_copy(
            w_qkv.at[0, :, pl.ds(2 * inner_width + g * GROUP, GROUP)],
            wkv_v.at[g, :, pl.ds(GROUP, GROUP)], weight_sem.at[1, g])

    def query_copy(g):
        return pltpu.make_async_copy(
            w_qkv.at[0, :, pl.ds(g * GROUP, GROUP)], wq_v.at[g], weight_sem.at[2, g])

    def out_weight_copy(n):
        return pltpu.make_async_copy(
            w_out.at[0, :, pl.ds(n * chunk, chunk)], wout_v.at[n], weight_sem.at[3, n])

    half = groups // 2
    for g in range(half):
        key_copy(g).start()
        value_copy(g).start()

    barrier = pltpu.get_barrier_semaphore()
    side = 4
    row_of, column_of = me // side, lax.rem(me, side)
    steps = [(y, x) for y in range(seq_count // side) for x in range(side)][1:]
    steps.sort(key=lambda s: -min(s[0], seq_count // side - s[0]) - min(s[1], side - s[1]))
    peers = [
        lax.rem(row_of + y, seq_count // side) * side + lax.rem(column_of + x, side)
        for y, x in steps]
    for peer in peers:
        for other in range(2):
            pl.semaphore_signal(
                barrier, inc=1, device_id={"section": other, "seq": peer}, device_id_type=MESH)
    pl.semaphore_signal(barrier, inc=1, device_id={"section": 1 - section}, device_id_type=MESH)
    entered = 2 * seq_count - 1

    def tail(maps, offsets, states, weights, write):
        parts = []
        for pair in range(heads // 2):
            start = jnp.concatenate([states[2 * pair], states[2 * pair + 1]], axis=0)
            parts.append((dot(maps[pair], start) + offsets[pair]).astype(BF16))
        inner = jnp.concatenate(parts, axis=1)
        for n in range(chunks):
            piece = slice(n * chunk, (n + 1) * chunk)
            write(piece, (hidden[:, piece].astype(F32) + dot(inner, weights[n])).astype(BF16))

    half_pairs = heads // 4

    def side_copy(index):
        if index < chunks:
            source, target = wout_v.at[index], wout_first.at[index]
        else:
            pairs = pl.ds((index - chunks) // 2 * half_pairs, half_pairs)
            source, target = [
                (query_map.at[pairs], query_first.at[pairs]),
                (offset.at[pairs], offset_first.at[pairs])][(index - chunks) % 2]
        return pltpu.make_async_remote_copy(
            src_ref=source, dst_ref=target,
            send_sem=side_send.at[index], recv_sem=side_recv.at[index],
            device_id={"section": 1 - section}, device_id_type=MESH)

    def first_copy(peer):
        return pltpu.make_async_remote_copy(
            src_ref=sent_state.at[peer], dst_ref=state_first.at[me],
            send_sem=first_send.at[peer], recv_sem=first_recv.at[me],
            device_id={"section": 1 - section, "seq": peer}, device_id_type=MESH)

    def first_arrival(peer):
        return pltpu.make_async_remote_copy(
            src_ref=sent_state.at[peer], dst_ref=state_first.at[peer],
            send_sem=first_send.at[peer], recv_sem=first_recv.at[peer],
            device_id={"section": 1 - section, "seq": peer}, device_id_type=MESH)

    for copy in small:
        copy.wait()
    token_copy.wait()

    @pl.when(section == 1)
    def _():
        for index in range(chunks + 4):
            side_copy(index).wait_recv()
        for peer in peers + [me]:
            first_arrival(peer).wait_recv()

        def write(piece, value):
            hidden[:, piece] = value

        tail(query_first, offset_first, state_first, wout_first, write)

    for g in range(1):
        key_copy(g).wait()
        value_copy(g).wait()
    for g in range(half, groups):
        key_copy(g).start()
        value_copy(g).start()
    for g in range(1, half):
        key_copy(g).wait()
        value_copy(g).wait()
    wide = hidden[...].astype(F32)
    row_scale = lax.rsqrt(jnp.mean(wide * wide, axis=-1, keepdims=True) + EPS)
    scaled_rows[...] = jnp.broadcast_to(row_scale, (rows, PAIR))
    normed[...] = (wide * gain_v[...]).astype(BF16)
    rates = rbase_v[...] * jax.nn.sigmoid(
        row_scale * dot(normed[...], wrate_v[...], ((1,), (1,))))
    spread = jnp.where(
        iota((heads, inner_width), 0) == iota((heads, inner_width), 1) // HD, 1.0, 0.0).astype(BF16)
    high, low = split(rates)
    rate_all[...] = dot(high, spread) + dot(low, spread)

    lane_low = iota((HD, PAIR), 1) < HD
    wide_shape = (PAIR, 4 * PAIR)
    diagonal = iota(wide_shape, 0) // HD == (iota(wide_shape, 1) % PAIR) // HD
    ones = head_ones()
    blank = jnp.zeros((MB, 2 * PAIR), BF16)

    def map_copy(peer):
        return pltpu.make_async_remote_copy(
            src_ref=sent_map.at[peer], dst_ref=got_map.at[me],
            send_sem=map_send.at[peer], recv_sem=map_recv.at[me],
            device_id={"seq": peer}, device_id_type=MESH)

    def row_factor():
        return jnp.concatenate([scaled_rows[...]] * (GROUP // PAIR), axis=1)

    def key_group(g):
        both = dot(normed[...], wkv_v[g])
        key, value = both[:, :GROUP], both[:, GROUP:]
        row_wide = row_factor()
        scale = unit_scale(key, row_wide, ones)
        rate = rate_all[:, g * GROUP:(g + 1) * GROUP] * scale
        key_bf = key.astype(BF16)
        rated_value = (rate * (row_wide * value)).astype(BF16)
        rated_key = (rate * scale * key).astype(BF16)
        for i in range(2):
            lanes = slice(i * PAIR, (i + 1) * PAIR)
            pair = 2 * g + i
            pair_key = key_bf[:, lanes]
            pair_scaled = jnp.concatenate([rated_value[:, lanes], rated_key[:, lanes]], axis=1)
            keys[pair] = pair_key
            scaled[pair] = pair_scaled
            by_block = jnp.concatenate([
                jnp.concatenate([pair_scaled[:MB], blank], axis=1),
                jnp.concatenate([blank, pair_scaled[MB:]], axis=1)], axis=0)
            maps = jnp.where(diagonal, dot(pair_key, by_block, ((0,), (0,))), 0.0)
            first, second = maps[:, :2 * PAIR], maps[:, 2 * PAIR:]
            first_bf = first.astype(BF16)
            first_map[pair] = first_bf
            total = first + second - dot(second[:, PAIR:].astype(BF16), first_bf)
            packed = total[:HD] + total[HD:]
            pack_b, pack_d = packed[:, :PAIR], pltpu.roll(packed[:, PAIR:], HD, 1)
            sent_map[2 * pair] = jnp.where(lane_low, pack_b, pack_d).astype(BF16)
            sent_map[2 * pair + 1] = jnp.where(lane_low, pack_d, pack_b).astype(BF16)

    for g in range(half):
        key_group(g)
    pl.semaphore_wait(barrier, entered)
    for h in range(heads // 2):
        @pl.when(h != me)
        def _():
            map_copy(h).start()

    for g in range(half, groups):
        key_copy(g).wait()
        value_copy(g).wait()
    for g in range(groups):
        query_copy(g).start()
    for n in range(chunks):
        out_weight_copy(n).start()
    for g in range(half, groups):
        key_group(g)

    for h in range(heads // 2, heads):
        @pl.when(h != me)
        def _():
            map_copy(h).start()

    got_map[me] = sent_map[me]

    row = iota((4 * MB, PAIR), 0)
    column = iota((4 * MB, PAIR), 1)
    causal = (column // MB == row // PAIR) & (column % MB <= row % MB)
    low_half = iota((MB, 2 * PAIR), 1) % PAIR < HD

    def query_group(g):
        query_all = dot(normed[...], wq_v[g])
        scale_all = unit_scale(query_all, row_factor(), ones)
        for i in range(2):
            pair = 2 * g + i
            query = query_all[:, i * PAIR:(i + 1) * PAIR]
            scale = scale_all[:, i * PAIR:(i + 1) * PAIR]
            parts = []
            for b in range(2):
                piece = query[b * MB:(b + 1) * MB]
                parts += [jnp.where(lane_low, piece, 0.0), jnp.where(lane_low, 0.0, piece)]
            stacked = jnp.concatenate(parts, axis=0).astype(BF16)
            scores = jnp.where(causal, dot(stacked, keys[pair], ((1,), (1,))), 0.0).astype(BF16)
            mixed = dot(scores, scaled[pair])
            mix_one = jnp.where(low_half, mixed[:MB], mixed[MB:2 * MB])
            mix_two = jnp.where(low_half, mixed[2 * MB:3 * MB], mixed[3 * MB:])
            map_one = query[:MB] - mix_one[:, PAIR:]
            map_two = query[MB:] - mix_two[:, PAIR:]
            through = dot(map_two.astype(BF16), first_map[pair])
            query_map[pair, pl.ds(0, MB), :] = (scale[:MB] * map_one).astype(BF16)
            query_map[pair, pl.ds(MB, MB), :] = (
                scale[MB:] * (map_two - through[:, PAIR:])).astype(BF16)
            offset[pair, pl.ds(0, MB), :] = scale[:MB] * mix_one[:, :PAIR]
            offset[pair, pl.ds(MB, MB), :] = (
                scale[MB:] * (mix_two[:, :PAIR] + through[:, :PAIR]))

    for g in range(groups):
        query_copy(g).wait()
    for n in range(chunks):
        out_weight_copy(n).wait()

    @pl.when(section == 0)
    def _():
        for n in range(chunks):
            side_copy(n).start()

    for g in range(half):
        query_group(g)

    @pl.when(section == 0)
    def _():
        for index in range(chunks, chunks + 2):
            side_copy(index).start()


    for g in range(half, groups):
        query_group(g)

    @pl.when(section == 0)
    def _():
        for index in range(chunks + 2, chunks + 4):
            side_copy(index).start()

    odd = lax.rem(me, 2)
    offset_half = (iota((HD, PAIR), 1) // HD) == odd

    def state_copy(peer):
        return pltpu.make_async_remote_copy(
            src_ref=sent_state.at[peer], dst_ref=got_state.at[me],
            send_sem=state_send.at[peer], recv_sem=state_recv.at[me],
            device_id={"seq": peer}, device_id_type=MESH)

    def map_arrival(peer):
        return pltpu.make_async_remote_copy(
            src_ref=sent_map.at[peer], dst_ref=got_map.at[peer],
            send_sem=map_send.at[peer], recv_sem=map_recv.at[peer],
            device_id={"seq": peer}, device_id_type=MESH)

    def state_arrival(peer):
        return pltpu.make_async_remote_copy(
            src_ref=sent_state.at[peer], dst_ref=got_state.at[peer],
            send_sem=state_send.at[peer], recv_sem=state_recv.at[peer],
            device_id={"seq": peer}, device_id_type=MESH)

    for peer in peers:
        map_arrival(peer).wait_recv()

    def after(later, earlier):
        contracted = jnp.where(offset_half, 0.0, later).astype(BF16)
        operand = earlier.astype(BF16)
        return earlier + later - dot(contracted, jnp.concatenate([operand, operand], axis=0))

    step = [got_map[s].astype(F32) for s in range(seq_count)]
    state = [None] * seq_count
    state[0] = jnp.where(offset_half, jnp.concatenate([init_v[...], init_v[...]], axis=1), 0.0)
    prefix = {}
    for g in range(seq_count // 4):
        lead = 4 * g
        prefix[g, 1] = step[lead]
        prefix[g, 2] = after(step[lead + 1], step[lead])
        if g + 1 < seq_count // 4:
            prefix[g, 4] = after(after(step[lead + 3], step[lead + 2]), prefix[g, 2])
        prefix[g, 3] = after(step[lead + 2], prefix[g, 2])
    state[4] = after(prefix[0, 4], state[0])
    state[8] = after(after(prefix[1, 4], prefix[0, 4]), state[0])
    state[12] = after(after(prefix[2, 4], prefix[1, 4]), state[4])
    for g in range(seq_count // 4):
        for i in range(1, 4):
            state[4 * g + i] = after(prefix[g, i], state[4 * g])
    for s in range(seq_count):
        sent_state[s] = jnp.where(offset_half, state[s], 0.0).astype(BF16)

    @pl.when(section == 0)
    def _():
        for peer in peers + [me]:
            first_copy(peer).start()

    for peer in peers:
        state_copy(peer).start()
    got_state[me] = sent_state[me]

    for peer in peers:
        state_arrival(peer).wait_recv()

    def write_out(piece, value):
        out[0, :, piece] = value

    tail(query_map, offset, got_state, wout_v, write_out)

    for peer in peers:
        map_copy(peer).wait_send()
        state_copy(peer).wait_send()

    @pl.when(section == 0)
    def _():
        for index in range(chunks + 4):
            side_copy(index).wait_send()
        for peer in peers + [me]:
            first_copy(peer).wait_send()


def solution(mesh):
    seq_count = mesh.shape["seq"]

    def shards(tokens, norm_gain, w_qkv, w_rate, rate_base, init_state, w_out):
        rows, width = tokens.shape
        heads = rate_base.shape[1]
        inner_width = heads * HD
        groups = inner_width // GROUP
        chunks = 4
        chunk = width // chunks
        hbm = pl.BlockSpec(memory_space=pltpu.HBM)

        def body(*refs):
            kernel(seq_count, *refs)

        return pl.pallas_call(
            body,
            name="layers",
            out_shape=jax.ShapeDtypeStruct((1, rows, width), BF16),
            in_specs=[hbm] * 7,
            out_specs=pl.BlockSpec(memory_space=pltpu.VMEM),
            scratch_shapes=[
                pltpu.VMEM((rows, width), BF16),
                pltpu.VMEM((1, width), F32),
                pltpu.VMEM((groups, width, 2 * GROUP), BF16),
                pltpu.VMEM((groups, width, GROUP), BF16),
                pltpu.VMEM((heads, width), BF16),
                pltpu.VMEM((1, heads), F32),
                pltpu.VMEM((chunks, inner_width, chunk), BF16),
                pltpu.VMEM((HD, HD), F32),
                pltpu.VMEM((rows, width), BF16),
                pltpu.VMEM((rows, PAIR), F32),
                pltpu.VMEM((rows, inner_width), F32),
                pltpu.VMEM((heads // 2, rows, PAIR), BF16),
                pltpu.VMEM((heads // 2, rows, 2 * PAIR), BF16),
                pltpu.VMEM((heads // 2, PAIR, 2 * PAIR), BF16),
                pltpu.VMEM((heads, HD, PAIR), BF16),
                pltpu.VMEM((seq_count, HD, PAIR), BF16),
                pltpu.VMEM((seq_count, HD, PAIR), BF16),
                pltpu.VMEM((heads, HD, PAIR), BF16),
                pltpu.VMEM((heads // 2, rows, PAIR), BF16),
                pltpu.VMEM((heads // 2, rows, PAIR), F32),
                pltpu.VMEM((chunks, inner_width, chunk), BF16),
                pltpu.VMEM((seq_count, HD, PAIR), BF16),
                pltpu.VMEM((heads // 2, rows, PAIR), BF16),
                pltpu.VMEM((heads // 2, rows, PAIR), F32),
                pltpu.SemaphoreType.DMA((5,)),
                pltpu.SemaphoreType.DMA((4, max(groups, chunks))),
                pltpu.SemaphoreType.DMA((heads,)),
                pltpu.SemaphoreType.DMA((seq_count,)),
                pltpu.SemaphoreType.DMA((seq_count,)),
                pltpu.SemaphoreType.DMA((heads,)),
                pltpu.SemaphoreType.DMA((seq_count,)),
                pltpu.SemaphoreType.DMA((seq_count,)),
                pltpu.SemaphoreType.DMA((chunks + 4,)),
                pltpu.SemaphoreType.DMA((chunks + 4,)),
            ],
            compiler_params=pltpu.CompilerParams(
                collective_id=0, has_side_effects=True, vmem_limit_bytes=40 * 1024 * 1024),
        )(*(
            pltpu.with_memory_space_constraint(array, pltpu.HBM)
            for array in (
                tokens, norm_gain, w_qkv, jnp.swapaxes(w_rate, 1, 2), rate_base, init_state, w_out)
        ))

    return jax.shard_map(
        shards,
        mesh=mesh,
        in_specs=(
            P(("traj", "seq"), None),
            P("section", None),
            P("section", None, None),
            P("section", None, None),
            P("section", None),
            P("section", None, None, None),
            P("section", None, None),
        ),
        out_specs=P("section", ("traj", "seq"), None),
        check_vma=False,
    )
```

```python
import jax
import jax.numpy as jnp
from jax import lax
from jax.experimental import pallas as pl
from jax.experimental.pallas import tpu as pltpu
from jax.sharding import PartitionSpec as P

HD = 64
MB = 64
PAIR = 2 * HD
GROUP = 4 * HD
EPS = 1e-06
MESH = pl.DeviceIdType.MESH
F32 = jnp.float32
BF16 = jnp.bfloat16


def dot(a, b, dims=((1,), (0,))):
    return lax.dot_general(a, b, (dims, ((), ())), preferred_element_type=F32)


def split(x):
    high = x.astype(BF16)
    return high, (x - high.astype(F32)).astype(BF16)


def iota(shape, axis):
    return lax.broadcasted_iota(jnp.int32, shape, axis)


def head_ones():
    same = iota((GROUP, GROUP), 0) // HD == iota((GROUP, GROUP), 1) // HD
    return jnp.where(same, 1.0, 0.0).astype(BF16)


def unit_scale(x, row_scale, ones):
    return row_scale * lax.rsqrt(row_scale * row_scale * dot((x * x).astype(BF16), ones) + EPS)


def kernel(
    seq_count,
    tok, gain, w_qkv, w_rate, rate_base, init_state, w_out,
    out,
    hidden, gain_v, wkv_v, wq_v, wrate_v, rbase_v, wout_v, init_v,
    normed, scaled_rows, rate_all, keys, scaled, first_map, sent_map, got_map, sent_state, got_state,
    query_map, offset, wout_first, state_first, query_first, offset_first,
    load_sem, weight_sem,
    map_send, map_recv, state_send, state_recv, first_send, first_recv, side_send, side_recv,
):
    section = lax.axis_index("section")
    me = lax.axis_index("seq")
    rows, width = tok.shape
    heads = rate_base.shape[1]
    inner_width = heads * HD
    groups = inner_width // GROUP
    chunks = wout_v.shape[0]
    chunk = width // chunks

    token_copy = pltpu.make_async_copy(tok, hidden, load_sem.at[0])
    token_copy.start()
    small = [
        pltpu.make_async_copy(gain, gain_v, load_sem.at[1]),
        pltpu.make_async_copy(w_rate.at[0], wrate_v, load_sem.at[2]),
        pltpu.make_async_copy(rate_base, rbase_v, load_sem.at[3]),
        pltpu.make_async_copy(init_state.at[0, me], init_v, load_sem.at[4]),
    ]
    for copy in small:
        copy.start()

    def key_copy(g):
        return pltpu.make_async_copy(
            w_qkv.at[0, :, pl.ds(inner_width + g * GROUP, GROUP)],
            wkv_v.at[g, :, pl.ds(0, GROUP)], weight_sem.at[0, g])

    def value_copy(g):
        return pltpu.make_async_copy(
            w_qkv.at[0, :, pl.ds(2 * inner_width + g * GROUP, GROUP)],
            wkv_v.at[g, :, pl.ds(GROUP, GROUP)], weight_sem.at[1, g])

    def query_copy(g):
        return pltpu.make_async_copy(
            w_qkv.at[0, :, pl.ds(g * GROUP, GROUP)], wq_v.at[g], weight_sem.at[2, g])

    def out_weight_copy(n):
        return pltpu.make_async_copy(
            w_out.at[0, :, pl.ds(n * chunk, chunk)], wout_v.at[n], weight_sem.at[3, n])

    half = groups // 2
    for g in range(half):
        key_copy(g).start()
        value_copy(g).start()

    barrier = pltpu.get_barrier_semaphore()
    side = 4
    row_of, column_of = me // side, lax.rem(me, side)
    steps = [(y, x) for y in range(seq_count // side) for x in range(side)][1:]
    steps.sort(key=lambda s: -min(s[0], seq_count // side - s[0]) - min(s[1], side - s[1]))
    peers = [
        lax.rem(row_of + y, seq_count // side) * side + lax.rem(column_of + x, side)
        for y, x in steps]
    for peer in peers:
        for other in range(2):
            pl.semaphore_signal(
                barrier, inc=1, device_id={"section": other, "seq": peer}, device_id_type=MESH)
    pl.semaphore_signal(barrier, inc=1, device_id={"section": 1 - section}, device_id_type=MESH)
    entered = 2 * seq_count - 1

    def tail(maps, offsets, states, weights, write):
        parts = []
        for pair in range(heads // 2):
            start = jnp.concatenate([states[2 * pair], states[2 * pair + 1]], axis=0)
            parts.append((dot(maps[pair], start) + offsets[pair]).astype(BF16))
        inner = jnp.concatenate(parts, axis=1)
        for n in range(chunks):
            piece = slice(n * chunk, (n + 1) * chunk)
            write(piece, (hidden[:, piece].astype(F32) + dot(inner, weights[n])).astype(BF16))

    half_pairs = heads // 4

    def side_copy(index):
        if index < chunks:
            source, target = wout_v.at[index], wout_first.at[index]
        else:
            pairs = pl.ds((index - chunks) // 2 * half_pairs, half_pairs)
            source, target = [
                (query_map.at[pairs], query_first.at[pairs]),
                (offset.at[pairs], offset_first.at[pairs])][(index - chunks) % 2]
        return pltpu.make_async_remote_copy(
            src_ref=source, dst_ref=target,
            send_sem=side_send.at[index], recv_sem=side_recv.at[index],
            device_id={"section": 1 - section}, device_id_type=MESH)

    def first_copy(peer):
        return pltpu.make_async_remote_copy(
            src_ref=sent_state.at[peer], dst_ref=state_first.at[me],
            send_sem=first_send.at[peer], recv_sem=first_recv.at[me],
            device_id={"section": 1 - section, "seq": peer}, device_id_type=MESH)

    def first_arrival(peer):
        return pltpu.make_async_remote_copy(
            src_ref=sent_state.at[peer], dst_ref=state_first.at[peer],
            send_sem=first_send.at[peer], recv_sem=first_recv.at[peer],
            device_id={"section": 1 - section, "seq": peer}, device_id_type=MESH)

    for copy in small:
        copy.wait()
    token_copy.wait()

    @pl.when(section == 1)
    def _():
        for g in range(half, groups):
            key_copy(g).start()
            value_copy(g).start()
        for g in range(groups):
            query_copy(g).start()
        for n in range(chunks):
            out_weight_copy(n).start()
        for g in range(groups):
            key_copy(g).wait()
            value_copy(g).wait()
        for g in range(groups):
            query_copy(g).wait()
        for n in range(chunks):
            out_weight_copy(n).wait()
        pl.semaphore_wait(barrier, entered)
        for index in range(chunks + 4):
            side_copy(index).wait_recv()
        for peer in peers + [me]:
            first_arrival(peer).wait_recv()

        def write(piece, value):
            hidden[:, piece] = value

        tail(query_first, offset_first, state_first, wout_first, write)

    @pl.when(section == 0)
    def _():
        key_copy(0).wait()
        value_copy(0).wait()
        for g in range(half, groups):
            key_copy(g).start()
            value_copy(g).start()
        for g in range(1, half):
            key_copy(g).wait()
            value_copy(g).wait()

    wide = hidden[...].astype(F32)
    row_scale = lax.rsqrt(jnp.mean(wide * wide, axis=-1, keepdims=True) + EPS)
    scaled_rows[...] = jnp.broadcast_to(row_scale, (rows, PAIR))
    normed[...] = (wide * gain_v[...]).astype(BF16)
    rates = rbase_v[...] * jax.nn.sigmoid(
        row_scale * dot(normed[...], wrate_v[...], ((1,), (1,))))
    spread = jnp.where(
        iota((heads, inner_width), 0) == iota((heads, inner_width), 1) // HD, 1.0, 0.0).astype(BF16)
    high, low = split(rates)
    rate_all[...] = dot(high, spread) + dot(low, spread)

    lane_low = iota((HD, PAIR), 1) < HD
    wide_shape = (PAIR, 4 * PAIR)
    diagonal = iota(wide_shape, 0) // HD == (iota(wide_shape, 1) % PAIR) // HD
    ones = head_ones()
    blank = jnp.zeros((MB, 2 * PAIR), BF16)

    def map_copy(peer):
        return pltpu.make_async_remote_copy(
            src_ref=sent_map.at[peer], dst_ref=got_map.at[me],
            send_sem=map_send.at[peer], recv_sem=map_recv.at[me],
            device_id={"seq": peer}, device_id_type=MESH)

    def row_factor():
        return jnp.concatenate([scaled_rows[...]] * (GROUP // PAIR), axis=1)

    def key_group(g):
        both = dot(normed[...], wkv_v[g])
        key, value = both[:, :GROUP], both[:, GROUP:]
        row_wide = row_factor()
        scale = unit_scale(key, row_wide, ones)
        rate = rate_all[:, g * GROUP:(g + 1) * GROUP] * scale
        key_bf = key.astype(BF16)
        rated_value = (rate * (row_wide * value)).astype(BF16)
        rated_key = (rate * scale * key).astype(BF16)
        for i in range(2):
            lanes = slice(i * PAIR, (i + 1) * PAIR)
            pair = 2 * g + i
            pair_key = key_bf[:, lanes]
            pair_scaled = jnp.concatenate([rated_value[:, lanes], rated_key[:, lanes]], axis=1)
            keys[pair] = pair_key
            scaled[pair] = pair_scaled
            by_block = jnp.concatenate([
                jnp.concatenate([pair_scaled[:MB], blank], axis=1),
                jnp.concatenate([blank, pair_scaled[MB:]], axis=1)], axis=0)
            maps = jnp.where(diagonal, dot(pair_key, by_block, ((0,), (0,))), 0.0)
            first, second = maps[:, :2 * PAIR], maps[:, 2 * PAIR:]
            first_bf = first.astype(BF16)
            first_map[pair] = first_bf
            total = first + second - dot(second[:, PAIR:].astype(BF16), first_bf)
            packed = total[:HD] + total[HD:]
            pack_b, pack_d = packed[:, :PAIR], pltpu.roll(packed[:, PAIR:], HD, 1)
            sent_map[2 * pair] = jnp.where(lane_low, pack_b, pack_d).astype(BF16)
            sent_map[2 * pair + 1] = jnp.where(lane_low, pack_d, pack_b).astype(BF16)

    @pl.when(section == 0)
    def _():
        for g in range(half):
            key_group(g)
        for g in range(groups):
            query_copy(g).start()
        pl.semaphore_wait(barrier, entered)
        for h in range(heads // 2):
            @pl.when(h != me)
            def _():
                map_copy(h).start()

        for g in range(half, groups):
            key_copy(g).wait()
            value_copy(g).wait()
        for n in range(chunks):
            out_weight_copy(n).start()
        for g in range(half, groups):
            key_group(g)
        for h in range(heads // 2, heads):
            @pl.when(h != me)
            def _():
                map_copy(h).start()

    @pl.when(section == 1)
    def _():
        for g in range(groups):
            key_group(g)
        for peer in peers:
            map_copy(peer).start()

    got_map[me] = sent_map[me]

    row = iota((4 * MB, PAIR), 0)
    column = iota((4 * MB, PAIR), 1)
    causal = (column // MB == row // PAIR) & (column % MB <= row % MB)
    low_half = iota((MB, 2 * PAIR), 1) % PAIR < HD

    def query_group(g):
        query_all = dot(normed[...], wq_v[g])
        scale_all = unit_scale(query_all, row_factor(), ones)
        for i in range(2):
            pair = 2 * g + i
            query = query_all[:, i * PAIR:(i + 1) * PAIR]
            scale = scale_all[:, i * PAIR:(i + 1) * PAIR]
            parts = []
            for b in range(2):
                piece = query[b * MB:(b + 1) * MB]
                parts += [jnp.where(lane_low, piece, 0.0), jnp.where(lane_low, 0.0, piece)]
            stacked = jnp.concatenate(parts, axis=0).astype(BF16)
            scores = jnp.where(causal, dot(stacked, keys[pair], ((1,), (1,))), 0.0).astype(BF16)
            mixed = dot(scores, scaled[pair])
            mix_one = jnp.where(low_half, mixed[:MB], mixed[MB:2 * MB])
            mix_two = jnp.where(low_half, mixed[2 * MB:3 * MB], mixed[3 * MB:])
            map_one = query[:MB] - mix_one[:, PAIR:]
            map_two = query[MB:] - mix_two[:, PAIR:]
            through = dot(map_two.astype(BF16), first_map[pair])
            query_map[pair, pl.ds(0, MB), :] = (scale[:MB] * map_one).astype(BF16)
            query_map[pair, pl.ds(MB, MB), :] = (
                scale[MB:] * (map_two - through[:, PAIR:])).astype(BF16)
            offset[pair, pl.ds(0, MB), :] = scale[:MB] * mix_one[:, :PAIR]
            offset[pair, pl.ds(MB, MB), :] = (
                scale[MB:] * (mix_two[:, :PAIR] + through[:, :PAIR]))

    @pl.when(section == 0)
    def _():
        for g in range(groups):
            query_copy(g).wait()

    for g in range(half):
        query_group(g)

    @pl.when(section == 0)
    def _():
        for n in range(chunks):
            out_weight_copy(n).wait()
        for index in range(chunks + 2):
            side_copy(index).start()

    for g in range(half, groups):
        query_group(g)

    @pl.when(section == 0)
    def _():
        for index in range(chunks + 2, chunks + 4):
            side_copy(index).start()

    odd = lax.rem(me, 2)
    offset_half = (iota((HD, PAIR), 1) // HD) == odd

    def state_copy(peer):
        return pltpu.make_async_remote_copy(
            src_ref=sent_state.at[peer], dst_ref=got_state.at[me],
            send_sem=state_send.at[peer], recv_sem=state_recv.at[me],
            device_id={"seq": peer}, device_id_type=MESH)

    def map_arrival(peer):
        return pltpu.make_async_remote_copy(
            src_ref=sent_map.at[peer], dst_ref=got_map.at[peer],
            send_sem=map_send.at[peer], recv_sem=map_recv.at[peer],
            device_id={"seq": peer}, device_id_type=MESH)

    def state_arrival(peer):
        return pltpu.make_async_remote_copy(
            src_ref=sent_state.at[peer], dst_ref=got_state.at[peer],
            send_sem=state_send.at[peer], recv_sem=state_recv.at[peer],
            device_id={"seq": peer}, device_id_type=MESH)

    for peer in peers:
        map_arrival(peer).wait_recv()

    def after(later, earlier):
        contracted = jnp.where(offset_half, 0.0, later).astype(BF16)
        operand = earlier.astype(BF16)
        return earlier + later - dot(contracted, jnp.concatenate([operand, operand], axis=0))

    step = [got_map[s].astype(F32) for s in range(seq_count)]
    state = [None] * seq_count
    state[0] = jnp.where(offset_half, jnp.concatenate([init_v[...], init_v[...]], axis=1), 0.0)
    prefix = {}
    for g in range(seq_count // 4):
        lead = 4 * g
        prefix[g, 1] = step[lead]
        prefix[g, 2] = after(step[lead + 1], step[lead])
        if g + 1 < seq_count // 4:
            prefix[g, 4] = after(after(step[lead + 3], step[lead + 2]), prefix[g, 2])
        prefix[g, 3] = after(step[lead + 2], prefix[g, 2])
    state[4] = after(prefix[0, 4], state[0])
    state[8] = after(after(prefix[1, 4], prefix[0, 4]), state[0])
    state[12] = after(after(prefix[2, 4], prefix[1, 4]), state[4])
    for g in range(seq_count // 4):
        for i in range(1, 4):
            state[4 * g + i] = after(prefix[g, i], state[4 * g])
    for s in range(seq_count):
        sent_state[s] = jnp.where(offset_half, state[s], 0.0).astype(BF16)

    @pl.when(section == 0)
    def _():
        for peer in peers + [me]:
            first_copy(peer).start()

    for peer in peers:
        state_copy(peer).start()
    got_state[me] = sent_state[me]

    for peer in peers:
        state_arrival(peer).wait_recv()

    def write_out(piece, value):
        out[0, :, piece] = value

    tail(query_map, offset, got_state, wout_v, write_out)

    for peer in peers:
        map_copy(peer).wait_send()
        state_copy(peer).wait_send()

    @pl.when(section == 0)
    def _():
        for index in range(chunks + 4):
            side_copy(index).wait_send()
        for peer in peers + [me]:
            first_copy(peer).wait_send()


def solution(mesh):
    seq_count = mesh.shape["seq"]

    def shards(tokens, norm_gain, w_qkv, w_rate, rate_base, init_state, w_out):
        rows, width = tokens.shape
        heads = rate_base.shape[1]
        inner_width = heads * HD
        groups = inner_width // GROUP
        chunks = 4
        chunk = width // chunks
        hbm = pl.BlockSpec(memory_space=pltpu.HBM)

        def body(*refs):
            kernel(seq_count, *refs)

        return pl.pallas_call(
            body,
            name="layers",
            out_shape=jax.ShapeDtypeStruct((1, rows, width), BF16),
            in_specs=[hbm] * 7,
            out_specs=pl.BlockSpec(memory_space=pltpu.VMEM),
            scratch_shapes=[
                pltpu.VMEM((rows, width), BF16),
                pltpu.VMEM((1, width), F32),
                pltpu.VMEM((groups, width, 2 * GROUP), BF16),
                pltpu.VMEM((groups, width, GROUP), BF16),
                pltpu.VMEM((heads, width), BF16),
                pltpu.VMEM((1, heads), F32),
                pltpu.VMEM((chunks, inner_width, chunk), BF16),
                pltpu.VMEM((HD, HD), F32),
                pltpu.VMEM((rows, width), BF16),
                pltpu.VMEM((rows, PAIR), F32),
                pltpu.VMEM((rows, inner_width), F32),
                pltpu.VMEM((heads // 2, rows, PAIR), BF16),
                pltpu.VMEM((heads // 2, rows, 2 * PAIR), BF16),
                pltpu.VMEM((heads // 2, PAIR, 2 * PAIR), BF16),
                pltpu.VMEM((heads, HD, PAIR), BF16),
                pltpu.VMEM((seq_count, HD, PAIR), BF16),
                pltpu.VMEM((seq_count, HD, PAIR), BF16),
                pltpu.VMEM((heads, HD, PAIR), BF16),
                pltpu.VMEM((heads // 2, rows, PAIR), BF16),
                pltpu.VMEM((heads // 2, rows, PAIR), F32),
                pltpu.VMEM((chunks, inner_width, chunk), BF16),
                pltpu.VMEM((seq_count, HD, PAIR), BF16),
                pltpu.VMEM((heads // 2, rows, PAIR), BF16),
                pltpu.VMEM((heads // 2, rows, PAIR), F32),
                pltpu.SemaphoreType.DMA((5,)),
                pltpu.SemaphoreType.DMA((4, max(groups, chunks))),
                pltpu.SemaphoreType.DMA((heads,)),
                pltpu.SemaphoreType.DMA((seq_count,)),
                pltpu.SemaphoreType.DMA((seq_count,)),
                pltpu.SemaphoreType.DMA((heads,)),
                pltpu.SemaphoreType.DMA((seq_count,)),
                pltpu.SemaphoreType.DMA((seq_count,)),
                pltpu.SemaphoreType.DMA((chunks + 4,)),
                pltpu.SemaphoreType.DMA((chunks + 4,)),
            ],
            compiler_params=pltpu.CompilerParams(
                collective_id=0, has_side_effects=True, vmem_limit_bytes=40 * 1024 * 1024),
        )(*(
            pltpu.with_memory_space_constraint(array, pltpu.HBM)
            for array in (
                tokens, norm_gain, w_qkv, jnp.swapaxes(w_rate, 1, 2), rate_base, init_state, w_out)
        ))

    return jax.shard_map(
        shards,
        mesh=mesh,
        in_specs=(
            P(("traj", "seq"), None),
            P("section", None),
            P("section", None, None),
            P("section", None, None),
            P("section", None),
            P("section", None, None, None),
            P("section", None, None),
        ),
        out_specs=P("section", ("traj", "seq"), None),
        check_vma=False,
    )
```

```python
import jax
import jax.numpy as jnp
from jax import lax
from jax.experimental import pallas as pl
from jax.experimental.pallas import tpu as pltpu
from jax.sharding import PartitionSpec as P

HD = 64
MB = 64
PAIR = 2 * HD
GROUP = 4 * HD
EPS = 1e-06
MESH = pl.DeviceIdType.MESH
F32 = jnp.float32
BF16 = jnp.bfloat16


def dot(a, b, dims=((1,), (0,))):
    return lax.dot_general(a, b, (dims, ((), ())), preferred_element_type=F32)


def split(x):
    high = x.astype(BF16)
    return high, (x - high.astype(F32)).astype(BF16)


def iota(shape, axis):
    return lax.broadcasted_iota(jnp.int32, shape, axis)


def head_ones():
    same = iota((GROUP, GROUP), 0) // HD == iota((GROUP, GROUP), 1) // HD
    return jnp.where(same, 1.0, 0.0).astype(BF16)


def unit_scale(x, row_scale, ones):
    return row_scale * lax.rsqrt(row_scale * row_scale * dot((x * x).astype(BF16), ones) + EPS)


def kernel(
    seq_count,
    tok, gain, w_qkv, w_rate, rate_base, init_state, w_out,
    out,
    hidden, gain_v, wkv_v, wq_v, wrate_v, rbase_v, wout_v, init_v,
    normed, scaled_rows, rate_all, keys, scaled, first_map, sent_map, got_map, sent_state, got_state,
    query_map, offset, wout_first, state_first, query_first, offset_first,
    load_sem, weight_sem,
    map_send, map_recv, state_send, state_recv, first_send, first_recv, side_send, side_recv,
):
    section = lax.axis_index("section")
    me = lax.axis_index("seq")
    rows, width = tok.shape
    heads = rate_base.shape[1]
    inner_width = heads * HD
    groups = inner_width // GROUP
    chunks = wout_v.shape[0]
    chunk = width // chunks

    token_copy = pltpu.make_async_copy(tok, hidden, load_sem.at[0])
    token_copy.start()
    small = [
        pltpu.make_async_copy(gain, gain_v, load_sem.at[1]),
        pltpu.make_async_copy(w_rate.at[0], wrate_v, load_sem.at[2]),
        pltpu.make_async_copy(rate_base, rbase_v, load_sem.at[3]),
        pltpu.make_async_copy(init_state.at[0, me], init_v, load_sem.at[4]),
    ]
    for copy in small:
        copy.start()

    def key_copy(g):
        return pltpu.make_async_copy(
            w_qkv.at[0, :, pl.ds(inner_width + g * GROUP, GROUP)],
            wkv_v.at[g, :, pl.ds(0, GROUP)], weight_sem.at[0, g])

    def value_copy(g):
        return pltpu.make_async_copy(
            w_qkv.at[0, :, pl.ds(2 * inner_width + g * GROUP, GROUP)],
            wkv_v.at[g, :, pl.ds(GROUP, GROUP)], weight_sem.at[1, g])

    def query_copy(g):
        return pltpu.make_async_copy(
            w_qkv.at[0, :, pl.ds(g * GROUP, GROUP)], wq_v.at[g], weight_sem.at[2, g])

    def out_weight_copy(n):
        return pltpu.make_async_copy(
            w_out.at[0, :, pl.ds(n * chunk, chunk)], wout_v.at[n], weight_sem.at[3, n])

    half = groups // 2
    for g in range(half):
        key_copy(g).start()
        value_copy(g).start()

    barrier = pltpu.get_barrier_semaphore()
    side = 4
    row_of, column_of = me // side, lax.rem(me, side)
    steps = [(y, x) for y in range(seq_count // side) for x in range(side)][1:]
    steps.sort(key=lambda s: -min(s[0], seq_count // side - s[0]) - min(s[1], side - s[1]))
    peers = [
        lax.rem(row_of + y, seq_count // side) * side + lax.rem(column_of + x, side)
        for y, x in steps]
    for peer in peers:
        for other in range(2):
            pl.semaphore_signal(
                barrier, inc=1, device_id={"section": other, "seq": peer}, device_id_type=MESH)
    pl.semaphore_signal(barrier, inc=1, device_id={"section": 1 - section}, device_id_type=MESH)
    entered = 2 * seq_count - 1

    def tail(maps, offsets, states, weights, write):
        parts = []
        for pair in range(heads // 2):
            start = jnp.concatenate([states[2 * pair], states[2 * pair + 1]], axis=0)
            parts.append((dot(maps[pair], start) + offsets[pair]).astype(BF16))
        inner = jnp.concatenate(parts, axis=1)
        for n in range(chunks):
            piece = slice(n * chunk, (n + 1) * chunk)
            write(piece, (hidden[:, piece].astype(F32) + dot(inner, weights[n])).astype(BF16))

    half_pairs = heads // 4

    def side_copy(index):
        if index < chunks:
            source, target = wout_v.at[index], wout_first.at[index]
        else:
            pairs = pl.ds((index - chunks) // 2 * half_pairs, half_pairs)
            source, target = [
                (query_map.at[pairs], query_first.at[pairs]),
                (offset.at[pairs], offset_first.at[pairs])][(index - chunks) % 2]
        return pltpu.make_async_remote_copy(
            src_ref=source, dst_ref=target,
            send_sem=side_send.at[index], recv_sem=side_recv.at[index],
            device_id={"section": 1 - section}, device_id_type=MESH)

    def first_copy(peer):
        return pltpu.make_async_remote_copy(
            src_ref=sent_state.at[peer], dst_ref=state_first.at[me],
            send_sem=first_send.at[peer], recv_sem=first_recv.at[me],
            device_id={"section": 1 - section, "seq": peer}, device_id_type=MESH)

    def first_arrival(peer):
        return pltpu.make_async_remote_copy(
            src_ref=sent_state.at[peer], dst_ref=state_first.at[peer],
            send_sem=first_send.at[peer], recv_sem=first_recv.at[peer],
            device_id={"section": 1 - section, "seq": peer}, device_id_type=MESH)

    for copy in small:
        copy.wait()
    token_copy.wait()

    def norm():
        wide = hidden[...].astype(F32)
        row_scale = lax.rsqrt(jnp.mean(wide * wide, axis=-1, keepdims=True) + EPS)
        scaled_rows[...] = jnp.broadcast_to(row_scale, (rows, PAIR))
        normed[...] = (wide * gain_v[...]).astype(BF16)
        return row_scale

    def rate_parts(row_scale):
        return split(rbase_v[...] * jax.nn.sigmoid(
            row_scale * dot(normed[...], wrate_v[...], ((1,), (1,)))))

    def rate_spread(parts):
        spread = jnp.where(
            iota((heads, inner_width), 0) == iota((heads, inner_width), 1) // HD,
            1.0, 0.0).astype(BF16)
        rate_all[...] = dot(parts[0], spread) + dot(parts[1], spread)

    lane_low = iota((HD, PAIR), 1) < HD
    wide_shape = (PAIR, 4 * PAIR)
    diagonal = iota(wide_shape, 0) // HD == (iota(wide_shape, 1) % PAIR) // HD
    ones = head_ones()
    blank = jnp.zeros((MB, 2 * PAIR), BF16)

    def map_copy(peer):
        return pltpu.make_async_remote_copy(
            src_ref=sent_map.at[peer], dst_ref=got_map.at[me],
            send_sem=map_send.at[peer], recv_sem=map_recv.at[me],
            device_id={"seq": peer}, device_id_type=MESH)

    def row_factor():
        return jnp.concatenate([scaled_rows[...]] * (GROUP // PAIR), axis=1)

    def key_dot(g):
        return dot(normed[...], wkv_v[g])

    def key_scale(g, both):
        key, value = both[:, :GROUP], both[:, GROUP:]
        row_wide = row_factor()
        scale = unit_scale(key, row_wide, ones)
        rate = rate_all[:, g * GROUP:(g + 1) * GROUP] * scale
        key_bf = key.astype(BF16)
        rated_value = (rate * (row_wide * value)).astype(BF16)
        rated_key = (rate * scale * key).astype(BF16)
        made = []
        for i in range(2):
            lanes = slice(i * PAIR, (i + 1) * PAIR)
            pair_key = key_bf[:, lanes]
            pair_scaled = jnp.concatenate([rated_value[:, lanes], rated_key[:, lanes]], axis=1)
            keys[2 * g + i] = pair_key
            scaled[2 * g + i] = pair_scaled
            made.append((pair_key, pair_scaled))
        return made

    def key_maps(g, made):
        found = []
        for i, (pair_key, pair_scaled) in enumerate(made):
            by_block = jnp.concatenate([
                jnp.concatenate([pair_scaled[:MB], blank], axis=1),
                jnp.concatenate([blank, pair_scaled[MB:]], axis=1)], axis=0)
            maps = jnp.where(diagonal, dot(pair_key, by_block, ((0,), (0,))), 0.0)
            first_bf = maps[:, :2 * PAIR].astype(BF16)
            first_map[2 * g + i] = first_bf
            found.append((maps, first_bf))
        return found

    def key_pack(g, found):
        for i, (maps, first_bf) in enumerate(found):
            pair = 2 * g + i
            first, second = maps[:, :2 * PAIR], maps[:, 2 * PAIR:]
            total = first + second - dot(second[:, PAIR:].astype(BF16), first_bf)
            packed = total[:HD] + total[HD:]
            pack_b, pack_d = packed[:, :PAIR], pltpu.roll(packed[:, PAIR:], HD, 1)
            sent_map[2 * pair] = jnp.where(lane_low, pack_b, pack_d).astype(BF16)
            sent_map[2 * pair + 1] = jnp.where(lane_low, pack_d, pack_b).astype(BF16)

    def key_groups(which, before=lambda position: None, gap=0):
        stages = [lambda g, unused: key_dot(g)]
        stages += [lambda g, value: value] * gap + [key_scale, key_maps, key_pack]
        held = {}
        for step in range(len(which) + len(stages) - 1):
            if step < len(which):
                before(step)
            for depth, stage in enumerate(stages):
                position = step - depth
                if 0 <= position < len(which):
                    held[position] = stage(which[position], held.get(position))

    @pl.when(section == 0)
    def _():
        for g in range(half, groups - 1):
            key_copy(g).start()
            value_copy(g).start()
        rate_spread(rate_parts(norm()))
        for g in range(half):
            key_copy(g).wait()
            value_copy(g).wait()
            if g == 0:
                key_copy(groups - 1).start()
                value_copy(groups - 1).start()
        key_groups(range(half))
        for g in range(groups):
            query_copy(g).start()
        pl.semaphore_wait(barrier, entered)
        for h in range(heads // 2):
            @pl.when(h != me)
            def _():
                map_copy(h).start()

        def arrive(position):
            key_copy(half + position).wait()
            value_copy(half + position).wait()
            if position == groups - half - 1:
                for n in range(chunks):
                    out_weight_copy(n).start()

        key_groups(range(half, groups), arrive)
        for h in range(heads // 2, heads):
            @pl.when(h != me)
            def _():
                map_copy(h).start()

    @pl.when(section == 1)
    def _():
        for g in range(half, groups):
            key_copy(g).start()
            value_copy(g).start()
        for g in range(groups):
            query_copy(g).start()
        for n in range(chunks):
            out_weight_copy(n).start()
        for g in range(groups):
            key_copy(g).wait()
            value_copy(g).wait()
        for g in range(groups):
            query_copy(g).wait()
        for n in range(chunks):
            out_weight_copy(n).wait()
        pl.semaphore_wait(barrier, entered)
        for index in range(chunks + 4):
            side_copy(index).wait_recv()
        for peer in peers + [me]:
            first_arrival(peer).wait_recv()

        def write(piece, value):
            hidden[:, piece] = value

        tail(query_first, offset_first, state_first, wout_first, write)
        row_scale = norm()
        parts = []

        def rates(position):
            if position == 1:
                parts.append(rate_parts(row_scale))
            if position == 2:
                rate_spread(parts[0])

        key_groups(range(groups), rates, gap=1)
        for peer in peers:
            map_copy(peer).start()

    got_map[me] = sent_map[me]

    row = iota((4 * MB, PAIR), 0)
    column = iota((4 * MB, PAIR), 1)
    causal = (column // MB == row // PAIR) & (column % MB <= row % MB)
    low_half = iota((MB, 2 * PAIR), 1) % PAIR < HD

    def query_group(g):
        query_all = dot(normed[...], wq_v[g])
        scale_all = unit_scale(query_all, row_factor(), ones)
        for i in range(2):
            pair = 2 * g + i
            query = query_all[:, i * PAIR:(i + 1) * PAIR]
            scale = scale_all[:, i * PAIR:(i + 1) * PAIR]
            parts = []
            for b in range(2):
                piece = query[b * MB:(b + 1) * MB]
                parts += [jnp.where(lane_low, piece, 0.0), jnp.where(lane_low, 0.0, piece)]
            stacked = jnp.concatenate(parts, axis=0).astype(BF16)
            scores = jnp.where(causal, dot(stacked, keys[pair], ((1,), (1,))), 0.0).astype(BF16)
            mixed = dot(scores, scaled[pair])
            mix_one = jnp.where(low_half, mixed[:MB], mixed[MB:2 * MB])
            mix_two = jnp.where(low_half, mixed[2 * MB:3 * MB], mixed[3 * MB:])
            map_one = query[:MB] - mix_one[:, PAIR:]
            map_two = query[MB:] - mix_two[:, PAIR:]
            through = dot(map_two.astype(BF16), first_map[pair])
            query_map[pair, pl.ds(0, MB), :] = (scale[:MB] * map_one).astype(BF16)
            query_map[pair, pl.ds(MB, MB), :] = (
                scale[MB:] * (map_two - through[:, PAIR:])).astype(BF16)
            offset[pair, pl.ds(0, MB), :] = scale[:MB] * mix_one[:, :PAIR]
            offset[pair, pl.ds(MB, MB), :] = (
                scale[MB:] * (mix_two[:, :PAIR] + through[:, :PAIR]))

    @pl.when(section == 0)
    def _():
        for g in range(groups):
            query_copy(g).wait()

    for g in range(half):
        query_group(g)

    @pl.when(section == 0)
    def _():
        for n in range(chunks):
            out_weight_copy(n).wait()
        for index in range(chunks + 2):
            side_copy(index).start()

    for g in range(half, groups):
        query_group(g)

    @pl.when(section == 0)
    def _():
        for index in range(chunks + 2, chunks + 4):
            side_copy(index).start()

    odd = lax.rem(me, 2)
    offset_half = (iota((HD, PAIR), 1) // HD) == odd

    def state_copy(peer):
        return pltpu.make_async_remote_copy(
            src_ref=sent_state.at[peer], dst_ref=got_state.at[me],
            send_sem=state_send.at[peer], recv_sem=state_recv.at[me],
            device_id={"seq": peer}, device_id_type=MESH)

    def map_arrival(peer):
        return pltpu.make_async_remote_copy(
            src_ref=sent_map.at[peer], dst_ref=got_map.at[peer],
            send_sem=map_send.at[peer], recv_sem=map_recv.at[peer],
            device_id={"seq": peer}, device_id_type=MESH)

    def state_arrival(peer):
        return pltpu.make_async_remote_copy(
            src_ref=sent_state.at[peer], dst_ref=got_state.at[peer],
            send_sem=state_send.at[peer], recv_sem=state_recv.at[peer],
            device_id={"seq": peer}, device_id_type=MESH)

    for peer in peers:
        map_arrival(peer).wait_recv()

    def after(later, earlier):
        contracted = jnp.where(offset_half, 0.0, later).astype(BF16)
        operand = earlier.astype(BF16)
        return earlier + later - dot(contracted, jnp.concatenate([operand, operand], axis=0))

    step = [got_map[s].astype(F32) for s in range(seq_count)]
    state = [None] * seq_count
    state[0] = jnp.where(offset_half, jnp.concatenate([init_v[...], init_v[...]], axis=1), 0.0)
    runs = range(seq_count // 4)
    one = [step[4 * g] for g in runs]
    two = [after(step[4 * g + 1], step[4 * g]) for g in runs]
    last_two = [after(step[4 * g + 3], step[4 * g + 2]) for g in runs[:-1]]
    four = [after(last_two[g], two[g]) for g in runs[:-1]]
    three = [after(step[4 * g + 2], two[g]) for g in runs]
    state[4] = after(four[0], state[0])
    eight = after(four[1], four[0])
    next_eight = after(four[2], four[1])
    prefixes = (one, two, three)

    def fill(g):
        for i in range(3):
            state[4 * g + i + 1] = after(prefixes[i][g], state[4 * g])

    fill(0)
    state[8] = after(eight, state[0])
    state[12] = after(next_eight, state[4])
    for g in runs[1:]:
        fill(g)
    for s in range(seq_count):
        sent_state[s] = jnp.where(offset_half, state[s], 0.0).astype(BF16)

    @pl.when(section == 0)
    def _():
        for peer in peers + [me]:
            first_copy(peer).start()

    for peer in peers:
        state_copy(peer).start()
    got_state[me] = sent_state[me]

    for peer in peers:
        state_arrival(peer).wait_recv()

    def write_out(piece, value):
        out[0, :, piece] = value

    tail(query_map, offset, got_state, wout_v, write_out)

    for peer in peers:
        map_copy(peer).wait_send()
        state_copy(peer).wait_send()

    @pl.when(section == 0)
    def _():
        for index in range(chunks + 4):
            side_copy(index).wait_send()
        for peer in peers + [me]:
            first_copy(peer).wait_send()


def solution(mesh):
    seq_count = mesh.shape["seq"]

    def shards(tokens, norm_gain, w_qkv, w_rate, rate_base, init_state, w_out):
        rows, width = tokens.shape
        heads = rate_base.shape[1]
        inner_width = heads * HD
        groups = inner_width // GROUP
        chunks = 4
        chunk = width // chunks
        hbm = pl.BlockSpec(memory_space=pltpu.HBM)

        def body(*refs):
            kernel(seq_count, *refs)

        return pl.pallas_call(
            body,
            name="layers",
            out_shape=jax.ShapeDtypeStruct((1, rows, width), BF16),
            in_specs=[hbm] * 7,
            out_specs=pl.BlockSpec(memory_space=pltpu.VMEM),
            scratch_shapes=[
                pltpu.VMEM((rows, width), BF16),
                pltpu.VMEM((1, width), F32),
                pltpu.VMEM((groups, width, 2 * GROUP), BF16),
                pltpu.VMEM((groups, width, GROUP), BF16),
                pltpu.VMEM((heads, width), BF16),
                pltpu.VMEM((1, heads), F32),
                pltpu.VMEM((chunks, inner_width, chunk), BF16),
                pltpu.VMEM((HD, HD), F32),
                pltpu.VMEM((rows, width), BF16),
                pltpu.VMEM((rows, PAIR), F32),
                pltpu.VMEM((rows, inner_width), F32),
                pltpu.VMEM((heads // 2, rows, PAIR), BF16),
                pltpu.VMEM((heads // 2, rows, 2 * PAIR), BF16),
                pltpu.VMEM((heads // 2, PAIR, 2 * PAIR), BF16),
                pltpu.VMEM((heads, HD, PAIR), BF16),
                pltpu.VMEM((seq_count, HD, PAIR), BF16),
                pltpu.VMEM((seq_count, HD, PAIR), BF16),
                pltpu.VMEM((heads, HD, PAIR), BF16),
                pltpu.VMEM((heads // 2, rows, PAIR), BF16),
                pltpu.VMEM((heads // 2, rows, PAIR), F32),
                pltpu.VMEM((chunks, inner_width, chunk), BF16),
                pltpu.VMEM((seq_count, HD, PAIR), BF16),
                pltpu.VMEM((heads // 2, rows, PAIR), BF16),
                pltpu.VMEM((heads // 2, rows, PAIR), F32),
                pltpu.SemaphoreType.DMA((5,)),
                pltpu.SemaphoreType.DMA((4, max(groups, chunks))),
                pltpu.SemaphoreType.DMA((heads,)),
                pltpu.SemaphoreType.DMA((seq_count,)),
                pltpu.SemaphoreType.DMA((seq_count,)),
                pltpu.SemaphoreType.DMA((heads,)),
                pltpu.SemaphoreType.DMA((seq_count,)),
                pltpu.SemaphoreType.DMA((seq_count,)),
                pltpu.SemaphoreType.DMA((chunks + 4,)),
                pltpu.SemaphoreType.DMA((chunks + 4,)),
            ],
            compiler_params=pltpu.CompilerParams(
                collective_id=0, has_side_effects=True, vmem_limit_bytes=40 * 1024 * 1024),
        )(*(
            pltpu.with_memory_space_constraint(array, pltpu.HBM)
            for array in (
                tokens, norm_gain, w_qkv, jnp.swapaxes(w_rate, 1, 2), rate_base, init_state, w_out)
        ))

    return jax.shard_map(
        shards,
        mesh=mesh,
        in_specs=(
            P(("traj", "seq"), None),
            P("section", None),
            P("section", None, None),
            P("section", None, None),
            P("section", None),
            P("section", None, None, None),
            P("section", None, None),
        ),
        out_specs=P("section", ("traj", "seq"), None),
        check_vma=False,
    )
```

```python
import jax
import jax.numpy as jnp
from jax import lax
from jax.experimental import pallas as pl
from jax.experimental.pallas import tpu as pltpu
from jax.sharding import PartitionSpec as P

HD = 64
MB = 64
PAIR = 2 * HD
GROUP = 4 * HD
EPS = 1e-06
MESH = pl.DeviceIdType.MESH
F32 = jnp.float32
BF16 = jnp.bfloat16


def dot(a, b, dims=((1,), (0,))):
    return lax.dot_general(a, b, (dims, ((), ())), preferred_element_type=F32)


def split(x):
    high = x.astype(BF16)
    return high, (x - high.astype(F32)).astype(BF16)


def iota(shape, axis):
    return lax.broadcasted_iota(jnp.int32, shape, axis)


def head_ones():
    same = iota((GROUP, GROUP), 0) // HD == iota((GROUP, GROUP), 1) // HD
    return jnp.where(same, 1.0, 0.0).astype(BF16)


def unit_scale(x, row_scale, ones):
    return row_scale * lax.rsqrt(row_scale * row_scale * dot((x * x).astype(BF16), ones) + EPS)


def kernel(
    seq_count,
    tok, gain, w_qkv, w_rate, rate_base, init_state, w_out,
    out,
    hidden, gain_v, wkv_v, wq_v, wrate_v, rbase_v, wout_v, init_v,
    normed, scaled_rows, rate_all, keys, scaled, first_map, sent_map, got_map, sent_state, got_state,
    query_map, offset, wout_first, state_first, query_first, offset_first,
    load_sem, weight_sem,
    map_send, map_recv, state_send, state_recv, first_send, first_recv, side_send, side_recv,
):
    section = lax.axis_index("section")
    me = lax.axis_index("seq")
    rows, width = tok.shape
    heads = rate_base.shape[1]
    inner_width = heads * HD
    groups = inner_width // GROUP
    chunks = 4
    chunk = width // chunks
    side = 4
    row_of, column_of = me // side, lax.rem(me, side)
    order = [lax.rem(row_of + turn, groups) for turn in (2, 1, 3, 0)]

    token_copy = pltpu.make_async_copy(tok, hidden, load_sem.at[0])
    token_copy.start()
    small = [
        pltpu.make_async_copy(gain, gain_v, load_sem.at[1]),
        pltpu.make_async_copy(w_rate.at[0], wrate_v, load_sem.at[2]),
        pltpu.make_async_copy(rate_base, rbase_v, load_sem.at[3]),
        pltpu.make_async_copy(init_state.at[0, me], init_v, load_sem.at[4]),
    ]
    for copy in small:
        copy.start()

    def columns(start, p):
        return pl.ds(pl.multiple_of(start + order[p] * GROUP, GROUP), GROUP)

    def key_copy(p):
        return pltpu.make_async_copy(
            w_qkv.at[0, :, columns(inner_width, p)],
            wkv_v.at[p, :, pl.ds(0, GROUP)], weight_sem.at[0, p])

    def value_copy(p):
        return pltpu.make_async_copy(
            w_qkv.at[0, :, columns(2 * inner_width, p)],
            wkv_v.at[p, :, pl.ds(GROUP, GROUP)], weight_sem.at[1, p])

    def query_copy(p):
        return pltpu.make_async_copy(
            w_qkv.at[0, :, columns(0, p)], wq_v.at[p], weight_sem.at[2, p])

    def out_weight_copy(p):
        return pltpu.make_async_copy(
            w_out.at[0, columns(0, p), :], wout_v.at[p], weight_sem.at[3, p])

    half = groups // 2
    for g in range(half):
        key_copy(g).start()
        value_copy(g).start()

    barrier = pltpu.get_barrier_semaphore()
    steps = [(y, x) for y in range(seq_count // side) for x in range(side)][1:]
    steps.sort(key=lambda s: -min(s[0], seq_count // side - s[0]) - min(s[1], side - s[1]))
    peers = [
        lax.rem(row_of + y, seq_count // side) * side + lax.rem(column_of + x, side)
        for y, x in steps]
    for peer in peers:
        for other in range(2):
            pl.semaphore_signal(
                barrier, inc=1, device_id={"section": other, "seq": peer}, device_id_type=MESH)
    pl.semaphore_signal(barrier, inc=1, device_id={"section": 1 - section}, device_id_type=MESH)
    entered = 2 * seq_count - 1

    def tail(maps, offsets, states, weights, write):
        parts = []
        for pair in range(heads // 2):
            h = 2 * (2 * order[pair // 2] + pair % 2)
            start = jnp.concatenate([states[h], states[h + 1]], axis=0)
            parts.append((dot(maps[pair], start) + offsets[pair]).astype(BF16))
        inner = jnp.concatenate(parts, axis=1)
        for n in range(chunks):
            piece = slice(n * chunk, (n + 1) * chunk)
            weight = jnp.concatenate([weights[p, :, piece] for p in range(groups)], axis=0)
            write(piece, (hidden[:, piece].astype(F32) + dot(inner, weight)).astype(BF16))

    early_pairs = heads // 2 - 2

    def side_copy(index):
        if index < groups:
            source, target = wout_v.at[index], wout_first.at[index]
        else:
            pairs = pl.ds(0, early_pairs) if index < groups + 2 else pl.ds(early_pairs, 2)
            source, target = [
                (query_map.at[pairs], query_first.at[pairs]),
                (offset.at[pairs], offset_first.at[pairs])][(index - groups) % 2]
        return pltpu.make_async_remote_copy(
            src_ref=source, dst_ref=target,
            send_sem=side_send.at[index], recv_sem=side_recv.at[index],
            device_id={"section": 1 - section}, device_id_type=MESH)

    def first_copy(peer):
        return pltpu.make_async_remote_copy(
            src_ref=sent_state.at[peer], dst_ref=state_first.at[me],
            send_sem=first_send.at[peer], recv_sem=first_recv.at[me],
            device_id={"section": 1 - section, "seq": peer}, device_id_type=MESH)

    def first_arrival(peer):
        return pltpu.make_async_remote_copy(
            src_ref=sent_state.at[peer], dst_ref=state_first.at[peer],
            send_sem=first_send.at[peer], recv_sem=first_recv.at[peer],
            device_id={"section": 1 - section, "seq": peer}, device_id_type=MESH)

    for copy in small:
        copy.wait()
    token_copy.wait()

    def norm():
        wide = hidden[...].astype(F32)
        row_scale = lax.rsqrt(jnp.mean(wide * wide, axis=-1, keepdims=True) + EPS)
        scaled_rows[...] = jnp.broadcast_to(row_scale, (rows, PAIR))
        normed[...] = (wide * gain_v[...]).astype(BF16)
        return row_scale

    def rate_parts(row_scale):
        return split(rbase_v[...] * jax.nn.sigmoid(
            row_scale * dot(normed[...], wrate_v[...], ((1,), (1,)))))

    def rate_spread(parts):
        head, lane = iota((heads, GROUP), 0), iota((heads, GROUP), 1)
        spread = jnp.concatenate([
            jnp.where(head == side * g + lane // HD, 1.0, 0.0) for g in order], axis=1).astype(BF16)
        rate_all[...] = dot(parts[0], spread) + dot(parts[1], spread)

    lane_low = iota((HD, PAIR), 1) < HD
    wide_shape = (PAIR, 4 * PAIR)
    diagonal = iota(wide_shape, 0) // HD == (iota(wide_shape, 1) % PAIR) // HD
    ones = head_ones()
    blank = jnp.zeros((MB, 2 * PAIR), BF16)

    def map_copy(peer):
        return pltpu.make_async_remote_copy(
            src_ref=sent_map.at[peer], dst_ref=got_map.at[me],
            send_sem=map_send.at[peer], recv_sem=map_recv.at[me],
            device_id={"seq": peer}, device_id_type=MESH)

    def row_factor():
        return jnp.concatenate([scaled_rows[...]] * (GROUP // PAIR), axis=1)

    def key_dot(g):
        return dot(normed[...], wkv_v[g])

    def key_scale(g, both):
        key, value = both[:, :GROUP], both[:, GROUP:]
        row_wide = row_factor()
        scale = unit_scale(key, row_wide, ones)
        rate = rate_all[:, g * GROUP:(g + 1) * GROUP] * scale
        key_bf = key.astype(BF16)
        rated_value = (rate * (row_wide * value)).astype(BF16)
        rated_key = (rate * scale * key).astype(BF16)
        made = []
        for i in range(2):
            lanes = slice(i * PAIR, (i + 1) * PAIR)
            pair_key = key_bf[:, lanes]
            pair_scaled = jnp.concatenate([rated_value[:, lanes], rated_key[:, lanes]], axis=1)
            keys[2 * g + i] = pair_key
            scaled[2 * g + i] = pair_scaled
            made.append((pair_key, pair_scaled))
        return made

    def key_maps(g, made):
        found = []
        for i, (pair_key, pair_scaled) in enumerate(made):
            by_block = jnp.concatenate([
                jnp.concatenate([pair_scaled[:MB], blank], axis=1),
                jnp.concatenate([blank, pair_scaled[MB:]], axis=1)], axis=0)
            maps = jnp.where(diagonal, dot(pair_key, by_block, ((0,), (0,))), 0.0)
            first_bf = maps[:, :2 * PAIR].astype(BF16)
            first_map[2 * g + i] = first_bf
            found.append((maps, first_bf))
        return found

    def key_pack(g, found):
        for i, (maps, first_bf) in enumerate(found):
            first, second = maps[:, :2 * PAIR], maps[:, 2 * PAIR:]
            total = first + second - dot(second[:, PAIR:].astype(BF16), first_bf)
            packed = total[:HD] + total[HD:]
            pack_b, pack_d = packed[:, :PAIR], pltpu.roll(packed[:, PAIR:], HD, 1)
            h = side * order[g] + 2 * i
            sent_map[h] = jnp.where(lane_low, pack_b, pack_d).astype(BF16)
            sent_map[h + 1] = jnp.where(lane_low, pack_d, pack_b).astype(BF16)
        own = g == groups - 1
        for turn in (2, 1, 3) if own else (2, 1, 3, 0):
            map_copy(side * order[g] + lax.rem(column_of + turn, side)).start()

    def key_groups(which, before=lambda position: None, gap=0):
        wait = [lambda g, value: value] * gap
        pipeline([lambda g, unused: key_dot(g)] + wait + [key_scale, key_maps, key_pack], which, before)

    def pipeline(stages, which, before=lambda position: None):
        held = {}
        for step in range(len(which) + len(stages) - 1):
            if step < len(which):
                before(step)
            for depth, stage in enumerate(stages):
                position = step - depth
                if 0 <= position < len(which):
                    held[position] = stage(which[position], held.get(position))

    @pl.when(section == 0)
    def _():
        for g in range(half, groups - 1):
            key_copy(g).start()
            value_copy(g).start()
        rate_spread(rate_parts(norm()))
        pl.semaphore_wait(barrier, entered)
        for g in range(half):
            key_copy(g).wait()
            value_copy(g).wait()
            if g == 0:
                key_copy(groups - 1).start()
                value_copy(groups - 1).start()
        key_groups(range(half))
        for g in range(groups):
            query_copy(g).start()
        def arrive(position):
            key_copy(half + position).wait()
            value_copy(half + position).wait()
            if position == groups - half - 1:
                for n in range(groups):
                    out_weight_copy(n).start()

        key_groups(range(half, groups), arrive)

    @pl.when(section == 1)
    def _():
        for g in range(half, groups):
            key_copy(g).start()
            value_copy(g).start()
        for g in range(groups):
            query_copy(g).start()
        for n in range(groups):
            out_weight_copy(n).start()
        for g in range(groups):
            key_copy(g).wait()
            value_copy(g).wait()
        for g in range(groups):
            query_copy(g).wait()
        for n in range(groups):
            out_weight_copy(n).wait()
        pl.semaphore_wait(barrier, entered)
        for index in range(groups + 4):
            side_copy(index).wait_recv()
        for peer in peers + [me]:
            first_arrival(peer).wait_recv()

        def write(piece, value):
            hidden[:, piece] = value

        tail(query_first, offset_first, state_first, wout_first, write)
        row_scale = norm()
        parts = []

        def rates(position):
            if position == 1:
                parts.append(rate_parts(row_scale))
            if position == 2:
                rate_spread(parts[0])

        key_groups(range(groups), rates, gap=1)

    got_map[me] = sent_map[me]

    row = iota((4 * MB, PAIR), 0)
    column = iota((4 * MB, PAIR), 1)
    causal = (column // MB == row // PAIR) & (column % MB <= row % MB)
    low_half = iota((MB, 2 * PAIR), 1) % PAIR < HD

    def query_scores(g, query_all):
        scale_all = unit_scale(query_all, row_factor(), ones)
        made = []
        for i in range(2):
            query = query_all[:, i * PAIR:(i + 1) * PAIR]
            parts = []
            for b in range(2):
                piece = query[b * MB:(b + 1) * MB]
                parts += [jnp.where(lane_low, piece, 0.0), jnp.where(lane_low, 0.0, piece)]
            stacked = jnp.concatenate(parts, axis=0).astype(BF16)
            scores = jnp.where(causal, dot(stacked, keys[2 * g + i], ((1,), (1,))), 0.0)
            made.append((query, scale_all[:, i * PAIR:(i + 1) * PAIR], scores.astype(BF16)))
        return made

    def query_mix(g, made):
        found = []
        for i, (query, scale, scores) in enumerate(made):
            pair = 2 * g + i
            mixed = dot(scores, scaled[pair])
            mix_one = jnp.where(low_half, mixed[:MB], mixed[MB:2 * MB])
            mix_two = jnp.where(low_half, mixed[2 * MB:3 * MB], mixed[3 * MB:])
            map_one = query[:MB] - mix_one[:, PAIR:]
            map_two = query[MB:] - mix_two[:, PAIR:]
            query_map[pair, pl.ds(0, MB), :] = (scale[:MB] * map_one).astype(BF16)
            offset[pair, pl.ds(0, MB), :] = scale[:MB] * mix_one[:, :PAIR]
            found.append((map_two, mix_two[:, :PAIR], scale[MB:]))
        return found

    def query_through(g, found):
        for i, (map_two, mix_two, scale) in enumerate(found):
            pair = 2 * g + i
            through = dot(map_two.astype(BF16), first_map[pair])
            query_map[pair, pl.ds(MB, MB), :] = (
                scale * (map_two - through[:, PAIR:])).astype(BF16)
            offset[pair, pl.ds(MB, MB), :] = scale * (mix_two + through[:, :PAIR])

    def query_groups(which):
        pipeline(
            [lambda g, unused: dot(normed[...], wq_v[g]), query_scores, query_mix, query_through],
            which)

    @pl.when(section == 0)
    def _():
        for g in range(groups):
            query_copy(g).wait()

    query_groups(range(groups - 1))

    @pl.when(section == 0)
    def _():
        for n in range(groups):
            out_weight_copy(n).wait()
        for index in range(groups + 2):
            side_copy(index).start()

    odd = lax.rem(me, 2)
    offset_half = (iota((HD, PAIR), 1) // HD) == odd

    def state_copy(peer):
        return pltpu.make_async_remote_copy(
            src_ref=sent_state.at[peer], dst_ref=got_state.at[me],
            send_sem=state_send.at[peer], recv_sem=state_recv.at[me],
            device_id={"seq": peer}, device_id_type=MESH)

    def map_arrival(peer):
        return pltpu.make_async_remote_copy(
            src_ref=sent_map.at[peer], dst_ref=got_map.at[peer],
            send_sem=map_send.at[peer], recv_sem=map_recv.at[peer],
            device_id={"seq": peer}, device_id_type=MESH)

    def state_arrival(peer):
        return pltpu.make_async_remote_copy(
            src_ref=sent_state.at[peer], dst_ref=got_state.at[peer],
            send_sem=state_send.at[peer], recv_sem=state_recv.at[peer],
            device_id={"seq": peer}, device_id_type=MESH)

    for peer in peers:
        map_arrival(peer).wait_recv()

    def after(later, earlier):
        contracted = jnp.where(offset_half, 0.0, later).astype(BF16)
        operand = earlier.astype(BF16)
        return earlier + later - dot(contracted, jnp.concatenate([operand, operand], axis=0))

    step = [got_map[s].astype(F32) for s in range(seq_count)]
    state = [None] * seq_count
    state[0] = jnp.where(offset_half, jnp.concatenate([init_v[...], init_v[...]], axis=1), 0.0)
    runs = range(seq_count // 4)
    one = [step[4 * g] for g in runs]
    two = [after(step[4 * g + 1], step[4 * g]) for g in runs]
    last_two = [after(step[4 * g + 3], step[4 * g + 2]) for g in runs[:-1]]
    four = [after(last_two[g], two[g]) for g in runs[:-1]]
    three = [after(step[4 * g + 2], two[g]) for g in runs]
    state[4] = after(four[0], state[0])
    eight = after(four[1], four[0])
    next_eight = after(four[2], four[1])
    prefixes = (one, two, three)

    def fill(g):
        for i in range(3):
            state[4 * g + i + 1] = after(prefixes[i][g], state[4 * g])

    fill(0)
    state[8] = after(eight, state[0])
    state[12] = after(next_eight, state[4])
    for g in runs[1:]:
        fill(g)
    for s in range(seq_count):
        sent_state[s] = jnp.where(offset_half, state[s], 0.0).astype(BF16)

    @pl.when(section == 0)
    def _():
        for peer in peers + [me]:
            first_copy(peer).start()

    for peer in peers:
        state_copy(peer).start()
    got_state[me] = sent_state[me]

    query_groups(range(groups - 1, groups))

    @pl.when(section == 0)
    def _():
        for index in range(groups + 2, groups + 4):
            side_copy(index).start()

    for peer in peers:
        state_arrival(peer).wait_recv()

    def write_out(piece, value):
        out[0, :, piece] = value

    tail(query_map, offset, got_state, wout_v, write_out)

    for peer in peers:
        map_copy(peer).wait_send()
        state_copy(peer).wait_send()

    @pl.when(section == 0)
    def _():
        for index in range(groups + 4):
            side_copy(index).wait_send()
        for peer in peers + [me]:
            first_copy(peer).wait_send()


def solution(mesh):
    seq_count = mesh.shape["seq"]

    def shards(tokens, norm_gain, w_qkv, w_rate, rate_base, init_state, w_out):
        rows, width = tokens.shape
        heads = rate_base.shape[1]
        inner_width = heads * HD
        groups = inner_width // GROUP
        hbm = pl.BlockSpec(memory_space=pltpu.HBM)

        def body(*refs):
            kernel(seq_count, *refs)

        return pl.pallas_call(
            body,
            name="layers",
            out_shape=jax.ShapeDtypeStruct((1, rows, width), BF16),
            in_specs=[hbm] * 7,
            out_specs=pl.BlockSpec(memory_space=pltpu.VMEM),
            scratch_shapes=[
                pltpu.VMEM((rows, width), BF16),
                pltpu.VMEM((1, width), F32),
                pltpu.VMEM((groups, width, 2 * GROUP), BF16),
                pltpu.VMEM((groups, width, GROUP), BF16),
                pltpu.VMEM((heads, width), BF16),
                pltpu.VMEM((1, heads), F32),
                pltpu.VMEM((groups, GROUP, width), BF16),
                pltpu.VMEM((HD, HD), F32),
                pltpu.VMEM((rows, width), BF16),
                pltpu.VMEM((rows, PAIR), F32),
                pltpu.VMEM((rows, inner_width), F32),
                pltpu.VMEM((heads // 2, rows, PAIR), BF16),
                pltpu.VMEM((heads // 2, rows, 2 * PAIR), BF16),
                pltpu.VMEM((heads // 2, PAIR, 2 * PAIR), BF16),
                pltpu.VMEM((heads, HD, PAIR), BF16),
                pltpu.VMEM((seq_count, HD, PAIR), BF16),
                pltpu.VMEM((seq_count, HD, PAIR), BF16),
                pltpu.VMEM((heads, HD, PAIR), BF16),
                pltpu.VMEM((heads // 2, rows, PAIR), BF16),
                pltpu.VMEM((heads // 2, rows, PAIR), F32),
                pltpu.VMEM((groups, GROUP, width), BF16),
                pltpu.VMEM((seq_count, HD, PAIR), BF16),
                pltpu.VMEM((heads // 2, rows, PAIR), BF16),
                pltpu.VMEM((heads // 2, rows, PAIR), F32),
                pltpu.SemaphoreType.DMA((5,)),
                pltpu.SemaphoreType.DMA((4, groups)),
                pltpu.SemaphoreType.DMA((heads,)),
                pltpu.SemaphoreType.DMA((seq_count,)),
                pltpu.SemaphoreType.DMA((seq_count,)),
                pltpu.SemaphoreType.DMA((heads,)),
                pltpu.SemaphoreType.DMA((seq_count,)),
                pltpu.SemaphoreType.DMA((seq_count,)),
                pltpu.SemaphoreType.DMA((groups + 4,)),
                pltpu.SemaphoreType.DMA((groups + 4,)),
            ],
            compiler_params=pltpu.CompilerParams(
                collective_id=0, has_side_effects=True, vmem_limit_bytes=40 * 1024 * 1024),
        )(*(
            pltpu.with_memory_space_constraint(array, pltpu.HBM)
            for array in (
                tokens, norm_gain, w_qkv, jnp.swapaxes(w_rate, 1, 2), rate_base, init_state, w_out)
        ))

    return jax.shard_map(
        shards,
        mesh=mesh,
        in_specs=(
            P(("traj", "seq"), None),
            P("section", None),
            P("section", None, None),
            P("section", None, None),
            P("section", None),
            P("section", None, None, None),
            P("section", None, None),
        ),
        out_specs=P("section", ("traj", "seq"), None),
        check_vma=False,
    )
```

```python
import jax
import jax.numpy as jnp
from jax import lax
from jax.experimental import pallas as pl
from jax.experimental.pallas import tpu as pltpu
from jax.sharding import PartitionSpec as P

HD = 64
MB = 64
PAIR = 2 * HD
GROUP = 4 * HD
EPS = 1e-06
MESH = pl.DeviceIdType.MESH
F32 = jnp.float32
BF16 = jnp.bfloat16


def dot(a, b, dims=((1,), (0,))):
    return lax.dot_general(a, b, (dims, ((), ())), preferred_element_type=F32)


def split(x):
    high = x.astype(BF16)
    return high, (x - high.astype(F32)).astype(BF16)


def iota(shape, axis):
    return lax.broadcasted_iota(jnp.int32, shape, axis)


def head_ones():
    same = iota((GROUP, GROUP), 0) // HD == iota((GROUP, GROUP), 1) // HD
    return jnp.where(same, 1.0, 0.0).astype(BF16)


def unit_scale(x, row_scale, ones):
    return row_scale * lax.rsqrt(row_scale * row_scale * dot((x * x).astype(BF16), ones) + EPS)


def kernel(
    seq_count,
    tok, gain, w_qkv, w_rate, rate_base, init_state, w_out,
    out,
    hidden, gain_v, wkv_v, wq_v, wrate_v, rbase_v, wout_v, init_v,
    normed, scaled_rows, rate_all, keys, scaled, first_map, sent_map, got_map, sent_state, got_state,
    query_map, offset, wout_first, state_first, query_first, offset_first,
    load_sem, weight_sem,
    map_send, map_recv, state_send, state_recv, first_send, first_recv, side_send, side_recv,
):
    section = lax.axis_index("section")
    me = lax.axis_index("seq")
    rows, width = tok.shape
    heads = rate_base.shape[1]
    inner_width = heads * HD
    groups = inner_width // GROUP
    chunks = 4
    chunk = width // chunks
    side = 4
    row_of, column_of = me // side, lax.rem(me, side)
    order = [lax.rem(row_of + turn, groups) for turn in (2, 1, 3, 0)]

    token_copy = pltpu.make_async_copy(tok, hidden, load_sem.at[0])
    token_copy.start()
    small = [
        pltpu.make_async_copy(gain, gain_v, load_sem.at[1]),
        pltpu.make_async_copy(w_rate.at[0], wrate_v, load_sem.at[2]),
        pltpu.make_async_copy(rate_base, rbase_v, load_sem.at[3]),
        pltpu.make_async_copy(init_state.at[0, me], init_v, load_sem.at[4]),
    ]
    for copy in small:
        copy.start()

    def columns(start, p):
        return pl.ds(pl.multiple_of(start + order[p] * GROUP, GROUP), GROUP)

    def key_copy(p):
        return pltpu.make_async_copy(
            w_qkv.at[0, :, columns(inner_width, p)],
            wkv_v.at[p, :, pl.ds(0, GROUP)], weight_sem.at[0, p])

    def value_copy(p):
        return pltpu.make_async_copy(
            w_qkv.at[0, :, columns(2 * inner_width, p)],
            wkv_v.at[p, :, pl.ds(GROUP, GROUP)], weight_sem.at[1, p])

    def query_copy(p):
        return pltpu.make_async_copy(
            w_qkv.at[0, :, columns(0, p)], wq_v.at[p], weight_sem.at[2, p])

    def out_weight_copy(p):
        return pltpu.make_async_copy(
            w_out.at[0, columns(0, p), :], wout_v.at[p], weight_sem.at[3, p])

    half = groups // 2
    for g in range(half):
        key_copy(g).start()
        value_copy(g).start()

    barrier = pltpu.get_barrier_semaphore()
    steps = [(y, x) for y in range(seq_count // side) for x in range(side)][1:]
    steps.sort(key=lambda s: -min(s[0], seq_count // side - s[0]) - min(s[1], side - s[1]))
    peers = [
        lax.rem(row_of + y, seq_count // side) * side + lax.rem(column_of + x, side)
        for y, x in steps]
    for peer in peers:
        for other in range(2):
            pl.semaphore_signal(
                barrier, inc=1, device_id={"section": other, "seq": peer}, device_id_type=MESH)
    pl.semaphore_signal(barrier, inc=1, device_id={"section": 1 - section}, device_id_type=MESH)
    entered = 2 * seq_count - 1

    def spread_state(packed, parity):
        packed = packed.astype(F32)
        own = (iota(packed.shape, 1) // HD) == parity
        return [
            jnp.where(own, part, 0.0).astype(BF16)
            for part in (packed, pltpu.roll(packed, HD, 1))]

    def tail(maps, offsets, states, weights, write):
        parts = []
        for pair in range(heads // 2):
            h = 2 * (2 * order[pair // 2] + pair % 2)
            start = jnp.concatenate(spread_state(states[h], 0) + spread_state(states[h + 1], 1), axis=0)
            parts.append((dot(maps[pair], start) + offsets[pair]).astype(BF16))
        inner = jnp.concatenate(parts, axis=1)
        for n in range(chunks):
            piece = slice(n * chunk, (n + 1) * chunk)
            weight = jnp.concatenate([weights[p, :, piece] for p in range(groups)], axis=0)
            write(piece, (hidden[:, piece].astype(F32) + dot(inner, weight)).astype(BF16))

    early_pairs = heads // 2 - 2

    def side_copy(index):
        if index < groups:
            source, target = wout_v.at[index], wout_first.at[index]
        else:
            pairs = pl.ds(0, early_pairs) if index < groups + 2 else pl.ds(early_pairs, 2)
            source, target = [
                (query_map.at[pairs], query_first.at[pairs]),
                (offset.at[pairs], offset_first.at[pairs])][(index - groups) % 2]
        return pltpu.make_async_remote_copy(
            src_ref=source, dst_ref=target,
            send_sem=side_send.at[index], recv_sem=side_recv.at[index],
            device_id={"section": 1 - section}, device_id_type=MESH)

    def first_copy(peer):
        return pltpu.make_async_remote_copy(
            src_ref=sent_state.at[peer], dst_ref=state_first.at[me],
            send_sem=first_send.at[peer], recv_sem=first_recv.at[me],
            device_id={"section": 1 - section, "seq": peer}, device_id_type=MESH)

    def first_arrival(peer):
        return pltpu.make_async_remote_copy(
            src_ref=sent_state.at[peer], dst_ref=state_first.at[peer],
            send_sem=first_send.at[peer], recv_sem=first_recv.at[peer],
            device_id={"section": 1 - section, "seq": peer}, device_id_type=MESH)

    for copy in small:
        copy.wait()
    token_copy.wait()

    def norm():
        wide = hidden[...].astype(F32)
        row_scale = lax.rsqrt(jnp.mean(wide * wide, axis=-1, keepdims=True) + EPS)
        scaled_rows[...] = jnp.broadcast_to(row_scale, (rows, PAIR))
        normed[...] = (wide * gain_v[...]).astype(BF16)
        return row_scale

    def rate_parts(row_scale):
        return split(rbase_v[...] * jax.nn.sigmoid(
            row_scale * dot(normed[...], wrate_v[...], ((1,), (1,)))))

    def rate_spread(parts):
        head, lane = iota((heads, GROUP), 0), iota((heads, GROUP), 1)
        spread = jnp.concatenate([
            jnp.where(head == side * g + lane // HD, 1.0, 0.0) for g in order], axis=1).astype(BF16)
        rate_all[...] = dot(parts[0], spread) + dot(parts[1], spread)

    lane_low = iota((HD, PAIR), 1) < HD
    wide_shape = (PAIR, 4 * PAIR)
    diagonal = iota(wide_shape, 0) // HD == (iota(wide_shape, 1) % PAIR) // HD
    ones = head_ones()
    blank = jnp.zeros((MB, 2 * PAIR), BF16)

    def map_copy(peer):
        return pltpu.make_async_remote_copy(
            src_ref=sent_map.at[peer], dst_ref=got_map.at[me],
            send_sem=map_send.at[peer], recv_sem=map_recv.at[me],
            device_id={"seq": peer}, device_id_type=MESH)

    def row_factor():
        return jnp.concatenate([scaled_rows[...]] * (GROUP // PAIR), axis=1)

    def key_dot(g):
        return dot(normed[...], wkv_v[g])

    def key_scale(g, both):
        key, value = both[:, :GROUP], both[:, GROUP:]
        row_wide = row_factor()
        scale = unit_scale(key, row_wide, ones)
        rate = rate_all[:, g * GROUP:(g + 1) * GROUP] * scale
        key_bf = key.astype(BF16)
        rated_value = (rate * (row_wide * value)).astype(BF16)
        rated_key = (rate * scale * key).astype(BF16)
        made = []
        for i in range(2):
            lanes = slice(i * PAIR, (i + 1) * PAIR)
            pair_key = key_bf[:, lanes]
            pair_scaled = jnp.concatenate([rated_value[:, lanes], rated_key[:, lanes]], axis=1)
            keys[2 * g + i] = pair_key
            scaled[2 * g + i] = pair_scaled
            made.append((pair_key, pair_scaled))
        return made

    def key_maps(g, made):
        found = []
        for i, (pair_key, pair_scaled) in enumerate(made):
            by_block = jnp.concatenate([
                jnp.concatenate([pair_scaled[:MB], blank], axis=1),
                jnp.concatenate([blank, pair_scaled[MB:]], axis=1)], axis=0)
            maps = jnp.where(diagonal, dot(pair_key, by_block, ((0,), (0,))), 0.0)
            first_bf = maps[:, :2 * PAIR].astype(BF16)
            first_map[2 * g + i] = first_bf
            found.append((maps, first_bf))
        return found

    def key_pack(g, found):
        for i, (maps, first_bf) in enumerate(found):
            first, second = maps[:, :2 * PAIR], maps[:, 2 * PAIR:]
            total = first + second - dot(second[:, PAIR:].astype(BF16), first_bf)
            packed = total[:HD] + total[HD:]
            pack_b, pack_d = packed[:, :PAIR], pltpu.roll(packed[:, PAIR:], HD, 1)
            h = side * order[g] + 2 * i
            sent_map[h] = jnp.where(lane_low, pack_b, pack_d).astype(BF16)
            sent_map[h + 1] = jnp.where(lane_low, pack_d, pack_b).astype(BF16)
        own = g == groups - 1
        for turn in (2, 1, 3) if own else (2, 1, 3, 0):
            map_copy(side * order[g] + lax.rem(column_of + turn, side)).start()

    def key_groups(which, before=lambda position: None, gap=0):
        wait = [lambda g, value: value] * gap
        pipeline([lambda g, unused: key_dot(g)] + wait + [key_scale, key_maps, key_pack], which, before)

    def pipeline(stages, which, before=lambda position: None):
        held = {}
        for step in range(len(which) + len(stages) - 1):
            if step < len(which):
                before(step)
            for depth, stage in enumerate(stages):
                position = step - depth
                if 0 <= position < len(which):
                    held[position] = stage(which[position], held.get(position))

    @pl.when(section == 0)
    def _():
        for g in range(half, groups - 1):
            key_copy(g).start()
            value_copy(g).start()
        rate_spread(rate_parts(norm()))
        pl.semaphore_wait(barrier, entered)
        for g in range(half):
            key_copy(g).wait()
            value_copy(g).wait()
            if g == 0:
                key_copy(groups - 1).start()
                value_copy(groups - 1).start()
        key_groups(range(half))
        for g in range(groups):
            query_copy(g).start()
        def arrive(position):
            key_copy(half + position).wait()
            value_copy(half + position).wait()
            if position == groups - half - 1:
                for n in range(groups):
                    out_weight_copy(n).start()

        key_groups(range(half, groups), arrive)

    @pl.when(section == 1)
    def _():
        for g in range(half, groups):
            key_copy(g).start()
            value_copy(g).start()
        for g in range(groups):
            query_copy(g).start()
        for n in range(groups):
            out_weight_copy(n).start()
        for g in range(groups):
            key_copy(g).wait()
            value_copy(g).wait()
        for g in range(groups):
            query_copy(g).wait()
        for n in range(groups):
            out_weight_copy(n).wait()
        pl.semaphore_wait(barrier, entered)
        for index in range(groups + 4):
            side_copy(index).wait_recv()
        for peer in peers + [me]:
            first_arrival(peer).wait_recv()

        def write(piece, value):
            hidden[:, piece] = value

        tail(query_first, offset_first, state_first, wout_first, write)
        row_scale = norm()
        parts = []

        def rates(position):
            if position == 1:
                parts.append(rate_parts(row_scale))
            if position == 2:
                rate_spread(parts[0])

        key_groups(range(groups), rates, gap=1)

    got_map[me] = sent_map[me]

    row = iota((4 * MB, PAIR), 0)
    column = iota((4 * MB, PAIR), 1)
    causal = (column // MB == row // PAIR) & (column % MB <= row % MB)
    low_half = iota((MB, 2 * PAIR), 1) % PAIR < HD

    def query_scores(g, query_all):
        scale_all = unit_scale(query_all, row_factor(), ones)
        made = []
        for i in range(2):
            query = query_all[:, i * PAIR:(i + 1) * PAIR]
            parts = []
            for b in range(2):
                piece = query[b * MB:(b + 1) * MB]
                parts += [jnp.where(lane_low, piece, 0.0), jnp.where(lane_low, 0.0, piece)]
            stacked = jnp.concatenate(parts, axis=0).astype(BF16)
            scores = jnp.where(causal, dot(stacked, keys[2 * g + i], ((1,), (1,))), 0.0)
            made.append((query, scale_all[:, i * PAIR:(i + 1) * PAIR], scores.astype(BF16)))
        return made

    def query_mix(g, made):
        found = []
        for i, (query, scale, scores) in enumerate(made):
            pair = 2 * g + i
            mixed = dot(scores, scaled[pair])
            mix_one = jnp.where(low_half, mixed[:MB], mixed[MB:2 * MB])
            mix_two = jnp.where(low_half, mixed[2 * MB:3 * MB], mixed[3 * MB:])
            map_one = query[:MB] - mix_one[:, PAIR:]
            map_two = query[MB:] - mix_two[:, PAIR:]
            query_map[pair, pl.ds(0, MB), :] = (scale[:MB] * map_one).astype(BF16)
            offset[pair, pl.ds(0, MB), :] = scale[:MB] * mix_one[:, :PAIR]
            found.append((map_two, mix_two[:, :PAIR], scale[MB:]))
        return found

    def query_through(g, found):
        for i, (map_two, mix_two, scale) in enumerate(found):
            pair = 2 * g + i
            through = dot(map_two.astype(BF16), first_map[pair])
            query_map[pair, pl.ds(MB, MB), :] = (
                scale * (map_two - through[:, PAIR:])).astype(BF16)
            offset[pair, pl.ds(MB, MB), :] = scale * (mix_two + through[:, :PAIR])

    def query_groups(which):
        pipeline(
            [lambda g, unused: dot(normed[...], wq_v[g]), query_scores, query_mix, query_through],
            which)

    @pl.when(section == 0)
    def _():
        for g in range(groups):
            query_copy(g).wait()

    query_groups(range(groups - 1))

    @pl.when(section == 0)
    def _():
        for n in range(groups):
            out_weight_copy(n).wait()
        for index in range(groups + 2):
            side_copy(index).start()

    odd = lax.rem(me, 2)
    offset_half = (iota((HD, PAIR), 1) // HD) == odd

    def state_copy(peer):
        return pltpu.make_async_remote_copy(
            src_ref=sent_state.at[peer], dst_ref=got_state.at[me],
            send_sem=state_send.at[peer], recv_sem=state_recv.at[me],
            device_id={"seq": peer}, device_id_type=MESH)

    def map_arrival(peer):
        return pltpu.make_async_remote_copy(
            src_ref=sent_map.at[peer], dst_ref=got_map.at[peer],
            send_sem=map_send.at[peer], recv_sem=map_recv.at[peer],
            device_id={"seq": peer}, device_id_type=MESH)

    def state_arrival(peer):
        return pltpu.make_async_remote_copy(
            src_ref=sent_state.at[peer], dst_ref=got_state.at[peer],
            send_sem=state_send.at[peer], recv_sem=state_recv.at[peer],
            device_id={"seq": peer}, device_id_type=MESH)

    for peer in peers:
        map_arrival(peer).wait_recv()

    def after(later, earlier):
        contracted = jnp.where(offset_half, 0.0, later).astype(BF16)
        operand = earlier.astype(BF16)
        return earlier + later - dot(contracted, jnp.concatenate([operand, operand], axis=0))

    step = [got_map[s].astype(F32) for s in range(seq_count)]
    state = [None] * seq_count
    state[0] = jnp.where(offset_half, jnp.concatenate([init_v[...], init_v[...]], axis=1), 0.0)
    runs = range(seq_count // 4)
    one = [step[4 * g] for g in runs]
    two = [after(step[4 * g + 1], step[4 * g]) for g in runs]
    last_two = [after(step[4 * g + 3], step[4 * g + 2]) for g in runs[:-1]]
    four = [after(last_two[g], two[g]) for g in runs[:-1]]
    three = [after(step[4 * g + 2], two[g]) for g in runs]
    state[4] = after(four[0], state[0])
    eight = after(four[1], four[0])
    next_eight = after(four[2], four[1])
    prefixes = (one, two, three)

    def fill(g):
        for i in range(3):
            state[4 * g + i + 1] = after(prefixes[i][g], state[4 * g])

    fill(0)
    state[8] = after(eight, state[0])
    state[12] = after(next_eight, state[4])
    for g in runs[1:]:
        fill(g)
    own_half = (iota((HD // 2, PAIR), 1) // HD) == odd
    for s in range(seq_count):
        sent_state[s] = jnp.where(
            own_half, state[s][:HD // 2],
            pltpu.roll(state[s][HD // 2:], HD, 1)).astype(BF16)

    @pl.when(section == 0)
    def _():
        for peer in peers + [me]:
            first_copy(peer).start()

    @pl.when(section == 1)
    def _():
        for peer in peers:
            state_copy(peer).start()

    got_state[me] = sent_state[me]

    query_groups(range(groups - 1, groups))

    @pl.when(section == 0)
    def _():
        for index in range(groups + 2, groups + 4):
            side_copy(index).start()
        for peer in peers:
            state_copy(peer).start()

    for peer in peers:
        state_arrival(peer).wait_recv()

    def write_out(piece, value):
        out[0, :, piece] = value

    tail(query_map, offset, got_state, wout_v, write_out)

    for peer in peers:
        map_copy(peer).wait_send()
        state_copy(peer).wait_send()

    @pl.when(section == 0)
    def _():
        for index in range(groups + 4):
            side_copy(index).wait_send()
        for peer in peers + [me]:
            first_copy(peer).wait_send()


def solution(mesh):
    seq_count = mesh.shape["seq"]

    def shards(tokens, norm_gain, w_qkv, w_rate, rate_base, init_state, w_out):
        rows, width = tokens.shape
        heads = rate_base.shape[1]
        inner_width = heads * HD
        groups = inner_width // GROUP
        hbm = pl.BlockSpec(memory_space=pltpu.HBM)

        def body(*refs):
            kernel(seq_count, *refs)

        return pl.pallas_call(
            body,
            name="layers",
            out_shape=jax.ShapeDtypeStruct((1, rows, width), BF16),
            in_specs=[hbm] * 7,
            out_specs=pl.BlockSpec(memory_space=pltpu.VMEM),
            scratch_shapes=[
                pltpu.VMEM((rows, width), BF16),
                pltpu.VMEM((1, width), F32),
                pltpu.VMEM((groups, width, 2 * GROUP), BF16),
                pltpu.VMEM((groups, width, GROUP), BF16),
                pltpu.VMEM((heads, width), BF16),
                pltpu.VMEM((1, heads), F32),
                pltpu.VMEM((groups, GROUP, width), BF16),
                pltpu.VMEM((HD, HD), F32),
                pltpu.VMEM((rows, width), BF16),
                pltpu.VMEM((rows, PAIR), F32),
                pltpu.VMEM((rows, inner_width), F32),
                pltpu.VMEM((heads // 2, rows, PAIR), BF16),
                pltpu.VMEM((heads // 2, rows, 2 * PAIR), BF16),
                pltpu.VMEM((heads // 2, PAIR, 2 * PAIR), BF16),
                pltpu.VMEM((heads, HD, PAIR), BF16),
                pltpu.VMEM((seq_count, HD, PAIR), BF16),
                pltpu.VMEM((seq_count, HD // 2, PAIR), BF16),
                pltpu.VMEM((heads, HD // 2, PAIR), BF16),
                pltpu.VMEM((heads // 2, rows, PAIR), BF16),
                pltpu.VMEM((heads // 2, rows, PAIR), F32),
                pltpu.VMEM((groups, GROUP, width), BF16),
                pltpu.VMEM((seq_count, HD // 2, PAIR), BF16),
                pltpu.VMEM((heads // 2, rows, PAIR), BF16),
                pltpu.VMEM((heads // 2, rows, PAIR), F32),
                pltpu.SemaphoreType.DMA((5,)),
                pltpu.SemaphoreType.DMA((4, groups)),
                pltpu.SemaphoreType.DMA((heads,)),
                pltpu.SemaphoreType.DMA((seq_count,)),
                pltpu.SemaphoreType.DMA((seq_count,)),
                pltpu.SemaphoreType.DMA((heads,)),
                pltpu.SemaphoreType.DMA((seq_count,)),
                pltpu.SemaphoreType.DMA((seq_count,)),
                pltpu.SemaphoreType.DMA((groups + 4,)),
                pltpu.SemaphoreType.DMA((groups + 4,)),
            ],
            compiler_params=pltpu.CompilerParams(
                collective_id=0, has_side_effects=True, vmem_limit_bytes=40 * 1024 * 1024),
        )(*(
            pltpu.with_memory_space_constraint(array, pltpu.HBM)
            for array in (
                tokens, norm_gain, w_qkv, jnp.swapaxes(w_rate, 1, 2), rate_base, init_state, w_out)
        ))

    return jax.shard_map(
        shards,
        mesh=mesh,
        in_specs=(
            P(("traj", "seq"), None),
            P("section", None),
            P("section", None, None),
            P("section", None, None),
            P("section", None),
            P("section", None, None, None),
            P("section", None, None),
        ),
        out_specs=P("section", ("traj", "seq"), None),
        check_vma=False,
    )
```

```python
import jax
import jax.numpy as jnp
from jax import lax
from jax.experimental import pallas as pl
from jax.experimental.pallas import tpu as pltpu
from jax.sharding import PartitionSpec as P

HD = 64
MB = 64
PAIR = 2 * HD
GROUP = 4 * HD
EPS = 1e-06
MESH = pl.DeviceIdType.MESH
F32 = jnp.float32
BF16 = jnp.bfloat16


def dot(a, b, dims=((1,), (0,))):
    return lax.dot_general(a, b, (dims, ((), ())), preferred_element_type=F32)


def split(x):
    high = x.astype(BF16)
    return high, (x - high.astype(F32)).astype(BF16)


def iota(shape, axis):
    return lax.broadcasted_iota(jnp.int32, shape, axis)


def head_ones():
    same = iota((GROUP, GROUP), 0) // HD == iota((GROUP, GROUP), 1) // HD
    return jnp.where(same, 1.0, 0.0).astype(BF16)


def unit_scale(x, row_scale, ones):
    return row_scale * lax.rsqrt(row_scale * row_scale * dot((x * x).astype(BF16), ones) + EPS)


def kernel(
    seq_count,
    tok, gain, w_qkv, w_rate, rate_base, init_state, w_out,
    out,
    hidden, gain_v, wkv_v, wq_v, wrate_v, rbase_v, wout_v, init_v,
    normed, scaled_rows, rate_all, keys, scaled, first_map, sent_map, got_map, sent_state, got_state,
    query_map, offset, wout_first, state_first, query_first, offset_first,
    load_sem, weight_sem,
    map_send, map_recv, state_send, state_recv, first_send, first_recv, side_send, side_recv,
):
    section = lax.axis_index("section")
    me = lax.axis_index("seq")
    rows, width = tok.shape
    heads = rate_base.shape[1]
    inner_width = heads * HD
    groups = inner_width // GROUP
    chunks = 4
    chunk = width // chunks
    side = 4
    row_of, column_of = me // side, lax.rem(me, side)
    order = [lax.rem(row_of + turn, groups) for turn in (2, 1, 3, 0)]

    token_copy = pltpu.make_async_copy(tok, hidden, load_sem.at[0])
    token_copy.start()
    small = [
        pltpu.make_async_copy(gain, gain_v, load_sem.at[1]),
        pltpu.make_async_copy(w_rate.at[0], wrate_v, load_sem.at[2]),
        pltpu.make_async_copy(rate_base, rbase_v, load_sem.at[3]),
        pltpu.make_async_copy(init_state.at[0, me], init_v, load_sem.at[4]),
    ]
    for copy in small:
        copy.start()

    def columns(start, p):
        return pl.ds(pl.multiple_of(start + order[p] * GROUP, GROUP), GROUP)

    def key_copy(p):
        return pltpu.make_async_copy(
            w_qkv.at[0, :, columns(inner_width, p)],
            wkv_v.at[p, :, pl.ds(0, GROUP)], weight_sem.at[0, p])

    def value_copy(p):
        return pltpu.make_async_copy(
            w_qkv.at[0, :, columns(2 * inner_width, p)],
            wkv_v.at[p, :, pl.ds(GROUP, GROUP)], weight_sem.at[1, p])

    def query_copy(p):
        return pltpu.make_async_copy(
            w_qkv.at[0, :, columns(0, p)], wq_v.at[p], weight_sem.at[2, p])

    def out_weight_copy(p):
        return pltpu.make_async_copy(
            w_out.at[0, columns(0, p), :], wout_v.at[p], weight_sem.at[3, p])

    half = groups // 2
    for g in range(half):
        key_copy(g).start()
        value_copy(g).start()

    barrier = pltpu.get_barrier_semaphore()
    steps = [(y, x) for y in range(seq_count // side) for x in range(side)][1:]
    steps.sort(key=lambda s: -min(s[0], seq_count // side - s[0]) - min(s[1], side - s[1]))
    peers = [
        lax.rem(row_of + y, seq_count // side) * side + lax.rem(column_of + x, side)
        for y, x in steps]
    for peer in peers:
        for other in range(2):
            pl.semaphore_signal(
                barrier, inc=1, device_id={"section": other, "seq": peer}, device_id_type=MESH)
    pl.semaphore_signal(barrier, inc=1, device_id={"section": 1 - section}, device_id_type=MESH)
    entered = 2 * seq_count - 1

    def spread_state(packed, parity):
        packed = packed.astype(F32)
        own = (iota(packed.shape, 1) // HD) == parity
        return [
            jnp.where(own, part, 0.0).astype(BF16)
            for part in (packed, pltpu.roll(packed, HD, 1))]

    def tail(maps, offsets, states, weights, write):
        parts = []
        for pair in range(heads // 2):
            h = 2 * (2 * order[pair // 2] + pair % 2)
            start = jnp.concatenate(spread_state(states[h], 0) + spread_state(states[h + 1], 1), axis=0)
            parts.append((dot(maps[pair], start) + offsets[pair]).astype(BF16))
        inner = jnp.concatenate(parts, axis=1)
        for n in range(chunks):
            piece = slice(n * chunk, (n + 1) * chunk)
            weight = jnp.concatenate([weights[p, :, piece] for p in range(groups)], axis=0)
            write(piece, (hidden[:, piece].astype(F32) + dot(inner, weight)).astype(BF16))

    early_pairs = heads // 2 - 2

    def side_copy(index):
        if index < groups:
            source, target = wout_v.at[index], wout_first.at[index]
        else:
            pairs = pl.ds(0, early_pairs) if index < groups + 2 else pl.ds(early_pairs, 2)
            source, target = [
                (query_map.at[pairs], query_first.at[pairs]),
                (offset.at[pairs], offset_first.at[pairs])][(index - groups) % 2]
        return pltpu.make_async_remote_copy(
            src_ref=source, dst_ref=target,
            send_sem=side_send.at[index], recv_sem=side_recv.at[index],
            device_id={"section": 1 - section}, device_id_type=MESH)

    def first_copy(peer):
        return pltpu.make_async_remote_copy(
            src_ref=sent_state.at[peer], dst_ref=state_first.at[me],
            send_sem=first_send.at[peer], recv_sem=first_recv.at[me],
            device_id={"section": 1 - section, "seq": peer}, device_id_type=MESH)

    def first_arrival(peer):
        return pltpu.make_async_remote_copy(
            src_ref=sent_state.at[peer], dst_ref=state_first.at[peer],
            send_sem=first_send.at[peer], recv_sem=first_recv.at[peer],
            device_id={"section": 1 - section, "seq": peer}, device_id_type=MESH)

    for copy in small:
        copy.wait()
    token_copy.wait()

    def norm():
        wide = hidden[...].astype(F32)
        row_scale = lax.rsqrt(jnp.mean(wide * wide, axis=-1, keepdims=True) + EPS)
        scaled_rows[...] = jnp.broadcast_to(row_scale, (rows, PAIR))
        normed[...] = (wide * gain_v[...]).astype(BF16)
        return row_scale

    def rate_parts(row_scale):
        return split(rbase_v[...] * jax.nn.sigmoid(
            row_scale * dot(normed[...], wrate_v[...], ((1,), (1,)))))

    def rate_spread(parts):
        head, lane = iota((heads, GROUP), 0), iota((heads, GROUP), 1)
        spread = jnp.concatenate([
            jnp.where(head == side * g + lane // HD, 1.0, 0.0) for g in order], axis=1).astype(BF16)
        rate_all[...] = dot(parts[0], spread) + dot(parts[1], spread)

    lane_low = iota((HD, PAIR), 1) < HD
    wide_shape = (PAIR, 4 * PAIR)
    diagonal = iota(wide_shape, 0) // HD == (iota(wide_shape, 1) % PAIR) // HD
    ones = head_ones()
    blank = jnp.zeros((MB, 2 * PAIR), BF16)

    def map_copy(peer):
        return pltpu.make_async_remote_copy(
            src_ref=sent_map.at[peer], dst_ref=got_map.at[me],
            send_sem=map_send.at[peer], recv_sem=map_recv.at[me],
            device_id={"seq": peer}, device_id_type=MESH)

    def row_factor():
        return jnp.concatenate([scaled_rows[...]] * (GROUP // PAIR), axis=1)

    def key_dot(g):
        return dot(normed[...], wkv_v[g])

    def key_scale(g, both):
        key, value = both[:, :GROUP], both[:, GROUP:]
        row_wide = row_factor()
        scale = unit_scale(key, row_wide, ones)
        rate = rate_all[:, g * GROUP:(g + 1) * GROUP] * scale
        key_bf = key.astype(BF16)
        rated_value = (rate * (row_wide * value)).astype(BF16)
        rated_key = (rate * scale * key).astype(BF16)
        made = []
        for i in range(2):
            lanes = slice(i * PAIR, (i + 1) * PAIR)
            pair_key = key_bf[:, lanes]
            pair_scaled = jnp.concatenate([rated_value[:, lanes], rated_key[:, lanes]], axis=1)
            keys[2 * g + i] = pair_key
            scaled[2 * g + i] = pair_scaled
            made.append((pair_key, pair_scaled))
        return made

    def key_maps(g, made):
        found = []
        for i, (pair_key, pair_scaled) in enumerate(made):
            by_block = jnp.concatenate([
                jnp.concatenate([pair_scaled[:MB], blank], axis=1),
                jnp.concatenate([blank, pair_scaled[MB:]], axis=1)], axis=0)
            maps = jnp.where(diagonal, dot(pair_key, by_block, ((0,), (0,))), 0.0)
            first_bf = maps[:, :2 * PAIR].astype(BF16)
            first_map[2 * g + i] = first_bf
            found.append((maps, first_bf))
        return found

    def key_pack(g, found):
        for i, (maps, first_bf) in enumerate(found):
            first, second = maps[:, :2 * PAIR], maps[:, 2 * PAIR:]
            total = first + second - dot(second[:, PAIR:].astype(BF16), first_bf)
            packed = total[:HD] + total[HD:]
            pack_b, pack_d = packed[:, :PAIR], pltpu.roll(packed[:, PAIR:], HD, 1)
            h = side * order[g] + 2 * i
            sent_map[h] = jnp.where(lane_low, pack_b, pack_d).astype(BF16)
            sent_map[h + 1] = jnp.where(lane_low, pack_d, pack_b).astype(BF16)
        own = g == groups - 1
        for turn in (2, 1, 3) if own else (2, 1, 3, 0):
            map_copy(side * order[g] + lax.rem(column_of + turn, side)).start()

    def key_groups(which, before=lambda position: None, gap=0):
        wait = [lambda g, value: value] * gap
        pipeline([lambda g, unused: key_dot(g)] + wait + [key_scale, key_maps, key_pack], which, before)

    def pipeline(stages, which, before=lambda position: None):
        held = {}
        for step in range(len(which) + len(stages) - 1):
            if step < len(which):
                before(step)
            for depth, stage in enumerate(stages):
                position = step - depth
                if 0 <= position < len(which):
                    held[position] = stage(which[position], held.get(position))

    @pl.when(section == 0)
    def _():
        for g in range(half, groups - 1):
            key_copy(g).start()
            value_copy(g).start()
        rate_spread(rate_parts(norm()))
        pl.semaphore_wait(barrier, entered)
        for g in range(half):
            key_copy(g).wait()
            value_copy(g).wait()
            if g == 0:
                key_copy(groups - 1).start()
                value_copy(groups - 1).start()
        key_groups(range(half))
        for g in range(groups):
            query_copy(g).start()
        def arrive(position):
            key_copy(half + position).wait()
            value_copy(half + position).wait()
            if position == groups - half - 1:
                for n in range(groups):
                    out_weight_copy(n).start()

        key_groups(range(half, groups), arrive)

    @pl.when(section == 1)
    def _():
        for g in range(half, groups):
            key_copy(g).start()
            value_copy(g).start()
        for g in range(groups):
            query_copy(g).start()
        for n in range(groups):
            out_weight_copy(n).start()
        for g in range(groups):
            key_copy(g).wait()
            value_copy(g).wait()
        for g in range(groups):
            query_copy(g).wait()
        for n in range(groups):
            out_weight_copy(n).wait()
        pl.semaphore_wait(barrier, entered)
        for index in range(groups + 4):
            side_copy(index).wait_recv()
        for peer in peers + [me]:
            first_arrival(peer).wait_recv()

        def write(piece, value):
            hidden[:, piece] = value

        tail(query_first, offset_first, state_first, wout_first, write)
        row_scale = norm()
        parts = []

        def rates(position):
            if position == 1:
                parts.append(rate_parts(row_scale))
            if position == 2:
                rate_spread(parts[0])

        key_groups(range(groups), rates, gap=1)

    got_map[me] = sent_map[me]

    row = iota((4 * MB, PAIR), 0)
    column = iota((4 * MB, PAIR), 1)
    causal = (column // MB == row // PAIR) & (column % MB <= row % MB)
    low_half = iota((MB, 2 * PAIR), 1) % PAIR < HD

    def query_scores(g, query_all):
        scale_all = unit_scale(query_all, row_factor(), ones)
        made = []
        for i in range(2):
            query = query_all[:, i * PAIR:(i + 1) * PAIR]
            parts = []
            for b in range(2):
                piece = query[b * MB:(b + 1) * MB]
                parts += [jnp.where(lane_low, piece, 0.0), jnp.where(lane_low, 0.0, piece)]
            stacked = jnp.concatenate(parts, axis=0).astype(BF16)
            scores = jnp.where(causal, dot(stacked, keys[2 * g + i], ((1,), (1,))), 0.0)
            made.append((query, scale_all[:, i * PAIR:(i + 1) * PAIR], scores.astype(BF16)))
        return made

    def query_mix(g, made):
        found = []
        for i, (query, scale, scores) in enumerate(made):
            pair = 2 * g + i
            mixed = dot(scores, scaled[pair])
            mix_one = jnp.where(low_half, mixed[:MB], mixed[MB:2 * MB])
            mix_two = jnp.where(low_half, mixed[2 * MB:3 * MB], mixed[3 * MB:])
            map_one = query[:MB] - mix_one[:, PAIR:]
            map_two = query[MB:] - mix_two[:, PAIR:]
            query_map[pair, pl.ds(0, MB), :] = (scale[:MB] * map_one).astype(BF16)
            offset[pair, pl.ds(0, MB), :] = scale[:MB] * mix_one[:, :PAIR]
            found.append((map_two, mix_two[:, :PAIR], scale[MB:]))
        return found

    def query_through(g, found):
        for i, (map_two, mix_two, scale) in enumerate(found):
            pair = 2 * g + i
            through = dot(map_two.astype(BF16), first_map[pair])
            query_map[pair, pl.ds(MB, MB), :] = (
                scale * (map_two - through[:, PAIR:])).astype(BF16)
            offset[pair, pl.ds(MB, MB), :] = scale * (mix_two + through[:, :PAIR])

    def query_groups(which):
        pipeline(
            [lambda g, unused: dot(normed[...], wq_v[g]), query_scores, query_mix, query_through],
            which)

    @pl.when(section == 0)
    def _():
        for g in range(groups):
            query_copy(g).wait()

    query_groups(range(groups - 1))

    @pl.when(section == 0)
    def _():
        for n in range(groups):
            out_weight_copy(n).wait()
        for index in range(groups + 2):
            side_copy(index).start()

    odd = lax.rem(me, 2)
    offset_half = (iota((HD, PAIR), 1) // HD) == odd

    def state_copy(peer):
        return pltpu.make_async_remote_copy(
            src_ref=sent_state.at[peer], dst_ref=got_state.at[me],
            send_sem=state_send.at[peer], recv_sem=state_recv.at[me],
            device_id={"seq": peer}, device_id_type=MESH)

    def map_arrival(peer):
        return pltpu.make_async_remote_copy(
            src_ref=sent_map.at[peer], dst_ref=got_map.at[peer],
            send_sem=map_send.at[peer], recv_sem=map_recv.at[peer],
            device_id={"seq": peer}, device_id_type=MESH)

    def state_arrival(peer):
        return pltpu.make_async_remote_copy(
            src_ref=sent_state.at[peer], dst_ref=got_state.at[peer],
            send_sem=state_send.at[peer], recv_sem=state_recv.at[peer],
            device_id={"seq": peer}, device_id_type=MESH)

    for peer in peers:
        map_arrival(peer).wait_recv()

    def after(later, earlier):
        contracted = jnp.where(offset_half, 0.0, later).astype(BF16)
        operand = earlier.astype(BF16)
        return earlier + later - dot(contracted, jnp.concatenate([operand, operand], axis=0))

    step = [got_map[s].astype(F32) for s in range(seq_count)]
    state = [None] * seq_count
    state[0] = jnp.where(offset_half, jnp.concatenate([init_v[...], init_v[...]], axis=1), 0.0)
    runs = range(seq_count // 4)
    one = [step[4 * g] for g in runs]
    two = [after(step[4 * g + 1], step[4 * g]) for g in runs]
    last_two = [after(step[4 * g + 3], step[4 * g + 2]) for g in runs[:-1]]
    four = [after(last_two[g], two[g]) for g in runs[:-1]]
    three = [after(step[4 * g + 2], two[g]) for g in runs]
    state[4] = after(four[0], state[0])
    eight = after(four[1], four[0])
    next_eight = after(four[2], four[1])
    prefixes = (one, two, three)

    def fill(g):
        for i in range(3):
            state[4 * g + i + 1] = after(prefixes[i][g], state[4 * g])

    fill(0)
    state[8] = after(eight, state[0])
    state[12] = after(next_eight, state[4])
    for g in runs[1:]:
        fill(g)
    own_half = (iota((HD // 2, PAIR), 1) // HD) == odd
    for s in range(seq_count):
        sent_state[s] = jnp.where(
            own_half, state[s][:HD // 2],
            pltpu.roll(state[s][HD // 2:], HD, 1)).astype(BF16)

    @pl.when(section == 0)
    def _():
        for peer in peers + [me]:
            first_copy(peer).start()

    @pl.when(section == 1)
    def _():
        for peer in peers:
            state_copy(peer).start()

    got_state[me] = sent_state[me]

    query_groups(range(groups - 1, groups))

    @pl.when(section == 0)
    def _():
        for index in range(groups + 2, groups + 4):
            side_copy(index).start()
        for peer in peers:
            state_copy(peer).start()

    for peer in peers:
        map_copy(peer).wait_send()
        state_copy(peer).wait_send()
    for peer in peers:
        state_arrival(peer).wait_recv()

    def write_out(piece, value):
        out[0, :, piece] = value

    tail(query_map, offset, got_state, wout_v, write_out)

    @pl.when(section == 0)
    def _():
        for index in range(groups + 4):
            side_copy(index).wait_send()
        for peer in peers + [me]:
            first_copy(peer).wait_send()


def solution(mesh):
    seq_count = mesh.shape["seq"]

    def shards(tokens, norm_gain, w_qkv, w_rate, rate_base, init_state, w_out):
        rows, width = tokens.shape
        heads = rate_base.shape[1]
        inner_width = heads * HD
        groups = inner_width // GROUP
        hbm = pl.BlockSpec(memory_space=pltpu.HBM)

        def body(*refs):
            kernel(seq_count, *refs)

        return pl.pallas_call(
            body,
            name="layers",
            out_shape=jax.ShapeDtypeStruct((1, rows, width), BF16),
            in_specs=[hbm] * 7,
            out_specs=pl.BlockSpec(memory_space=pltpu.VMEM),
            scratch_shapes=[
                pltpu.VMEM((rows, width), BF16),
                pltpu.VMEM((1, width), F32),
                pltpu.VMEM((groups, width, 2 * GROUP), BF16),
                pltpu.VMEM((groups, width, GROUP), BF16),
                pltpu.VMEM((heads, width), BF16),
                pltpu.VMEM((1, heads), F32),
                pltpu.VMEM((groups, GROUP, width), BF16),
                pltpu.VMEM((HD, HD), F32),
                pltpu.VMEM((rows, width), BF16),
                pltpu.VMEM((rows, PAIR), F32),
                pltpu.VMEM((rows, inner_width), F32),
                pltpu.VMEM((heads // 2, rows, PAIR), BF16),
                pltpu.VMEM((heads // 2, rows, 2 * PAIR), BF16),
                pltpu.VMEM((heads // 2, PAIR, 2 * PAIR), BF16),
                pltpu.VMEM((heads, HD, PAIR), BF16),
                pltpu.VMEM((seq_count, HD, PAIR), BF16),
                pltpu.VMEM((seq_count, HD // 2, PAIR), BF16),
                pltpu.VMEM((heads, HD // 2, PAIR), BF16),
                pltpu.VMEM((heads // 2, rows, PAIR), BF16),
                pltpu.VMEM((heads // 2, rows, PAIR), F32),
                pltpu.VMEM((groups, GROUP, width), BF16),
                pltpu.VMEM((seq_count, HD // 2, PAIR), BF16),
                pltpu.VMEM((heads // 2, rows, PAIR), BF16),
                pltpu.VMEM((heads // 2, rows, PAIR), F32),
                pltpu.SemaphoreType.DMA((5,)),
                pltpu.SemaphoreType.DMA((4, groups)),
                pltpu.SemaphoreType.DMA((heads,)),
                pltpu.SemaphoreType.DMA((seq_count,)),
                pltpu.SemaphoreType.DMA((seq_count,)),
                pltpu.SemaphoreType.DMA((heads,)),
                pltpu.SemaphoreType.DMA((seq_count,)),
                pltpu.SemaphoreType.DMA((seq_count,)),
                pltpu.SemaphoreType.DMA((groups + 4,)),
                pltpu.SemaphoreType.DMA((groups + 4,)),
            ],
            compiler_params=pltpu.CompilerParams(
                collective_id=0, has_side_effects=True, vmem_limit_bytes=40 * 1024 * 1024),
        )(*(
            pltpu.with_memory_space_constraint(array, pltpu.HBM)
            for array in (
                tokens, norm_gain, w_qkv, jnp.swapaxes(w_rate, 1, 2), rate_base, init_state, w_out)
        ))

    return jax.shard_map(
        shards,
        mesh=mesh,
        in_specs=(
            P(("traj", "seq"), None),
            P("section", None),
            P("section", None, None),
            P("section", None, None),
            P("section", None),
            P("section", None, None, None),
            P("section", None, None),
        ),
        out_specs=P("section", ("traj", "seq"), None),
        check_vma=False,
    )
```

```python
import jax
import jax.numpy as jnp
from jax import lax
from jax.experimental import pallas as pl
from jax.experimental.pallas import tpu as pltpu
from jax.sharding import PartitionSpec as P

HD = 64
MB = 64
PAIR = 2 * HD
GROUP = 4 * HD
EPS = 1e-06
MESH = pl.DeviceIdType.MESH
F32 = jnp.float32
BF16 = jnp.bfloat16


def dot(a, b, dims=((1,), (0,))):
    return lax.dot_general(a, b, (dims, ((), ())), preferred_element_type=F32)


def split(x):
    high = x.astype(BF16)
    return high, (x - high.astype(F32)).astype(BF16)


def iota(shape, axis):
    return lax.broadcasted_iota(jnp.int32, shape, axis)


def head_ones():
    same = iota((GROUP, GROUP), 0) // HD == iota((GROUP, GROUP), 1) // HD
    return jnp.where(same, 1.0, 0.0).astype(BF16)


def unit_scale(x, row_scale, ones):
    return row_scale * lax.rsqrt(row_scale * row_scale * dot((x * x).astype(BF16), ones) + EPS)


def kernel(
    seq_count,
    tok, gain, w_qkv, w_rate, rate_base, init_state, w_out,
    out,
    hidden, gain_v, wkv_v, wq_v, wrate_v, rbase_v, wout_v, init_v,
    normed, scaled_rows, rate_all, keys, scaled, first_map, sent_map, got_map, sent_state, got_state,
    query_map, offset, wout_first, state_first, query_first, offset_first,
    load_sem, weight_sem,
    map_send, map_recv, state_send, state_recv, first_send, first_recv, side_send, side_recv,
):
    section = lax.axis_index("section")
    me = lax.axis_index("seq")
    rows, width = tok.shape
    heads = rate_base.shape[1]
    inner_width = heads * HD
    groups = inner_width // GROUP
    chunks = 4
    chunk = width // chunks
    side = 4
    row_of, column_of = me // side, lax.rem(me, side)
    order = [lax.rem(row_of + turn, groups) for turn in (2, 1, 3, 0)]

    token_copy = pltpu.make_async_copy(tok, hidden, load_sem.at[0])
    token_copy.start()
    small = [
        pltpu.make_async_copy(gain, gain_v, load_sem.at[1]),
        pltpu.make_async_copy(w_rate.at[0], wrate_v, load_sem.at[2]),
        pltpu.make_async_copy(rate_base, rbase_v, load_sem.at[3]),
        pltpu.make_async_copy(init_state.at[0, me], init_v, load_sem.at[4]),
    ]
    for copy in small:
        copy.start()

    def columns(start, p):
        return pl.ds(pl.multiple_of(start + order[p] * GROUP, GROUP), GROUP)

    def key_copy(p):
        return pltpu.make_async_copy(
            w_qkv.at[0, :, columns(inner_width, p)],
            wkv_v.at[p, :, pl.ds(0, GROUP)], weight_sem.at[0, p])

    def value_copy(p):
        return pltpu.make_async_copy(
            w_qkv.at[0, :, columns(2 * inner_width, p)],
            wkv_v.at[p, :, pl.ds(GROUP, GROUP)], weight_sem.at[1, p])

    def query_copy(p):
        return pltpu.make_async_copy(
            w_qkv.at[0, :, columns(0, p)], wq_v.at[p], weight_sem.at[2, p])

    def out_weight_copy(p):
        return pltpu.make_async_copy(
            w_out.at[0, columns(0, p), :], wout_v.at[p], weight_sem.at[3, p])

    half = groups // 2
    for g in range(half):
        key_copy(g).start()
        value_copy(g).start()

    barrier = pltpu.get_barrier_semaphore()
    steps = [(y, x) for y in range(seq_count // side) for x in range(side)][1:]
    steps.sort(key=lambda s: -min(s[0], seq_count // side - s[0]) - min(s[1], side - s[1]))
    peers = [
        lax.rem(row_of + y, seq_count // side) * side + lax.rem(column_of + x, side)
        for y, x in steps]
    for peer in peers:
        for other in range(2):
            pl.semaphore_signal(
                barrier, inc=1, device_id={"section": other, "seq": peer}, device_id_type=MESH)
    pl.semaphore_signal(barrier, inc=1, device_id={"section": 1 - section}, device_id_type=MESH)
    entered = 2 * seq_count - 1

    def spread_state(packed, parity):
        packed = packed.astype(F32)
        own = (iota(packed.shape, 1) // HD) == parity
        return [
            jnp.where(own, part, 0.0).astype(BF16)
            for part in (packed, pltpu.roll(packed, HD, 1))]

    def tail(maps, offsets, states, weights, write):
        parts = []
        for pair in range(heads // 2):
            h = 2 * (2 * order[pair // 2] + pair % 2)
            start = jnp.concatenate(spread_state(states[h], 0) + spread_state(states[h + 1], 1), axis=0)
            parts.append((dot(maps[pair], start) + offsets[pair]).astype(BF16))
        inner = jnp.concatenate(parts, axis=1)
        for n in range(chunks):
            piece = slice(n * chunk, (n + 1) * chunk)
            weight = jnp.concatenate([weights[p, :, piece] for p in range(groups)], axis=0)
            write(piece, (hidden[:, piece].astype(F32) + dot(inner, weight)).astype(BF16))

    early_pairs = heads // 2 - 2

    def side_copy(index):
        if index < groups:
            source, target = w_out.at[0, columns(0, index), :], wout_first.at[index]
        else:
            pairs = pl.ds(0, early_pairs) if index < groups + 2 else pl.ds(early_pairs, 2)
            source, target = [
                (query_map.at[pairs], query_first.at[pairs]),
                (offset.at[pairs], offset_first.at[pairs])][(index - groups) % 2]
        return pltpu.make_async_remote_copy(
            src_ref=source, dst_ref=target,
            send_sem=side_send.at[index], recv_sem=side_recv.at[index],
            device_id={"section": 1 - section}, device_id_type=MESH)

    def first_copy(peer):
        return pltpu.make_async_remote_copy(
            src_ref=sent_state.at[peer], dst_ref=state_first.at[me],
            send_sem=first_send.at[peer], recv_sem=first_recv.at[me],
            device_id={"section": 1 - section, "seq": peer}, device_id_type=MESH)

    def first_arrival(peer):
        return pltpu.make_async_remote_copy(
            src_ref=sent_state.at[peer], dst_ref=state_first.at[peer],
            send_sem=first_send.at[peer], recv_sem=first_recv.at[peer],
            device_id={"section": 1 - section, "seq": peer}, device_id_type=MESH)

    for copy in small:
        copy.wait()
    token_copy.wait()

    def norm():
        wide = hidden[...].astype(F32)
        row_scale = lax.rsqrt(jnp.mean(wide * wide, axis=-1, keepdims=True) + EPS)
        scaled_rows[...] = jnp.broadcast_to(row_scale, (rows, PAIR))
        normed[...] = (wide * gain_v[...]).astype(BF16)
        return row_scale

    def rate_parts(row_scale):
        return split(rbase_v[...] * jax.nn.sigmoid(
            row_scale * dot(normed[...], wrate_v[...], ((1,), (1,)))))

    def rate_spread(parts):
        head, lane = iota((heads, GROUP), 0), iota((heads, GROUP), 1)
        spread = jnp.concatenate([
            jnp.where(head == side * g + lane // HD, 1.0, 0.0) for g in order], axis=1).astype(BF16)
        rate_all[...] = dot(parts[0], spread) + dot(parts[1], spread)

    lane_low = iota((HD, PAIR), 1) < HD
    wide_shape = (PAIR, 4 * PAIR)
    diagonal = iota(wide_shape, 0) // HD == (iota(wide_shape, 1) % PAIR) // HD
    ones = head_ones()
    blank = jnp.zeros((MB, 2 * PAIR), BF16)

    def map_copy(peer):
        return pltpu.make_async_remote_copy(
            src_ref=sent_map.at[peer], dst_ref=got_map.at[me],
            send_sem=map_send.at[peer], recv_sem=map_recv.at[me],
            device_id={"seq": peer}, device_id_type=MESH)

    def row_factor():
        return jnp.concatenate([scaled_rows[...]] * (GROUP // PAIR), axis=1)

    def key_dot(g):
        return dot(normed[...], wkv_v[g])

    def key_scale(g, both):
        key, value = both[:, :GROUP], both[:, GROUP:]
        row_wide = row_factor()
        scale = unit_scale(key, row_wide, ones)
        rate = rate_all[:, g * GROUP:(g + 1) * GROUP] * scale
        key_bf = key.astype(BF16)
        rated_value = (rate * (row_wide * value)).astype(BF16)
        rated_key = (rate * scale * key).astype(BF16)
        made = []
        for i in range(2):
            lanes = slice(i * PAIR, (i + 1) * PAIR)
            pair_key = key_bf[:, lanes]
            pair_scaled = jnp.concatenate([rated_value[:, lanes], rated_key[:, lanes]], axis=1)
            keys[2 * g + i] = pair_key
            scaled[2 * g + i] = pair_scaled
            made.append((pair_key, pair_scaled))
        return made

    def key_maps(g, made):
        found = []
        for i, (pair_key, pair_scaled) in enumerate(made):
            by_block = jnp.concatenate([
                jnp.concatenate([pair_scaled[:MB], blank], axis=1),
                jnp.concatenate([blank, pair_scaled[MB:]], axis=1)], axis=0)
            maps = jnp.where(diagonal, dot(pair_key, by_block, ((0,), (0,))), 0.0)
            first_bf = maps[:, :2 * PAIR].astype(BF16)
            first_map[2 * g + i] = first_bf
            found.append((maps, first_bf))
        return found

    def key_pack(g, found):
        for i, (maps, first_bf) in enumerate(found):
            first, second = maps[:, :2 * PAIR], maps[:, 2 * PAIR:]
            total = first + second - dot(second[:, PAIR:].astype(BF16), first_bf)
            packed = total[:HD] + total[HD:]
            pack_b, pack_d = packed[:, :PAIR], pltpu.roll(packed[:, PAIR:], HD, 1)
            h = side * order[g] + 2 * i
            sent_map[h] = jnp.where(lane_low, pack_b, pack_d).astype(BF16)
            sent_map[h + 1] = jnp.where(lane_low, pack_d, pack_b).astype(BF16)
        own = g == groups - 1
        for turn in (2, 1, 3) if own else (2, 1, 3, 0):
            map_copy(side * order[g] + lax.rem(column_of + turn, side)).start()

    def key_groups(which, before=lambda position: None, gap=0):
        wait = [lambda g, value: value] * gap
        pipeline([lambda g, unused: key_dot(g)] + wait + [key_scale, key_maps, key_pack], which, before)

    def pipeline(stages, which, before=lambda position: None):
        held = {}
        for step in range(len(which) + len(stages) - 1):
            if step < len(which):
                before(step)
            for depth, stage in enumerate(stages):
                position = step - depth
                if 0 <= position < len(which):
                    held[position] = stage(which[position], held.get(position))

    @pl.when(section == 0)
    def _():
        for g in range(half, groups - 1):
            key_copy(g).start()
            value_copy(g).start()
        rate_spread(rate_parts(norm()))
        pl.semaphore_wait(barrier, entered)
        for g in range(half):
            key_copy(g).wait()
            value_copy(g).wait()
            if g == 0:
                key_copy(groups - 1).start()
                value_copy(groups - 1).start()
        key_groups(range(half))
        for g in range(groups):
            query_copy(g).start()
        def arrive(position):
            key_copy(half + position).wait()
            value_copy(half + position).wait()
            if position == groups - half - 1:
                for n in range(groups):
                    out_weight_copy(n).start()

        key_groups(range(half, groups), arrive)

    @pl.when(section == 1)
    def _():
        for g in range(half, groups):
            key_copy(g).start()
            value_copy(g).start()
        for g in range(groups):
            query_copy(g).start()
        for n in range(groups):
            out_weight_copy(n).start()
        for g in range(groups):
            key_copy(g).wait()
            value_copy(g).wait()
        for g in range(groups):
            query_copy(g).wait()
        for n in range(groups):
            out_weight_copy(n).wait()
        pl.semaphore_wait(barrier, entered)
        for index in range(groups + 4):
            side_copy(index).wait_recv()
        for peer in peers + [me]:
            first_arrival(peer).wait_recv()

        def write(piece, value):
            hidden[:, piece] = value

        tail(query_first, offset_first, state_first, wout_first, write)
        row_scale = norm()
        parts = []

        def rates(position):
            if position == 1:
                parts.append(rate_parts(row_scale))
            if position == 2:
                rate_spread(parts[0])

        key_groups(range(groups), rates, gap=1)

    got_map[me] = sent_map[me]

    row = iota((4 * MB, PAIR), 0)
    column = iota((4 * MB, PAIR), 1)
    causal = (column // MB == row // PAIR) & (column % MB <= row % MB)
    low_half = iota((MB, 2 * PAIR), 1) % PAIR < HD

    def query_scores(g, query_all):
        scale_all = unit_scale(query_all, row_factor(), ones)
        made = []
        for i in range(2):
            query = query_all[:, i * PAIR:(i + 1) * PAIR]
            parts = []
            for b in range(2):
                piece = query[b * MB:(b + 1) * MB]
                parts += [jnp.where(lane_low, piece, 0.0), jnp.where(lane_low, 0.0, piece)]
            stacked = jnp.concatenate(parts, axis=0).astype(BF16)
            scores = jnp.where(causal, dot(stacked, keys[2 * g + i], ((1,), (1,))), 0.0)
            made.append((query, scale_all[:, i * PAIR:(i + 1) * PAIR], scores.astype(BF16)))
        return made

    def query_mix(g, made):
        found = []
        for i, (query, scale, scores) in enumerate(made):
            pair = 2 * g + i
            mixed = dot(scores, scaled[pair])
            mix_one = jnp.where(low_half, mixed[:MB], mixed[MB:2 * MB])
            mix_two = jnp.where(low_half, mixed[2 * MB:3 * MB], mixed[3 * MB:])
            map_one = query[:MB] - mix_one[:, PAIR:]
            map_two = query[MB:] - mix_two[:, PAIR:]
            query_map[pair, pl.ds(0, MB), :] = (scale[:MB] * map_one).astype(BF16)
            offset[pair, pl.ds(0, MB), :] = scale[:MB] * mix_one[:, :PAIR]
            found.append((map_two, mix_two[:, :PAIR], scale[MB:]))
        return found

    def query_through(g, found):
        for i, (map_two, mix_two, scale) in enumerate(found):
            pair = 2 * g + i
            through = dot(map_two.astype(BF16), first_map[pair])
            query_map[pair, pl.ds(MB, MB), :] = (
                scale * (map_two - through[:, PAIR:])).astype(BF16)
            offset[pair, pl.ds(MB, MB), :] = scale * (mix_two + through[:, :PAIR])

    def query_groups(which):
        pipeline(
            [lambda g, unused: dot(normed[...], wq_v[g]), query_scores, query_mix, query_through],
            which)

    @pl.when(section == 0)
    def _():
        for index in range(groups):
            side_copy(index).start()
        for g in range(groups):
            query_copy(g).wait()

    query_groups(range(groups - 1))

    @pl.when(section == 0)
    def _():
        for n in range(groups):
            out_weight_copy(n).wait()
        for index in range(groups, groups + 2):
            side_copy(index).start()

    odd = lax.rem(me, 2)
    offset_half = (iota((HD, PAIR), 1) // HD) == odd

    def state_copy(peer):
        return pltpu.make_async_remote_copy(
            src_ref=sent_state.at[peer], dst_ref=got_state.at[me],
            send_sem=state_send.at[peer], recv_sem=state_recv.at[me],
            device_id={"seq": peer}, device_id_type=MESH)

    def map_arrival(peer):
        return pltpu.make_async_remote_copy(
            src_ref=sent_map.at[peer], dst_ref=got_map.at[peer],
            send_sem=map_send.at[peer], recv_sem=map_recv.at[peer],
            device_id={"seq": peer}, device_id_type=MESH)

    def state_arrival(peer):
        return pltpu.make_async_remote_copy(
            src_ref=sent_state.at[peer], dst_ref=got_state.at[peer],
            send_sem=state_send.at[peer], recv_sem=state_recv.at[peer],
            device_id={"seq": peer}, device_id_type=MESH)

    for peer in peers:
        map_arrival(peer).wait_recv()

    def after(later, earlier):
        contracted = jnp.where(offset_half, 0.0, later).astype(BF16)
        operand = earlier.astype(BF16)
        return earlier + later - dot(contracted, jnp.concatenate([operand, operand], axis=0))

    step = [got_map[s].astype(F32) for s in range(seq_count)]
    state = [None] * seq_count
    state[0] = jnp.where(offset_half, jnp.concatenate([init_v[...], init_v[...]], axis=1), 0.0)
    runs = range(seq_count // 4)
    one = [step[4 * g] for g in runs]
    two = [after(step[4 * g + 1], step[4 * g]) for g in runs]
    last_two = [after(step[4 * g + 3], step[4 * g + 2]) for g in runs[:-1]]
    four = [after(last_two[g], two[g]) for g in runs[:-1]]
    three = [after(step[4 * g + 2], two[g]) for g in runs]
    state[4] = after(four[0], state[0])
    eight = after(four[1], four[0])
    next_eight = after(four[2], four[1])
    prefixes = (one, two, three)

    def fill(g):
        for i in range(3):
            state[4 * g + i + 1] = after(prefixes[i][g], state[4 * g])

    fill(0)
    state[8] = after(eight, state[0])
    state[12] = after(next_eight, state[4])
    for g in runs[1:]:
        fill(g)
    own_half = (iota((HD // 2, PAIR), 1) // HD) == odd
    for s in range(seq_count):
        sent_state[s] = jnp.where(
            own_half, state[s][:HD // 2],
            pltpu.roll(state[s][HD // 2:], HD, 1)).astype(BF16)

    @pl.when(section == 0)
    def _():
        for peer in peers + [me]:
            first_copy(peer).start()

    @pl.when(section == 1)
    def _():
        for peer in peers:
            state_copy(peer).start()

    got_state[me] = sent_state[me]

    query_groups(range(groups - 1, groups))

    @pl.when(section == 0)
    def _():
        for index in range(groups + 2, groups + 4):
            side_copy(index).start()
        for peer in peers:
            state_copy(peer).start()

    for peer in peers:
        map_copy(peer).wait_send()
        state_copy(peer).wait_send()
    for peer in peers:
        state_arrival(peer).wait_recv()

    def write_out(piece, value):
        out[0, :, piece] = value

    tail(query_map, offset, got_state, wout_v, write_out)

    @pl.when(section == 0)
    def _():
        for index in range(groups + 4):
            side_copy(index).wait_send()
        for peer in peers + [me]:
            first_copy(peer).wait_send()


def solution(mesh):
    seq_count = mesh.shape["seq"]

    def shards(tokens, norm_gain, w_qkv, w_rate, rate_base, init_state, w_out):
        rows, width = tokens.shape
        heads = rate_base.shape[1]
        inner_width = heads * HD
        groups = inner_width // GROUP
        hbm = pl.BlockSpec(memory_space=pltpu.HBM)

        def body(*refs):
            kernel(seq_count, *refs)

        return pl.pallas_call(
            body,
            name="layers",
            out_shape=jax.ShapeDtypeStruct((1, rows, width), BF16),
            in_specs=[hbm] * 7,
            out_specs=pl.BlockSpec(memory_space=pltpu.VMEM),
            scratch_shapes=[
                pltpu.VMEM((rows, width), BF16),
                pltpu.VMEM((1, width), F32),
                pltpu.VMEM((groups, width, 2 * GROUP), BF16),
                pltpu.VMEM((groups, width, GROUP), BF16),
                pltpu.VMEM((heads, width), BF16),
                pltpu.VMEM((1, heads), F32),
                pltpu.VMEM((groups, GROUP, width), BF16),
                pltpu.VMEM((HD, HD), F32),
                pltpu.VMEM((rows, width), BF16),
                pltpu.VMEM((rows, PAIR), F32),
                pltpu.VMEM((rows, inner_width), F32),
                pltpu.VMEM((heads // 2, rows, PAIR), BF16),
                pltpu.VMEM((heads // 2, rows, 2 * PAIR), BF16),
                pltpu.VMEM((heads // 2, PAIR, 2 * PAIR), BF16),
                pltpu.VMEM((heads, HD, PAIR), BF16),
                pltpu.VMEM((seq_count, HD, PAIR), BF16),
                pltpu.VMEM((seq_count, HD // 2, PAIR), BF16),
                pltpu.VMEM((heads, HD // 2, PAIR), BF16),
                pltpu.VMEM((heads // 2, rows, PAIR), BF16),
                pltpu.VMEM((heads // 2, rows, PAIR), F32),
                pltpu.VMEM((groups, GROUP, width), BF16),
                pltpu.VMEM((seq_count, HD // 2, PAIR), BF16),
                pltpu.VMEM((heads // 2, rows, PAIR), BF16),
                pltpu.VMEM((heads // 2, rows, PAIR), F32),
                pltpu.SemaphoreType.DMA((5,)),
                pltpu.SemaphoreType.DMA((4, groups)),
                pltpu.SemaphoreType.DMA((heads,)),
                pltpu.SemaphoreType.DMA((seq_count,)),
                pltpu.SemaphoreType.DMA((seq_count,)),
                pltpu.SemaphoreType.DMA((heads,)),
                pltpu.SemaphoreType.DMA((seq_count,)),
                pltpu.SemaphoreType.DMA((seq_count,)),
                pltpu.SemaphoreType.DMA((groups + 4,)),
                pltpu.SemaphoreType.DMA((groups + 4,)),
            ],
            compiler_params=pltpu.CompilerParams(
                collective_id=0, has_side_effects=True, vmem_limit_bytes=40 * 1024 * 1024),
        )(*(
            pltpu.with_memory_space_constraint(array, pltpu.HBM)
            for array in (
                tokens, norm_gain, w_qkv, jnp.swapaxes(w_rate, 1, 2), rate_base, init_state, w_out)
        ))

    return jax.shard_map(
        shards,
        mesh=mesh,
        in_specs=(
            P(("traj", "seq"), None),
            P("section", None),
            P("section", None, None),
            P("section", None, None),
            P("section", None),
            P("section", None, None, None),
            P("section", None, None),
        ),
        out_specs=P("section", ("traj", "seq"), None),
        check_vma=False,
    )
```
